32 devices in a mesh: section: 4 (over y, x), dp: 8 (over z, core).
Axes of the slice: x: 2, y: 2, z: 4, core: 2. Of those that a mesh axis runs over, the one named last changes fastest.
Arguments:
- tokens: bfloat16 [2, 4, 448, 2048], P(None, None, 'dp'), may hold values from -6 to 6
- targets: bfloat16 [2, 4, 448, 2048], P(None, None, 'dp'), may hold values from -6 to 6
- weights: bfloat16 [4, 2, 2, 96, 128, 128], P('section'), as said below
- pattern: int32 [4, 2, 2, 96, 2], P('section'), may hold values from 0 to 63, as said below
- master: float32 [4, 2, 96, 128, 128], P('section', None, None, 'dp'), may hold values from -0.6 to 0.6
- moment: float32 [4, 2, 96, 128, 128], P('section', None, None, 'dp'), as said below
- variance: float32 [4, 2, 96, 128, 128], P('section', None, None, 'dp'), as said below
Outputs:
- adam_step: float32 [4, 2, 96, 128, 128], P('section', None, None, 'dp')
- new_master: float32 [4, 2, 96, 128, 128], P('section', None, None, 'dp')
The draws below stay inside these ranges and needn't reach their ends.
Inputs may be any that keep to these rules, and one draw needn't show every extreme that they name: Within one layer and projection the 96 blocks are distinct and sorted; every block column of the up projection and every block row of the down projection holds one or more blocks. pattern[s,1] equals pattern[3 - s, 0]. Up blocks have rows below 16 and columns below 64, down blocks the reverse. weights[s,1] equals weights[3 - s, 0]; entries are scaled by the inverse root of the mean number of inputs per output. `moment`: of the order of the gradient. `variance`: Positive, of the order of the squared gradient.
All inputs are finite; a program needn't handle non-finite values.
Results may differ from the reference program's by a relative error of at most 0.022.
Values may be sent and summed in bfloat16 or wider, within the bound.
No kernel may reach another device: no remote copies, remote signals or barrier semaphores. Data moves between devices by JAX's collectives and lax.ppermute only.
A program may use at most 192 MiB of HBM per device.

```python
import math
import jax
import jax.numpy as jnp
from jax import lax

D = 2048
FF = 8192
BS = 128
NNZ = 96
MICRO = 4
LAYERS = 4
REPLICA_ROWS = 448
TOTAL = 3584


def pick_blocks(seed_key, grid_rows, grid_cols, by_column):
    first_key, second_key = jax.random.split(seed_key)
    cell_count = grid_rows * grid_cols
    priority = jax.random.permutation(first_key, cell_count).astype(jnp.int32)
    if by_column:
        chosen = jax.random.randint(second_key, (grid_cols,), 0, grid_rows).astype(jnp.int32)
        forced = chosen * grid_cols + jnp.arange(grid_cols, dtype=jnp.int32)
    else:
        chosen = jax.random.randint(second_key, (grid_rows,), 0, grid_cols).astype(jnp.int32)
        forced = jnp.arange(grid_rows, dtype=jnp.int32) * grid_cols + chosen
    priority = priority.at[forced].add(cell_count)
    ignored, picked = lax.top_k(priority, NNZ)
    picked = jnp.sort(picked.astype(jnp.int32))
    return jnp.stack([picked // grid_cols, picked % grid_cols], axis=-1).astype(jnp.int32)


def draw_pattern(key, part):
    up_keys = jax.random.split(jax.random.fold_in(key, 11), LAYERS)
    down_keys = jax.random.split(jax.random.fold_in(key, 12), LAYERS)
    up_blocks = jax.vmap(lambda layer_key: pick_blocks(layer_key, D // BS, FF // BS, True))(up_keys)
    down_blocks = jax.vmap(lambda layer_key: pick_blocks(layer_key, FF // BS, D // BS, False))(down_keys)
    single = jnp.stack([up_blocks, down_blocks], axis=1)
    return jnp.stack([single, single[::-1]], axis=1)


def draw_weights(key, part):
    up_fan = BS * max(1.0, NNZ * BS / FF)
    down_fan = BS * max(1.0, NNZ * BS / D)
    single = jax.random.truncated_normal(jax.random.fold_in(key, 21), -4.0, 4.0, (LAYERS, 2, NNZ, BS, BS), jnp.float32)
    scales = jnp.array([up_fan ** (-0.5), down_fan ** (-0.5)], jnp.float32).reshape(1, 2, 1, 1, 1)
    single = single * scales
    return jnp.stack([single, single[::-1]], axis=1).astype(jnp.bfloat16)


def draw_moment(key, part):
    spread = 0.2 / math.sqrt(TOTAL)
    return (jax.random.normal(jax.random.fold_in(key, 31), (LAYERS, 2, NNZ, BS, BS), jnp.float32) * spread).astype(jnp.float32)


def draw_variance(key, part):
    lowest = math.log(0.01 / TOTAL)
    highest = math.log(0.1 / TOTAL)
    exponent = jax.random.uniform(jax.random.fold_in(key, 41), (LAYERS, 2, NNZ, BS, BS), jnp.float32, lowest, highest)
    return jnp.exp(exponent).astype(jnp.float32)


def block_scale(stream_key, dims, shards, smallest, top_value):
    def one(position, shards_of):
        steps = jax.random.uniform(jax.random.fold_in(jax.random.fold_in(stream_key, 6), position), (shards_of,), jnp.float32, smallest / len(shards), top_value / len(shards))
        return jnp.repeat(jnp.exp(steps), dims[position] // shards_of).reshape((-1,) + (1,) * (len(dims) - position - 1))

    loudness = one(*shards[0])
    for cut in shards[1:]:
        loudness = loudness * one(*cut)
    return loudness


def bell_draw(stream_key, dims, scale, limit, pieces=(), kind=jnp.bfloat16):
    values = jax.random.normal(stream_key, dims, jnp.float32) * scale
    if len(pieces) > 0:
        values = block_scale(stream_key, dims, pieces, -0.22, 0.18) * values
    return jnp.clip(values, min=-limit, max=limit).astype(kind)


def setup_inputs(seed: int = 0) -> dict:
    arg_keys = jax.random.split(jax.random.key(seed), 8)
    tokens = bell_draw(arg_keys[0], (2, MICRO, REPLICA_ROWS, D), 1.0, 6.0, ((2, 8),))
    targets = bell_draw(arg_keys[1], (2, MICRO, REPLICA_ROWS, D), 1.0, 6.0, ((2, 8),))
    weights = draw_weights(jax.random.fold_in(arg_keys[7], 71), 0)
    pattern = draw_pattern(jax.random.fold_in(arg_keys[7], 71), 0)
    master = bell_draw(arg_keys[4], (LAYERS, 2, NNZ, BS, BS), 0.1, 0.6, ((0, 4), (3, 8)), jnp.float32)
    moment = draw_moment(jax.random.fold_in(arg_keys[7], 71), 0)
    variance = draw_variance(jax.random.fold_in(arg_keys[7], 71), 0)
    return dict(tokens=tokens, targets=targets, weights=weights, pattern=pattern, master=master, moment=moment, variance=variance)


norm_eps = 1e-06
gelu_coef = 0.7978845608028654
beta_first = 0.9
beta_second = 0.95
adam_eps = 1e-08
learn_rate = 0.001
decay_rate = 0.1
update_count = 10

def sparse_product(left_rows, blocks, take_index, put_index, out_blocks):
    row_count = left_rows.shape[0]
    picked = jnp.take(left_rows.reshape(row_count, -1, BS), take_index, axis=1)
    product = jnp.einsum('rka,kab->krb', picked.astype(jnp.float32), blocks.astype(jnp.float32))
    summed = jax.ops.segment_sum(product, put_index, num_segments=out_blocks)
    return summed.transpose(1, 0, 2).reshape(row_count, out_blocks * BS)

def sparse_transposed(left_rows, blocks, take_index, put_index, out_blocks):
    row_count = left_rows.shape[0]
    picked = jnp.take(left_rows.reshape(row_count, -1, BS), take_index, axis=1)
    product = jnp.einsum('rkb,kab->kra', picked.astype(jnp.float32), blocks.astype(jnp.float32))
    summed = jax.ops.segment_sum(product, put_index, num_segments=out_blocks)
    return summed.transpose(1, 0, 2).reshape(row_count, out_blocks * BS)

def gelu_slope(preact):
    tanh_input = gelu_coef * (preact + 0.044715 * preact ** 3)
    tangent = jnp.tanh(tanh_input)
    return 0.5 * (1.0 + tangent) + 0.5 * preact * (1.0 - tangent * tangent) * gelu_coef * (1.0 + 3.0 * 0.044715 * preact * preact)

def layer_forward(inputs, layer_weights, layer_pattern):
    widened = inputs.astype(jnp.float32)
    factor = lax.rsqrt(lax.optimization_barrier(jnp.mean(widened * widened, axis=-1, keepdims=True)) + norm_eps)
    normed = (widened * factor).astype(jnp.bfloat16)
    preact = sparse_product(normed, layer_weights[0], layer_pattern[0, :, 0], layer_pattern[0, :, 1], FF // BS)
    hidden = jax.nn.gelu(preact, approximate=True).astype(jnp.bfloat16)
    mixed = sparse_product(hidden, layer_weights[1], layer_pattern[1, :, 0], layer_pattern[1, :, 1], D // BS)
    result = (widened + mixed).astype(jnp.bfloat16)
    return (result, normed, preact, hidden)

def layer_backward(inputs, preact, upstream, layer_weights, layer_pattern):
    grad_hidden = sparse_transposed(upstream, layer_weights[1], layer_pattern[1, :, 1], layer_pattern[1, :, 0], FF // BS)
    grad_preact = (grad_hidden * gelu_slope(preact)).astype(jnp.bfloat16)
    grad_normed = sparse_transposed(grad_preact, layer_weights[0], layer_pattern[0, :, 1], layer_pattern[0, :, 0], D // BS)
    widened = inputs.astype(jnp.float32)
    factor = lax.rsqrt(lax.optimization_barrier(jnp.mean(widened * widened, axis=-1, keepdims=True)) + norm_eps)
    coupling = lax.optimization_barrier(jnp.mean(widened * grad_normed, axis=-1, keepdims=True))
    downstream = upstream.astype(jnp.float32) + factor * grad_normed - widened * factor ** 3 * coupling
    return (downstream.astype(jnp.bfloat16), grad_preact)

def block_pairs(left_rows, right_rows, left_index, right_index):
    row_count = left_rows.shape[0]
    left_picked = jnp.take(left_rows.reshape(row_count, -1, BS), left_index, axis=1)
    right_picked = jnp.take(right_rows.reshape(row_count, -1, BS), right_index, axis=1)
    return jnp.einsum('rka,rkb->kab', left_picked.astype(jnp.float32), right_picked.astype(jnp.float32))

def weight_grads(normed, grad_preact, hidden, upstream, layer_pattern):
    up_part = block_pairs(normed, grad_preact, layer_pattern[0, :, 0], layer_pattern[0, :, 1])
    down_part = block_pairs(hidden, upstream, layer_pattern[1, :, 0], layer_pattern[1, :, 1])
    return jnp.stack([up_part, down_part])

def adam_update(grad_sum, master, moment, variance, token_total):
    gradient = grad_sum / token_total
    moment_next = beta_first * moment + (1.0 - beta_first) * gradient
    variance_next = beta_second * variance + (1.0 - beta_second) * gradient * gradient
    corrected = moment_next / (1.0 - beta_first ** update_count)
    spread = jnp.sqrt(variance_next / (1.0 - beta_second ** update_count))
    step_direction = corrected / (spread + adam_eps)
    return (step_direction, master - learn_rate * (step_direction + decay_rate * master))

def reference(tokens, targets, weights, pattern, master, moment, variance):
    layer_count = weights.shape[0]
    grad_list = [jnp.zeros((2, NNZ, BS, BS), jnp.float32) for layer_index in range(layer_count)]
    for stream in range(2):
        for micro_index in range(MICRO):
            current = tokens[stream, micro_index]
            history = []
            for layer_index in range(layer_count):
                result, normed, preact, hidden = layer_forward(current, weights[layer_index, 0], pattern[layer_index, 0])
                history.append((current, normed, preact, hidden))
                current = result
            upstream = (current.astype(jnp.float32) - targets[stream, micro_index].astype(jnp.float32)).astype(jnp.bfloat16)
            for layer_index in reversed(range(layer_count)):
                inputs, normed, preact, hidden = history[layer_index]
                downstream, grad_preact = layer_backward(inputs, preact, upstream, weights[layer_index, 0], pattern[layer_index, 0])
                grad_list[layer_index] = grad_list[layer_index] + weight_grads(normed, grad_preact, hidden, upstream, pattern[layer_index, 0])
                upstream = downstream
    token_total = 2 * MICRO * tokens.shape[2]
    grad_sum = jnp.stack(grad_list)
    return adam_update(grad_sum, master, moment, variance, token_total)
```

```python
import functools

import jax
import jax.numpy as jnp
from jax import lax
from jax.experimental import pallas as pl
from jax.experimental.pallas import tpu as pltpu
from jax.sharding import PartitionSpec as P

BS = 128
norm_eps = 1e-06
gelu_coef = 0.7978845608028654
beta_first = 0.9
beta_second = 0.95
adam_eps = 1e-08
learn_rate = 0.001
decay_rate = 0.1
update_count = 10
ROW_TILE = 16
VMEM_LIMIT = 60 * 1024 * 1024


def gelu(preact):
    tangent = jnp.tanh(gelu_coef * (preact + 0.044715 * preact * preact * preact))
    return 0.5 * preact * (1.0 + tangent)


def gelu_both(preact):
    square = preact * preact
    tangent = jnp.tanh(gelu_coef * (preact + 0.044715 * square * preact))
    half = 0.5 * (1.0 + tangent)
    slope = half + 0.5 * preact * (1.0 - tangent * tangent) * gelu_coef * (
        1.0 + 3.0 * 0.044715 * square
    )
    return (preact * half, slope)


def dot_plain(left, right):
    return jnp.dot(left, right, preferred_element_type=jnp.float32)


def dot_right_t(left, right):
    return lax.dot_general(left, right, (((1,), (1,)), ((), ())), preferred_element_type=jnp.float32)


def dot_left_t(left, right):
    return lax.dot_general(left, right, (((0,), (0,)), ((), ())), preferred_element_type=jnp.float32)


def fill_normed(x_ref, normed, base):
    rows, width = x_ref.shape

    def tile(i, carry):
        at = pl.multiple_of(i * ROW_TILE, ROW_TILE)
        wide = x_ref[pl.ds(at, ROW_TILE), :].astype(jnp.float32)
        factor = lax.rsqrt(jnp.mean(wide * wide, axis=-1, keepdims=True) + norm_eps)
        value = (wide * factor).astype(jnp.bfloat16)
        for b in range(width // BS):
            normed[b, pl.ds(base + at, ROW_TILE), :] = value[:, b * BS : (b + 1) * BS]
        return carry

    lax.fori_loop(0, rows // ROW_TILE, tile, 0)


def fill_split(x_ref, split, base):
    rows, width = x_ref.shape
    for b in range(width // BS):
        split[b, pl.ds(base, rows), :] = x_ref[:, b * BS : (b + 1) * BS]


def clear(ref):
    def one(i, carry):
        ref[i] = jnp.zeros(ref.shape[1:], ref.dtype)
        return carry

    lax.fori_loop(0, ref.shape[0], one, 0)


def accumulate(pattern, which, source, take, blocks, target, put, dot, base, rows):
    clear(target)

    def one(k, carry):
        left = source[pattern[which, k, take], pl.ds(base, rows), :]
        place = pattern[which, k, put]
        target[place] += dot(left, blocks[k])
        return carry

    lax.fori_loop(0, blocks.shape[0], one, 0, unroll=4)


def each(count, body):
    def one(i, carry):
        body(i)
        return carry

    lax.fori_loop(0, count, one, 0)


def forward_rows(x_ref, out_ref, pattern, weights, normed, wide_a, hidden, narrow):
    rows, width = x_ref.shape
    fill_normed(x_ref, normed, 0)
    accumulate(pattern, 0, normed, 0, weights.at[0], wide_a, 1, dot_plain, 0, rows)

    def act(c):
        hidden[c] = gelu(wide_a[c]).astype(jnp.bfloat16)

    each(wide_a.shape[0], act)
    accumulate(pattern, 1, hidden, 0, weights.at[1], narrow, 1, dot_plain, 0, rows)
    for b in range(width // BS):
        cols = slice(b * BS, (b + 1) * BS)
        out_ref[:, cols] = (x_ref[:, cols].astype(jnp.float32) + narrow[b]).astype(jnp.bfloat16)


def backward_rows(x_ref, cot_ref, out_ref, pattern, weights, normed, wide_a, wide_b, hidden, narrow):
    rows, width = x_ref.shape
    fill_normed(x_ref, normed, 0)
    accumulate(pattern, 0, normed, 0, weights.at[0], wide_a, 1, dot_plain, 0, rows)
    fill_split(cot_ref, normed, 0)
    accumulate(pattern, 1, normed, 1, weights.at[1], wide_b, 0, dot_right_t, 0, rows)

    def act(c):
        hidden[c] = (wide_b[c] * gelu_both(wide_a[c])[1]).astype(jnp.bfloat16)

    each(wide_a.shape[0], act)
    accumulate(pattern, 0, hidden, 1, weights.at[0], narrow, 0, dot_right_t, 0, rows)

    def tile(i):
        at = pl.multiple_of(i * ROW_TILE, ROW_TILE)
        wide = x_ref[pl.ds(at, ROW_TILE), :].astype(jnp.float32)
        factor = lax.rsqrt(jnp.mean(wide * wide, axis=-1, keepdims=True) + norm_eps)
        grad = jnp.concatenate(
            [narrow[b, pl.ds(at, ROW_TILE), :] for b in range(width // BS)], axis=-1
        )
        coupling = jnp.mean(wide * grad, axis=-1, keepdims=True)
        upstream = cot_ref[pl.ds(at, ROW_TILE), :].astype(jnp.float32)
        value = upstream + factor * grad - wide * (factor * factor * factor * coupling)
        out_ref[pl.ds(at, ROW_TILE), :] = value.astype(jnp.bfloat16)

    each(rows // ROW_TILE, tile)


def wide_shape(rows, blocks, dtype):
    return pltpu.VMEM((blocks, rows, BS), dtype)


def weight_spec(weights, step_copy):
    return pl.BlockSpec(
        (None,) + weights.shape[1:],
        lambda i, copies: (step_copy(i, copies), 0, 0, 0, 0),
    )


def pattern_spec(pattern, step_copy):
    return pl.BlockSpec(
        (None,) + pattern.shape[1:],
        lambda i, copies: (step_copy(i, copies), 0, 0, 0),
        memory_space=pltpu.SMEM,
    )


def whole_spec(array):
    return pl.BlockSpec(array.shape, lambda i, copies: (0,) * len(array.shape))


def rows_shape(array):
    return jax.ShapeDtypeStruct(array.shape, jnp.bfloat16)


def run_steps(kernel, copies, step_copy, step_total, pattern, weights, rows_in, outs, scratch, name):
    grid_spec = pltpu.PrefetchScalarGridSpec(
        num_scalar_prefetch=1,
        grid=(step_total,),
        in_specs=[pattern_spec(pattern, step_copy), weight_spec(weights, step_copy)]
        + [whole_spec(r) for r in rows_in],
        out_specs=[whole_spec(o) for o in outs],
        scratch_shapes=scratch,
    )
    return pl.pallas_call(
        kernel,
        grid_spec=grid_spec,
        out_shape=outs,
        name=name,
        compiler_params=pltpu.CompilerParams(
            dimension_semantics=("arbitrary",), vmem_limit_bytes=VMEM_LIMIT
        ),
    )(copies, pattern, weights, *rows_in)


def forward_call(x, copies, start, total, pattern, weights, ff_blocks):
    rows, width = x.shape

    def kernel(copies_ref, pattern_ref, weights_ref, x_ref, *rest):
        outs, (normed, wide_a, hidden, narrow) = rest[:total], rest[total:]
        for step in range(total):

            @pl.when(pl.program_id(0) == step)
            def run(step=step):
                source = x_ref if step == 0 else outs[step - 1]
                forward_rows(
                    source, outs[step], pattern_ref, weights_ref, normed, wide_a, hidden, narrow
                )

    scratch = [
        wide_shape(rows, width // BS, jnp.bfloat16),
        wide_shape(rows, ff_blocks, jnp.float32),
        wide_shape(rows, ff_blocks, jnp.bfloat16),
        wide_shape(rows, width // BS, jnp.float32),
    ]
    return run_steps(
        kernel, copies, lambda i, c: c[start + i], total, pattern, weights, [x],
        [rows_shape(x)] * total, scratch, "forward"
    )


def backward_call(xs, cot, copies, start, pattern, weights, ff_blocks):
    rows, width = cot.shape
    total = len(xs)

    def kernel(copies_ref, pattern_ref, weights_ref, *rest):
        inputs, cot_ref, rest = rest[:total], rest[total], rest[total + 1 :]
        outs, (normed, wide_a, wide_b, hidden, narrow) = rest[:total], rest[total:]
        for step in range(total):

            @pl.when(pl.program_id(0) == step)
            def run(step=step):
                upstream = cot_ref if step == 0 else outs[step - 1]
                backward_rows(
                    inputs[step], upstream, outs[step], pattern_ref, weights_ref,
                    normed, wide_a, wide_b, hidden, narrow
                )

    scratch = [
        wide_shape(rows, width // BS, jnp.bfloat16),
        wide_shape(rows, ff_blocks, jnp.float32),
        wide_shape(rows, ff_blocks, jnp.float32),
        wide_shape(rows, ff_blocks, jnp.bfloat16),
        wide_shape(rows, width // BS, jnp.float32),
    ]
    return run_steps(
        kernel, copies, lambda i, c: c[start - i], total, pattern, weights, list(xs) + [cot],
        [rows_shape(cot)] * total, scratch, "backward"
    )


def turn_call(x, targets, copies, pattern, weights, ff_blocks):
    rows, width = x.shape

    def kernel(copies_ref, pattern_ref, weights_ref, x_ref, target_ref, residue, out,
               normed, wide_a, wide_b, hidden, narrow):
        forward_rows(x_ref, residue, pattern_ref, weights_ref, normed, wide_a, hidden, narrow)
        for b in range(width // BS):
            cols = slice(b * BS, (b + 1) * BS)
            difference = residue[:, cols].astype(jnp.float32) - target_ref[:, cols].astype(jnp.float32)
            residue[:, cols] = difference.astype(jnp.bfloat16)
        backward_rows(
            x_ref, residue, out, pattern_ref, weights_ref, normed, wide_a, wide_b, hidden, narrow
        )

    scratch = [
        wide_shape(rows, width // BS, jnp.bfloat16),
        wide_shape(rows, ff_blocks, jnp.float32),
        wide_shape(rows, ff_blocks, jnp.float32),
        wide_shape(rows, ff_blocks, jnp.bfloat16),
        wide_shape(rows, width // BS, jnp.float32),
    ]
    return run_steps(
        kernel, copies, lambda i, c: c[1], 1, pattern, weights, [x, targets],
        [rows_shape(x)] * 2, scratch, "turn"
    )


def grads_call(xs, cots, copies, pattern, weights, ff_blocks, shares):
    rows, width = xs[0].shape
    parts = len(xs)
    block_total = weights.shape[2]
    share_rows = BS // shares

    def kernel(copies_ref, pattern_ref, weights_ref, *rest):
        inputs, upstreams, out = rest[:parts], rest[parts : 2 * parts], rest[2 * parts]
        normed, split, wide_a, wide_b, hidden, grad_pre = rest[2 * parts + 1 :]
        for part in range(parts):
            base = part * rows
            fill_normed(inputs[part], normed, base)
            fill_split(upstreams[part], split, base)
            accumulate(
                pattern_ref, 0, normed, 0, weights_ref.at[0], wide_a, 1, dot_plain, base, rows
            )
            accumulate(
                pattern_ref, 1, split, 1, weights_ref.at[1], wide_b, 0, dot_right_t, base, rows
            )

            def act(c):
                value, slope = gelu_both(wide_a[c])
                hidden[c, pl.ds(base, rows), :] = value.astype(jnp.bfloat16)
                grad_pre[c, pl.ds(base, rows), :] = (wide_b[c] * slope).astype(jnp.bfloat16)

            each(wide_a.shape[0], act)

        def one(k, carry):
            up = dot_left_t(
                normed[pattern_ref[0, k, 0]], grad_pre[pattern_ref[0, k, 1]]
            ).astype(jnp.bfloat16)
            down = dot_left_t(
                hidden[pattern_ref[1, k, 0]], split[pattern_ref[1, k, 1]]
            ).astype(jnp.bfloat16)
            for share in range(shares):
                span = slice(share * share_rows, (share + 1) * share_rows)
                out[share, 0, k] = up[span]
                out[share, 1, k] = down[span]
            return carry

        lax.fori_loop(0, block_total, one, 0, unroll=2)

    all_rows = rows * parts
    scratch = [
        wide_shape(all_rows, width // BS, jnp.bfloat16),
        wide_shape(all_rows, width // BS, jnp.bfloat16),
        wide_shape(rows, ff_blocks, jnp.float32),
        wide_shape(rows, ff_blocks, jnp.float32),
        wide_shape(all_rows, ff_blocks, jnp.bfloat16),
        wide_shape(all_rows, ff_blocks, jnp.bfloat16),
    ]
    out = jax.ShapeDtypeStruct((shares, 2, block_total, share_rows, BS), jnp.bfloat16)
    return run_steps(
        kernel, copies, lambda i, c: 0, 1, pattern, weights, list(xs) + list(cots),
        [out], scratch, "grads"
    )[0]


def adam_update(grad_sum, master, moment, variance, token_total):
    gradient = grad_sum / token_total
    moment_next = beta_first * moment + (1.0 - beta_first) * gradient
    variance_next = beta_second * variance + (1.0 - beta_second) * gradient * gradient
    corrected = moment_next / (1.0 - beta_first**update_count)
    spread = jnp.sqrt(variance_next / (1.0 - beta_second**update_count))
    step_direction = corrected / (spread + adam_eps)
    return (step_direction, master - learn_rate * (step_direction + decay_rate * master))


def shards(ff_blocks, tokens, targets, weights, pattern, master, moment, variance):
    section = lax.axis_index("section")
    sections = lax.axis_size("section")
    shares = lax.axis_size("dp")
    groups = sections // 2
    micro, rows_each, width = tokens.shape[1:]
    rows = micro * rows_each
    half = rows // 2
    high_member = (section >= groups).astype(jnp.int32)
    group = jnp.minimum(section, sections - 1 - section)
    copies = jnp.stack([high_member, 1 - high_member])
    weights, pattern = weights[0], pattern[0]

    def own_stream(array):
        return lax.dynamic_index_in_dim(array, high_member, 0, keepdims=False).reshape(rows, width)

    mirror = lambda i: sections - 1 - i
    straight = [(i, i + 1) for i in range(groups - 1)]
    straight += [(mirror(i), mirror(j)) for i, j in straight]
    crossed = [(i, mirror(i + 1)) for i in range(groups - 1)]
    crossed += [(mirror(i), mirror(j)) for i, j in crossed]

    def hop(x, inward):
        turned = lambda pairs: pairs if inward else [(j, i) for i, j in pairs]
        return jnp.concatenate(
            [
                lax.ppermute(x[:half], "section", turned(straight)),
                lax.ppermute(x[half:], "section", turned(crossed)),
            ]
        )

    def swap(x):
        return lax.ppermute(x, "section", [(i, mirror(i)) for i in range(sections)])

    def pick(at_group, fresh, kept):
        return jnp.where(group == at_group, fresh, kept)

    current = own_stream(tokens)
    x_low = current
    for i in range(groups - 1):
        (current,) = forward_call(current, copies, 0, 1, pattern, weights, ff_blocks)
        current = hop(current, True)
        x_low = pick(i + 1, current, x_low)
    if groups > 1:
        x_high, current = forward_call(current, copies, 0, 2, pattern, weights, ff_blocks)
        for i in reversed(range(groups - 1)):
            current = hop(current, False)
            x_high = pick(i, current, x_high)
            if i > 0:
                (current,) = forward_call(current, copies, 1, 1, pattern, weights, ff_blocks)
    residue, current = turn_call(x_high, own_stream(targets), copies, pattern, weights, ff_blocks)
    cot_high = residue
    for i in range(1, groups):
        current = hop(current, True)
        cot_high = pick(i, current, cot_high)
        if i < groups - 1:
            (current,) = backward_call([x_high], current, copies, 1, pattern, weights, ff_blocks)
    cot_low, current = backward_call(
        [x_high, x_low], cot_high, copies, 1, pattern, weights, ff_blocks
    )
    for i in reversed(range(groups - 1)):
        current = hop(current, False)
        cot_low = pick(i, current, cot_low)
        if i > 0:
            (current,) = backward_call([x_low], cot_low, copies, 0, pattern, weights, ff_blocks)

    is_high = high_member == 1
    x_other = swap(jnp.where(is_high, x_low, x_high))
    cot_other = swap(jnp.where(is_high, cot_low, cot_high))
    x_own = jnp.where(is_high, x_high, x_low)
    cot_own = jnp.where(is_high, cot_high, cot_low)
    grads = grads_call(
        [x_own, x_other], [cot_own, cot_other], copies, pattern, weights, ff_blocks, shares
    )
    share = lax.psum_scatter(grads, "dp", scatter_dimension=0, tiled=True)[0].astype(jnp.float32)
    token_total = 2 * rows * shares
    step_direction, master_next = adam_update(share, master[0], moment[0], variance[0], token_total)
    return (step_direction[None], master_next[None])


def solution(mesh):
    rows_split = P(None, None, "dp", None)
    by_section = P("section", None, None, "dp", None)
    return jax.shard_map(
        functools.partial(shards, FF_BLOCKS),
        mesh=mesh,
        in_specs=(
            rows_split,
            rows_split,
            P("section", None, None, None, None, None),
            P("section", None, None, None, None),
            by_section,
            by_section,
            by_section,
        ),
        out_specs=(by_section, by_section),
        check_vma=False,
    )


FF_BLOCKS = 8192 // BS
```

```python
import functools

import jax
import jax.numpy as jnp
from jax import lax
from jax.experimental import pallas as pl
from jax.experimental.pallas import tpu as pltpu
from jax.sharding import PartitionSpec as P

BS = 128
FF_BLOCKS = 8192 // BS
norm_eps = 1e-06
gelu_coef = 0.7978845608028654
gelu_cubic = gelu_coef * 0.044715
beta_first = 0.9
beta_second = 0.95
adam_eps = 1e-08
learn_rate = 0.001
decay_rate = 0.1
update_count = 10
ROW_TILE = 16
VMEM_LIMIT = 60 * 1024 * 1024
UP_WIDE, DOWN_WIDE, DOWN_NARROW, UP_NARROW = range(4)
FIELDS = 9
FIRST, FIRST_TAKE, SECOND, SECOND_TAKE, PUT, EXTRA, EXTRA_TAKE, EXTRA_PUT, COUNT = range(FIELDS)


def block_lists(pattern):
    total = pattern.shape[2]
    up_row, up_col = pattern[:, 0, :, 0], pattern[:, 0, :, 1]
    down_row, down_col = pattern[:, 1, :, 0], pattern[:, 1, :, 1]
    key = jnp.stack([up_col, down_row, down_col, up_row], 1)
    take = jnp.stack([up_row, down_col, down_row, up_col], 1)
    order = jnp.arange(total, dtype=jnp.int32)
    before = order[None, :] < order[:, None]

    def count(mask):
        return jnp.sum(mask.astype(jnp.int32), axis=-1)

    same = key[..., None, :] == key[..., :, None]
    rank = count(same & before)
    even = rank % 2 == 0
    wide = (jnp.arange(4) < 2)[None, :, None]
    extra = rank >= 2
    extra_place = count(extra[..., None, :] & before)
    pair = count((key[..., None, :] < key[..., :, None]) & even[..., None, :]) + rank // 2
    place_first = jnp.where(wide, jnp.where(rank == 0, key, -1), jnp.where(even, pair, -1))
    place_second = jnp.where(wide, jnp.where(rank == 1, key, -1), jnp.where(even, -1, pair))
    place_extra = jnp.where(wide & extra, extra_place, -1)
    number = jnp.broadcast_to(order, key.shape)
    places = jnp.stack(
        [place_first] * 2 + [place_second] * 2 + [place_first] + [place_extra] * 3, 2
    )
    values = jnp.stack([number, take, number - total, take, key, number, take, key], 2)
    hit = places[..., None, :] == order[:, None]
    fields = jnp.sum(jnp.where(hit, values[..., None, :], 0), axis=-1)
    fields = fields + jnp.where(jnp.arange(8) == SECOND, total, 0)[:, None]
    counts = jnp.where(wide[..., 0], count(extra), count(even))
    counts = jnp.broadcast_to(counts[..., None, None], key.shape[:2] + (1, total))
    return jnp.concatenate([fields, counts], axis=2).astype(jnp.int32).reshape(-1)


class Lists:
    def __init__(self, ref, copy, total):
        self.ref, self.total = ref, total
        self.base = copy * (4 * FIELDS * total)

    def __call__(self, kind, field, index):
        return self.ref[self.base + ((kind * FIELDS + field) * self.total) + index]


def hidden_of(preact):
    inner = preact * (gelu_coef + gelu_cubic * (preact * preact))
    half = 0.5 * preact
    return half + half * jnp.tanh(inner)


def slope_of(preact):
    cubic = gelu_cubic * (preact * preact)
    tangent = jnp.tanh(preact * (gelu_coef + cubic))
    bend = preact * (gelu_coef + 3.0 * cubic)
    return (0.5 + 0.5 * tangent) * (1.0 + bend * (1.0 - tangent))


def both_of(preact):
    cubic = gelu_cubic * (preact * preact)
    tangent = jnp.tanh(preact * (gelu_coef + cubic))
    bend = preact * (gelu_coef + 3.0 * cubic)
    half = 0.5 + 0.5 * tangent
    return (preact * half, half * (1.0 + bend * (1.0 - tangent)))


def dot_plain(left, right):
    return jnp.dot(left, right, preferred_element_type=jnp.float32)


def dot_right_t(left, right):
    return lax.dot_general(left, right, (((1,), (1,)), ((), ())), preferred_element_type=jnp.float32)


def each(count, body, unroll=1):
    def one(i, carry):
        body(i)
        return carry

    lax.fori_loop(0, count, one, 0, unroll=unroll)


def fill_normed(x_ref, normed, base):
    rows, width = x_ref.shape

    def tile(i):
        at = pl.multiple_of(i * ROW_TILE, ROW_TILE)
        wide = x_ref[pl.ds(at, ROW_TILE), :].astype(jnp.float32)
        factor = lax.rsqrt(jnp.mean(wide * wide, axis=-1, keepdims=True) + norm_eps)
        value = (wide * factor).astype(jnp.bfloat16)
        for b in range(width // BS):
            normed[b, pl.ds(base + at, ROW_TILE), :] = value[:, b * BS : (b + 1) * BS]

    each(rows // ROW_TILE, tile)


def fill_split(x_ref, split, base):
    rows, width = x_ref.shape
    for b in range(width // BS):
        split[b, pl.ds(base, rows), :] = x_ref[:, b * BS : (b + 1) * BS]


def pair_product(source, blocks, lists, kind, p, transposed):
    left = jnp.concatenate(
        [source[lists(kind, FIRST_TAKE, p)], source[lists(kind, SECOND_TAKE, p)]], axis=1
    )
    one, two = blocks[lists(kind, FIRST, p)], blocks[lists(kind, SECOND, p)]
    if transposed:
        return dot_right_t(left, jnp.concatenate([one, two], axis=1))
    return dot_plain(left, jnp.concatenate([one, two], axis=0))


def wide_pass(source, blocks, lists, kind, sums, finish, transposed):
    def main(c):
        value = pair_product(source, blocks, lists, kind, c, transposed)
        sums[c] = value
        finish(c, value)

    each(sums.shape[0], main, 2)
    dot = dot_right_t if transposed else dot_plain

    def more(e):
        c = lists(kind, EXTRA_PUT, e)
        left = source[lists(kind, EXTRA_TAKE, e)]
        value = sums[c] + dot(left, blocks[lists(kind, EXTRA, e)])
        sums[c] = value
        finish(c, value)

    each(lists(kind, COUNT, 0), more)


def narrow_pass(source, blocks, lists, kind, sums, transposed):
    sums[...] = jnp.zeros(sums.shape, sums.dtype)

    def one(p):
        sums[lists(kind, PUT, p)] += pair_product(source, blocks, lists, kind, p, transposed)

    count = lists(kind, COUNT, 0)

    def two(i):
        one(2 * i)
        one(2 * i + 1)

    each(count // 2, two)

    @pl.when(count % 2 == 1)
    def last():
        one(count - 1)


def forward_rows(x_ref, out_ref, lists, weights, scratch, slopes=None):
    normed, sums, hidden, narrow = scratch
    rows, width = x_ref.shape
    fill_normed(x_ref, normed, 0)
    weights.wait(0)

    def finish(c, value):
        if slopes is None:
            hidden[c] = hidden_of(value).astype(jnp.bfloat16)
        else:
            value, slope = both_of(value)
            hidden[c] = value.astype(jnp.bfloat16)
            slopes[c] = slope

    wide_pass(normed, weights.blocks(0), lists, UP_WIDE, sums, finish, False)
    weights.wait(1)
    narrow_pass(hidden, weights.blocks(1), lists, DOWN_NARROW, narrow, False)
    for b in range(width // BS):
        cols = slice(b * BS, (b + 1) * BS)
        out_ref[:, cols] = (x_ref[:, cols].astype(jnp.float32) + narrow[b]).astype(jnp.bfloat16)


def slope_rows(x_ref, lists, weights, scratch, slopes):
    normed, sums, hidden, narrow = scratch
    fill_normed(x_ref, normed, 0)
    weights.wait(0)

    def finish(c, value):
        slopes[c] = slope_of(value)

    wide_pass(normed, weights.blocks(0), lists, UP_WIDE, sums, finish, False)
    weights.wait(1)


def backward_rows(x_ref, cot_ref, out_ref, lists, weights, scratch, slopes):
    normed, sums, hidden, narrow = scratch
    rows, width = x_ref.shape
    fill_split(cot_ref, normed, 0)

    def finish(c, value):
        hidden[c] = (value * slopes[c]).astype(jnp.bfloat16)

    wide_pass(normed, weights.blocks(1), lists, DOWN_WIDE, sums, finish, True)
    narrow_pass(hidden, weights.blocks(0), lists, UP_NARROW, narrow, True)

    def tile(i):
        at = pl.multiple_of(i * ROW_TILE, ROW_TILE)
        wide = x_ref[pl.ds(at, ROW_TILE), :].astype(jnp.float32)
        factor = lax.rsqrt(jnp.mean(wide * wide, axis=-1, keepdims=True) + norm_eps)
        grad = jnp.concatenate(
            [narrow[b, pl.ds(at, ROW_TILE), :] for b in range(width // BS)], axis=-1
        )
        coupling = jnp.mean(wide * grad, axis=-1, keepdims=True)
        upstream = cot_ref[pl.ds(at, ROW_TILE), :].astype(jnp.float32)
        value = upstream + factor * grad - wide * (factor * factor * factor * coupling)
        out_ref[pl.ds(at, ROW_TILE), :] = value.astype(jnp.bfloat16)

    each(rows // ROW_TILE, tile)


class Weights:
    def __init__(self, hbm, local, sems, slot, copy):
        self.hbm, self.local, self.sems, self.slot, self.copy = hbm, local, sems, slot, copy

    def move(self, part):
        total = self.hbm.shape[2]
        return pltpu.make_async_copy(
            self.hbm.at[self.copy, part],
            self.local.at[self.slot, part, pl.ds(0, total)],
            self.sems.at[self.slot, part],
        )

    def start(self):
        for part in range(2):
            self.move(part).start()
            self.local[self.slot, part, self.hbm.shape[2]] = jnp.zeros((BS, BS), jnp.bfloat16)

    def wait(self, part):
        self.move(part).wait()

    def blocks(self, part):
        return self.local.at[self.slot, part]


def stage(kernel, rows_in, others, outs, scratch, slots, copies, lists, weights, flops, name):
    total = weights.shape[2]
    any_spec = pl.BlockSpec(memory_space=pl.ANY)
    smem_spec = pl.BlockSpec(memory_space=pltpu.SMEM)
    vmem_spec = pl.BlockSpec(memory_space=pltpu.VMEM)

    def body(copies_ref, lists_ref, weights_ref, *rest):
        ins, rest = rest[: len(rows_in) + len(others)], rest[len(rows_in) + len(others) :]
        results, rest = rest[: len(outs)], rest[len(outs) :]
        local, sems, rest = rest[0], rest[1], rest[2:]
        loaded = []
        for slot, which in enumerate(slots):
            copy = copies_ref[which]
            moved = Weights(weights_ref, local, sems, slot, copy)
            moved.start()
            loaded.append((Lists(lists_ref, copy, total), moved))
        kernel(loaded, ins, results, rest)

    return pl.pallas_call(
        body,
        in_specs=[smem_spec, smem_spec, any_spec]
        + [vmem_spec] * len(rows_in)
        + [any_spec] * len(others),
        out_specs=[vmem_spec if space else any_spec for space, _ in outs],
        out_shape=[shape for _, shape in outs],
        scratch_shapes=[
            pltpu.VMEM((len(slots), 2, total + 1, BS, BS), jnp.bfloat16),
            pltpu.SemaphoreType.DMA((len(slots), 2)),
        ]
        + scratch,
        name=name,
        cost_estimate=pl.CostEstimate(
            flops=flops * 8, transcendentals=0, bytes_accessed=len(slots) * weights.size
        ),
        compiler_params=pltpu.CompilerParams(vmem_limit_bytes=VMEM_LIMIT),
    )(copies, lists, weights, *rows_in, *others)


def layer_scratch(rows, width):
    return [
        pltpu.VMEM((width // BS, rows, BS), jnp.bfloat16),
        pltpu.VMEM((FF_BLOCKS, rows, BS), jnp.float32),
        pltpu.VMEM((FF_BLOCKS, rows, BS), jnp.bfloat16),
        pltpu.VMEM((width // BS, rows, BS), jnp.float32),
    ]


def slope_scratch(rows):
    return [pltpu.VMEM((FF_BLOCKS, rows, BS), jnp.float32)]


def rows_out(array):
    return (True, jax.ShapeDtypeStruct(array.shape, jnp.bfloat16))


def dense_flops(rows, weights):
    return 2 * rows * weights.shape[2] * BS * BS * 2


def forward_call(x, slots, copies, lists, weights):
    rows, width = x.shape

    def kernel(loaded, ins, results, scratch):
        source = ins[0]
        for (own_lists, moved), out in zip(loaded, results):
            forward_rows(source, out, own_lists, moved, scratch)
            source = out

    flops = dense_flops(rows, weights) * len(slots)
    return stage(
        kernel, [x], [], [rows_out(x)] * len(slots), layer_scratch(rows, width), slots, copies,
        lists, weights, flops, "forward"
    )


def turn_call(x, targets, copies, lists, weights):
    rows, width = x.shape

    def kernel(loaded, ins, results, scratch):
        x_ref, target_ref = ins
        residue, out = results
        own_lists, moved = loaded[0]
        layer, slopes = scratch[:-1], scratch[-1]
        forward_rows(x_ref, residue, own_lists, moved, layer, slopes)
        for b in range(width // BS):
            cols = slice(b * BS, (b + 1) * BS)
            difference = residue[:, cols].astype(jnp.float32) - target_ref[:, cols].astype(jnp.float32)
            residue[:, cols] = difference.astype(jnp.bfloat16)
        backward_rows(x_ref, residue, out, own_lists, moved, layer, slopes)

    return stage(
        kernel, [x, targets], [], [rows_out(x)] * 2,
        layer_scratch(rows, width) + slope_scratch(rows), [1], copies, lists, weights,
        2 * dense_flops(rows, weights), "turn"
    )


def backward_call(xs, cot, slots, copies, lists, weights):
    rows, width = cot.shape

    def kernel(loaded, ins, results, scratch):
        layer, slopes = scratch[:-1], scratch[-1]
        upstream = ins[-1]
        for (own_lists, moved), x_ref, out in zip(loaded, ins, results):
            slope_rows(x_ref, own_lists, moved, layer, slopes)
            backward_rows(x_ref, upstream, out, own_lists, moved, layer, slopes)
            upstream = out

    return stage(
        kernel, list(xs) + [cot], [], [rows_out(cot)] * len(slots),
        layer_scratch(rows, width) + slope_scratch(rows), slots, copies, lists, weights,
        2 * dense_flops(rows, weights) * len(slots), "backward"
    )


def own_layer_rows(ins, own_lists, moved, normed, split, slopes, sums, hidden, grad_pre):
    pieces = len(ins) // 2
    rows = ins[0].shape[0]
    for i in range(pieces):
        fill_normed(ins[i], normed, i * rows)
        fill_split(ins[pieces + i], split, i * rows)
    moved.wait(0)

    def finish_up(c, value):
        value, slope = both_of(value)
        hidden[c] = value.astype(jnp.bfloat16)
        slopes[c] = slope

    wide_pass(normed, moved.blocks(0), own_lists, UP_WIDE, sums, finish_up, False)
    moved.wait(1)

    def finish_down(c, value):
        grad_pre[c] = (value * slopes[c]).astype(jnp.bfloat16)

    wide_pass(split, moved.blocks(1), own_lists, DOWN_WIDE, sums, finish_down, True)


def prepare_call(pieces, copies, lists, weights):
    rows, width = pieces[0].shape
    rows = rows * len(pieces) // 2
    narrow_shape = (width // BS, BS, rows)
    wide_shape = (FF_BLOCKS, rows, BS)

    def kernel(loaded, ins, results, scratch):
        normed, split, slopes, sums, hidden, grad_pre, sems = scratch
        own_lists, moved = loaded[0]
        own_layer_rows(ins, own_lists, moved, normed, split, slopes, sums, hidden, grad_pre)
        moves = [
            pltpu.make_async_copy(source, target, sems.at[i])
            for i, (source, target) in enumerate(
                zip([hidden, grad_pre, normed, split], results)
            )
        ]
        for move in moves:
            move.start()
        for move in moves:
            move.wait()

    shapes = [wide_shape, wide_shape, (width // BS, rows, BS), (width // BS, rows, BS)]
    return stage(
        kernel, pieces, [], [(False, jax.ShapeDtypeStruct(s, jnp.bfloat16)) for s in shapes],
        [
            pltpu.VMEM((width // BS, rows, BS), jnp.bfloat16),
            pltpu.VMEM((width // BS, rows, BS), jnp.bfloat16),
            pltpu.VMEM(wide_shape, jnp.float32),
            pltpu.VMEM(wide_shape, jnp.float32),
            pltpu.VMEM(wide_shape, jnp.bfloat16),
            pltpu.VMEM(wide_shape, jnp.bfloat16),
            pltpu.SemaphoreType.DMA((4,)),
        ],
        [0], copies, lists, weights, 2 * dense_flops(rows, weights), "prepare"
    )


def grads_call(pieces, prepared, copies, lists, weights, pattern, shares):
    rows, width = pieces[0].shape
    rows = rows * len(pieces) // 2
    total = weights.shape[2]
    share_rows = BS // shares
    wide_shape = (FF_BLOCKS, rows, BS)
    pattern_flat = pattern[0].reshape(-1)

    def kernel(loaded, ins, results, scratch):
        normed, split, slopes, sums, hidden, grad_pre, turned, sems, pattern_sem, cells = scratch
        out = results[0]
        own_lists, moved = loaded[0]
        stored, pattern_ref = ins[-5:-1], ins[-1]
        load_cells = pltpu.make_async_copy(pattern_ref, cells, pattern_sem)
        load_cells.start()
        moves = [
            pltpu.make_async_copy(source, target.at[0], sems.at[i])
            for i, (source, target) in enumerate(zip(stored, [hidden, grad_pre, normed, split]))
        ]
        for move in moves:
            move.start()
        own_layer_rows(
            ins[:-5], own_lists, moved, normed.at[1], split.at[1], slopes, sums,
            hidden.at[1], grad_pre.at[1]
        )
        for move in moves:
            move.wait()
        load_cells.wait()
        for which, source in enumerate((normed, split)):
            for b in range(width // BS):
                for part in range(2):
                    turned[which, b, part] = source[part, b].T

        def one(k):
            row, col = cells[2 * k], cells[2 * k + 1]
            up = dot_plain(turned[0, row, 0], grad_pre[0, col])
            up = (up + dot_plain(turned[0, row, 1], grad_pre[1, col])).astype(jnp.bfloat16)
            row, col = cells[2 * (total + k)], cells[2 * (total + k) + 1]
            down = dot_plain(turned[1, col, 0], hidden[0, row])
            down = down + dot_plain(turned[1, col, 1], hidden[1, row])
            down = down.T.astype(jnp.bfloat16)
            for share in range(shares):
                span = slice(share * share_rows, (share + 1) * share_rows)
                out[share, 0, k] = up[span]
                out[share, 1, k] = down[span]

        each(total, one, 2)

    return stage(
        kernel, pieces, list(prepared) + [pattern_flat],
        [(True, jax.ShapeDtypeStruct((shares, 2, total, share_rows, BS), jnp.bfloat16))],
        [
            pltpu.VMEM((2, width // BS, rows, BS), jnp.bfloat16),
            pltpu.VMEM((2, width // BS, rows, BS), jnp.bfloat16),
            pltpu.VMEM(wide_shape, jnp.float32),
            pltpu.VMEM(wide_shape, jnp.float32),
            pltpu.VMEM((2,) + wide_shape, jnp.bfloat16),
            pltpu.VMEM((2,) + wide_shape, jnp.bfloat16),
            pltpu.VMEM((2, width // BS, 2, BS, rows), jnp.bfloat16),
            pltpu.SemaphoreType.DMA((4,)),
            pltpu.SemaphoreType.DMA,
            pltpu.SMEM((2 * total * 2,), jnp.int32),
        ],
        [0], copies, lists, weights, 4 * dense_flops(rows, weights), "grads"
    )[0]


def adam_update(grad_sum, master, moment, variance, token_total):
    gradient = grad_sum / token_total
    moment_next = beta_first * moment + (1.0 - beta_first) * gradient
    variance_next = beta_second * variance + (1.0 - beta_second) * gradient * gradient
    corrected = moment_next / (1.0 - beta_first**update_count)
    spread = jnp.sqrt(variance_next / (1.0 - beta_second**update_count))
    step_direction = corrected / (spread + adam_eps)
    return (step_direction, master - learn_rate * (step_direction + decay_rate * master))


def shards(tokens, targets, weights, pattern, master, moment, variance):
    section = lax.axis_index("section")
    sections = lax.axis_size("section")
    shares = lax.axis_size("dp")
    groups = sections // 2
    micro, rows_each, width = tokens.shape[1:]
    rows = micro * rows_each
    half = rows // 2
    high = section >= groups
    high_member = high.astype(jnp.int32)
    group = jnp.minimum(section, sections - 1 - section)
    copies = jnp.stack([high_member, 1 - high_member])
    own_copy = jnp.stack([jnp.zeros_like(high_member)] * 2)
    weights, pattern = weights[0], pattern[0]
    lists = block_lists(pattern)
    mirror = lambda i: sections - 1 - i

    def stream_half(array, member, h):
        stream = lax.dynamic_index_in_dim(array, member, 0, keepdims=False)
        return stream.reshape(rows, width)[h * half : (h + 1) * half]

    def lane(i, h):
        other = mirror(i + 1) if h else i + 1
        return [(i, other), (mirror(i), mirror(other))]

    def inward(x, i, h):
        return lax.ppermute(x, "section", lane(i, h))

    def outward(x, i, h):
        return lax.ppermute(x, "section", [(b, a) for a, b in lane(i, h)])

    halves = range(2)
    x_low = [[stream_half(tokens, high_member, h) for h in halves]]
    x_high, cot_low, cot_high = [[None] * groups for _ in range(3)]
    current = x_low[0]
    for i in range(groups - 1):
        current = [inward(forward_call(current[h], [0], copies, lists, weights)[0], i, h) for h in halves]
        x_low.append(current)
    both = [forward_call(current[h], [0, 1], copies, lists, weights) for h in halves]
    x_high[groups - 1] = [b[0] for b in both]
    current = [b[1] for b in both]
    for i in reversed(range(groups - 1)):
        current = [outward(current[h], i, h) for h in halves]
        x_high[i] = current
        if i > 0:
            current = [forward_call(current[h], [1], copies, lists, weights)[0] for h in halves]
    aims = [stream_half(targets, high_member, h) for h in halves]
    turned = [turn_call(current[h], aims[h], copies, lists, weights) for h in halves]
    cot_high[0] = [t[0] for t in turned]
    current = [t[1] for t in turned]
    for i in range(groups - 1):
        current = [inward(current[h], i, h) for h in halves]
        cot_high[i + 1] = current
        if i + 1 < groups - 1:
            current = [
                backward_call([x_high[i + 1][h]], current[h], [1], copies, lists, weights)[0]
                for h in halves
            ]
    last = groups - 1
    both = [
        backward_call([x_high[last][h], x_low[last][h]], current[h], [1, 0], copies, lists, weights)
        for h in halves
    ]
    cot_low[last] = [b[0] for b in both]
    current = [b[1] for b in both]
    for i in reversed(range(1, last)):
        current = [outward(current[h], i, h) for h in halves]
        cot_low[i] = current
        current = [
            backward_call([x_low[i][h]], current[h], [0], copies, lists, weights)[0] for h in halves
        ]
    from_low = [lax.ppermute(current[h], "section", [(1, 0)]) for h in halves]
    from_high = [lax.ppermute(current[h], "section", [(mirror(1), 0)]) for h in halves]

    to_low = [(mirror(i), i) for i in range(1, groups)]
    to_high = [(i, mirror(i)) for i in range(groups)]

    def at_half(records, h, start=0):
        value = records[start][h]
        for i in range(start + 1, groups):
            value = jnp.where(group == i, records[i][h], value)
        return value

    pieces = []
    first_group = (group == 0) & ~high
    for h in halves:
        x_from_high = lax.ppermute(at_half(x_low, h, 1), "section", to_low)
        x_from_low = lax.ppermute(at_half(x_high, h), "section", to_high)
        cot_from_high = lax.ppermute(at_half(cot_low, h, 1), "section", to_low)
        cot_from_low = lax.ppermute(at_half(cot_high, h), "section", to_high)
        straight, crossed = (from_high, from_low) if h else (from_low, from_high)
        x_own = jnp.where(high, at_half(x_high, h), at_half(x_low, h))
        x_other = jnp.where(
            high, x_from_low, jnp.where(group == 0, stream_half(tokens, 1, h), x_from_high)
        )
        cot_own = jnp.where(
            high, at_half(cot_high, h), jnp.where(group == 0, straight[h], at_half(cot_low, h, 1))
        )
        cot_other = jnp.where(high, cot_from_low, jnp.where(group == 0, crossed[h], cot_from_high))
        pieces.append([x_own, x_other, cot_own, cot_other])

    prepared = prepare_call(pieces[0], own_copy, lists, weights)
    grads = grads_call(pieces[1], prepared, own_copy, lists, weights, pattern, shares)
    share = lax.psum_scatter(grads, "dp", scatter_dimension=0, tiled=True)[0].astype(jnp.float32)
    token_total = 2 * rows * shares
    step_direction, master_next = adam_update(share, master[0], moment[0], variance[0], token_total)
    return (step_direction[None], master_next[None])


def solution(mesh):
    rows_split = P(None, None, "dp", None)
    by_section = P("section", None, None, "dp", None)
    return jax.shard_map(
        shards,
        mesh=mesh,
        in_specs=(
            rows_split,
            rows_split,
            P("section", None, None, None, None, None),
            P("section", None, None, None, None),
            by_section,
            by_section,
            by_section,
        ),
        out_specs=(by_section, by_section),
        check_vma=False,
    )
```

```python
import functools

import jax
import jax.numpy as jnp
from jax import lax
from jax.experimental import pallas as pl
from jax.experimental.pallas import tpu as pltpu
from jax.sharding import PartitionSpec as P

BS = 128
FF_BLOCKS = 8192 // BS
norm_eps = 1e-06
gelu_coef = 0.7978845608028654
gelu_cubic = gelu_coef * 0.044715
beta_first = 0.9
beta_second = 0.95
adam_eps = 1e-08
learn_rate = 0.001
decay_rate = 0.1
update_count = 10
ROW_TILE = 16
EXTRA_BATCH = 8
VMEM_LIMIT = 60 * 1024 * 1024
UP_WIDE, DOWN_WIDE, DOWN_NARROW, UP_NARROW = range(4)
FIELDS = 9
FIRST, FIRST_TAKE, SECOND, SECOND_TAKE, PUT, EXTRA, EXTRA_TAKE, EXTRA_PUT, COUNT = range(FIELDS)


def block_lists(pattern):
    total = pattern.shape[2]
    up_row, up_col = pattern[:, 0, :, 0], pattern[:, 0, :, 1]
    down_row, down_col = pattern[:, 1, :, 0], pattern[:, 1, :, 1]
    key = jnp.stack([up_col, down_row, down_col, up_row], 1)
    take = jnp.stack([up_row, down_col, down_row, up_col], 1)
    order = jnp.arange(total, dtype=jnp.int32)
    before = order[None, :] < order[:, None]

    def count(mask):
        return jnp.sum(mask.astype(jnp.int32), axis=-1)

    same = key[..., None, :] == key[..., :, None]
    rank = count(same & before)
    even = rank % 2 == 0
    wide = (jnp.arange(4) < 2)[None, :, None]
    extra = rank >= 2
    extra_place = count(extra[..., None, :] & before)
    pair = count((key[..., None, :] < key[..., :, None]) & even[..., None, :]) + rank // 2
    place_first = jnp.where(wide, jnp.where(rank == 0, key, -1), jnp.where(even, pair, -1))
    place_second = jnp.where(wide, jnp.where(rank == 1, key, -1), jnp.where(even, -1, pair))
    place_extra = jnp.where(wide & extra, extra_place, -1)
    number = jnp.broadcast_to(order, key.shape)
    places = jnp.stack(
        [place_first] * 2 + [place_second] * 2 + [place_first] + [place_extra] * 3, 2
    )
    lowered = number - total
    values = jnp.stack([lowered, take, lowered, take, key, lowered, take, key], 2)
    hit = places[..., None, :] == order[:, None]
    fields = jnp.sum(jnp.where(hit, values[..., None, :], 0), axis=-1)
    slot = jnp.arange(8)
    numbered = (slot == FIRST) | (slot == SECOND) | (slot == EXTRA)
    fields = fields + jnp.where(numbered, total, 0)[:, None]
    counts = jnp.where(wide[..., 0], count(extra), count(even))
    counts = jnp.broadcast_to(counts[..., None, None], key.shape[:2] + (1, total))
    return jnp.concatenate([fields, counts], axis=2).astype(jnp.int32).reshape(-1)


class Lists:
    def __init__(self, ref, copy, total):
        self.ref, self.total = ref, total
        self.base = copy * (4 * FIELDS * total)

    def __call__(self, kind, field, index):
        return self.ref[self.base + ((kind * FIELDS + field) * self.total) + index]


def hidden_of(preact):
    inner = preact * (gelu_coef + gelu_cubic * (preact * preact))
    half = 0.5 * preact
    return half + half * jnp.tanh(inner)


def slope_of(preact):
    cubic = gelu_cubic * (preact * preact)
    tangent = jnp.tanh(preact * (gelu_coef + cubic))
    bend = preact * (gelu_coef + 3.0 * cubic)
    return (0.5 + 0.5 * tangent) * (1.0 + bend * (1.0 - tangent))


def both_of(preact):
    cubic = gelu_cubic * (preact * preact)
    tangent = jnp.tanh(preact * (gelu_coef + cubic))
    bend = preact * (gelu_coef + 3.0 * cubic)
    half = 0.5 + 0.5 * tangent
    return (preact * half, half * (1.0 + bend * (1.0 - tangent)))


def dot_plain(left, right):
    return jnp.dot(left, right, preferred_element_type=jnp.float32)


def dot_right_t(left, right):
    return lax.dot_general(left, right, (((1,), (1,)), ((), ())), preferred_element_type=jnp.float32)


def each(count, body, unroll=1):
    def one(i, carry):
        body(i)
        return carry

    lax.fori_loop(0, count, one, 0, unroll=unroll)


def fill_normed(x_ref, normed, base):
    rows, width = x_ref.shape

    def tile(i):
        at = pl.multiple_of(i * ROW_TILE, ROW_TILE)
        wide = x_ref[pl.ds(at, ROW_TILE), :].astype(jnp.float32)
        factor = lax.rsqrt(jnp.mean(wide * wide, axis=-1, keepdims=True) + norm_eps)
        value = (wide * factor).astype(jnp.bfloat16)
        for b in range(width // BS):
            normed[b, pl.ds(base + at, ROW_TILE), :] = value[:, b * BS : (b + 1) * BS]

    each(rows // ROW_TILE, tile, 7)


def fill_split(x_ref, split, base):
    rows, width = x_ref.shape
    for b in range(width // BS):
        split[b, pl.ds(base, rows), :] = x_ref[:, b * BS : (b + 1) * BS]


def pair_product(source, blocks, lists, kind, p, transposed):
    left = jnp.concatenate(
        [source[lists(kind, FIRST_TAKE, p)], source[lists(kind, SECOND_TAKE, p)]], axis=1
    )
    one, two = blocks[lists(kind, FIRST, p)], blocks[lists(kind, SECOND, p)]
    if transposed:
        return dot_right_t(left, jnp.concatenate([one, two], axis=1))
    return dot_plain(left, jnp.concatenate([one, two], axis=0))


def wide_pass(source, blocks, lists, kind, sums, finish, transposed):
    def main(c):
        value = pair_product(source, blocks, lists, kind, c, transposed)
        sums[c] = value
        finish(c, value)

    each(sums.shape[0], main, 16)
    dot = dot_right_t if transposed else dot_plain

    def more(e):
        c = lists(kind, EXTRA_PUT, e)
        left = source[lists(kind, EXTRA_TAKE, e)]
        value = sums[c] + dot(left, blocks[lists(kind, EXTRA, e)])
        sums[c] = value
        finish(c, value)

    def batch(i):
        for j in range(EXTRA_BATCH):
            more(i * EXTRA_BATCH + j)

    each((lists(kind, COUNT, 0) + EXTRA_BATCH - 1) // EXTRA_BATCH, batch)


def narrow_pass(source, blocks, lists, kind, sums, transposed):
    sums[...] = jnp.zeros(sums.shape, sums.dtype)

    def one(p):
        sums[lists(kind, PUT, p)] += pair_product(source, blocks, lists, kind, p, transposed)

    each((lists.total + sums.shape[0]) // 2, one, 14)


def forward_rows(x_ref, out_ref, lists, weights, scratch, slopes=None):
    normed, sums, hidden, narrow = scratch
    rows, width = x_ref.shape
    fill_normed(x_ref, normed, 0)
    weights.wait(0)

    def finish(c, value):
        if slopes is None:
            hidden[c] = hidden_of(value).astype(jnp.bfloat16)
        else:
            value, slope = both_of(value)
            hidden[c] = value.astype(jnp.bfloat16)
            slopes[c] = slope

    wide_pass(normed, weights.blocks(0), lists, UP_WIDE, sums, finish, False)
    weights.wait(1)
    narrow_pass(hidden, weights.blocks(1), lists, DOWN_NARROW, narrow, False)
    for b in range(width // BS):
        cols = slice(b * BS, (b + 1) * BS)
        out_ref[:, cols] = (x_ref[:, cols].astype(jnp.float32) + narrow[b]).astype(jnp.bfloat16)


def slope_rows(x_ref, lists, weights, scratch, slopes):
    normed, sums, hidden, narrow = scratch
    fill_normed(x_ref, normed, 0)
    weights.wait(0)

    def finish(c, value):
        slopes[c] = slope_of(value)

    wide_pass(normed, weights.blocks(0), lists, UP_WIDE, sums, finish, False)
    weights.wait(1)


def backward_rows(x_ref, cot_ref, out_ref, lists, weights, scratch, slopes):
    normed, sums, hidden, narrow = scratch
    rows, width = x_ref.shape
    fill_split(cot_ref, normed, 0)

    def finish(c, value):
        hidden[c] = (value * slopes[c]).astype(jnp.bfloat16)

    wide_pass(normed, weights.blocks(1), lists, DOWN_WIDE, sums, finish, True)
    narrow_pass(hidden, weights.blocks(0), lists, UP_NARROW, narrow, True)

    def tile(i):
        at = pl.multiple_of(i * ROW_TILE, ROW_TILE)
        wide = x_ref[pl.ds(at, ROW_TILE), :].astype(jnp.float32)
        factor = lax.rsqrt(jnp.mean(wide * wide, axis=-1, keepdims=True) + norm_eps)
        grad = jnp.concatenate(
            [narrow[b, pl.ds(at, ROW_TILE), :] for b in range(width // BS)], axis=-1
        )
        coupling = jnp.mean(wide * grad, axis=-1, keepdims=True)
        upstream = cot_ref[pl.ds(at, ROW_TILE), :].astype(jnp.float32)
        value = upstream + factor * grad - wide * (factor * factor * factor * coupling)
        out_ref[pl.ds(at, ROW_TILE), :] = value.astype(jnp.bfloat16)

    each(rows // ROW_TILE, tile)


class Weights:
    def __init__(self, hbm, local, sems, slot, copy):
        self.hbm, self.local, self.sems, self.slot, self.copy = hbm, local, sems, slot, copy

    def move(self, part):
        total = self.hbm.shape[2]
        return pltpu.make_async_copy(
            self.hbm.at[self.copy, part],
            self.local.at[self.slot, part, pl.ds(0, total)],
            self.sems.at[self.slot, part],
        )

    def start(self):
        for part in range(2):
            self.move(part).start()
            self.local[self.slot, part, self.hbm.shape[2]] = jnp.zeros((BS, BS), jnp.bfloat16)

    def wait(self, part):
        self.move(part).wait()

    def blocks(self, part):
        return self.local.at[self.slot, part]


def stage(kernel, rows_in, others, outs, scratch, slots, copies, lists, weights, flops, name):
    total = weights.shape[2]
    any_spec = pl.BlockSpec(memory_space=pl.ANY)
    smem_spec = pl.BlockSpec(memory_space=pltpu.SMEM)
    vmem_spec = pl.BlockSpec(memory_space=pltpu.VMEM)

    def body(copies_ref, lists_ref, weights_ref, *rest):
        ins, rest = rest[: len(rows_in) + len(others)], rest[len(rows_in) + len(others) :]
        results, rest = rest[: len(outs)], rest[len(outs) :]
        local, sems, rest = rest[0], rest[1], rest[2:]
        loaded = []
        for slot, which in enumerate(slots):
            copy = copies_ref[which]
            moved = Weights(weights_ref, local, sems, slot, copy)
            moved.start()
            loaded.append((Lists(lists_ref, copy, total), moved))
        kernel(loaded, ins, results, rest)

    return pl.pallas_call(
        body,
        in_specs=[smem_spec, smem_spec, any_spec]
        + [vmem_spec] * len(rows_in)
        + [any_spec] * len(others),
        out_specs=[vmem_spec if space else any_spec for space, _ in outs],
        out_shape=[shape for _, shape in outs],
        scratch_shapes=[
            pltpu.VMEM((len(slots), 2, total + 1, BS, BS), jnp.bfloat16),
            pltpu.SemaphoreType.DMA((len(slots), 2)),
        ]
        + scratch,
        name=name,
        cost_estimate=pl.CostEstimate(
            flops=flops * 8, transcendentals=0, bytes_accessed=len(slots) * weights.size
        ),
        compiler_params=pltpu.CompilerParams(vmem_limit_bytes=VMEM_LIMIT),
    )(copies, lists, weights, *rows_in, *others)


def layer_scratch(rows, width):
    return [
        pltpu.VMEM((width // BS, rows, BS), jnp.bfloat16),
        pltpu.VMEM((FF_BLOCKS, rows, BS), jnp.float32),
        pltpu.VMEM((FF_BLOCKS, rows, BS), jnp.bfloat16),
        pltpu.VMEM((width // BS, rows, BS), jnp.float32),
    ]


def slope_scratch(rows):
    return [pltpu.VMEM((FF_BLOCKS, rows, BS), jnp.float32)]


def rows_out(array):
    return (True, jax.ShapeDtypeStruct(array.shape, jnp.bfloat16))


def dense_flops(rows, weights):
    return 2 * rows * weights.shape[2] * BS * BS * 2


def forward_call(x, slots, copies, lists, weights):
    rows, width = x.shape

    def kernel(loaded, ins, results, scratch):
        source = ins[0]
        for (own_lists, moved), out in zip(loaded, results):
            forward_rows(source, out, own_lists, moved, scratch)
            source = out

    flops = dense_flops(rows, weights) * len(slots)
    return stage(
        kernel, [x], [], [rows_out(x)] * len(slots), layer_scratch(rows, width), slots, copies,
        lists, weights, flops, "forward"
    )


def turn_call(x, targets, copies, lists, weights):
    rows, width = x.shape

    def kernel(loaded, ins, results, scratch):
        x_ref, target_ref = ins
        residue, out = results
        own_lists, moved = loaded[0]
        layer, slopes = scratch[:-1], scratch[-1]
        forward_rows(x_ref, residue, own_lists, moved, layer, slopes)
        for b in range(width // BS):
            cols = slice(b * BS, (b + 1) * BS)
            difference = residue[:, cols].astype(jnp.float32) - target_ref[:, cols].astype(jnp.float32)
            residue[:, cols] = difference.astype(jnp.bfloat16)
        backward_rows(x_ref, residue, out, own_lists, moved, layer, slopes)

    return stage(
        kernel, [x, targets], [], [rows_out(x)] * 2,
        layer_scratch(rows, width) + slope_scratch(rows), [1], copies, lists, weights,
        2 * dense_flops(rows, weights), "turn"
    )


def backward_call(xs, cot, slots, copies, lists, weights):
    rows, width = cot.shape

    def kernel(loaded, ins, results, scratch):
        layer, slopes = scratch[:-1], scratch[-1]
        upstream = ins[-1]
        for (own_lists, moved), x_ref, out in zip(loaded, ins, results):
            slope_rows(x_ref, own_lists, moved, layer, slopes)
            backward_rows(x_ref, upstream, out, own_lists, moved, layer, slopes)
            upstream = out

    return stage(
        kernel, list(xs) + [cot], [], [rows_out(cot)] * len(slots),
        layer_scratch(rows, width) + slope_scratch(rows), slots, copies, lists, weights,
        2 * dense_flops(rows, weights) * len(slots), "backward"
    )


def own_layer_rows(ins, own_lists, moved, normed, split, slopes, sums, hidden, grad_pre):
    pieces = len(ins) // 2
    rows = ins[0].shape[0]
    for i in range(pieces):
        fill_normed(ins[i], normed, i * rows)
        fill_split(ins[pieces + i], split, i * rows)
    moved.wait(0)

    def finish_up(c, value):
        value, slope = both_of(value)
        hidden[c] = value.astype(jnp.bfloat16)
        slopes[c] = slope

    wide_pass(normed, moved.blocks(0), own_lists, UP_WIDE, sums, finish_up, False)
    moved.wait(1)

    def finish_down(c, value):
        grad_pre[c] = (value * slopes[c]).astype(jnp.bfloat16)

    wide_pass(split, moved.blocks(1), own_lists, DOWN_WIDE, sums, finish_down, True)


def prepare_call(pieces, copies, lists, weights):
    rows, width = pieces[0].shape
    rows = rows * len(pieces) // 2
    narrow_shape = (width // BS, BS, rows)
    wide_shape = (FF_BLOCKS, rows, BS)

    def kernel(loaded, ins, results, scratch):
        normed, split, slopes, sums, hidden, grad_pre, sems = scratch
        own_lists, moved = loaded[0]
        own_layer_rows(ins, own_lists, moved, normed, split, slopes, sums, hidden, grad_pre)
        moves = [
            pltpu.make_async_copy(source, target, sems.at[i])
            for i, (source, target) in enumerate(
                zip([hidden, grad_pre, normed, split], results)
            )
        ]
        for move in moves:
            move.start()
        for move in moves:
            move.wait()

    shapes = [wide_shape, wide_shape, (width // BS, rows, BS), (width // BS, rows, BS)]
    return stage(
        kernel, pieces, [], [(False, jax.ShapeDtypeStruct(s, jnp.bfloat16)) for s in shapes],
        [
            pltpu.VMEM((width // BS, rows, BS), jnp.bfloat16),
            pltpu.VMEM((width // BS, rows, BS), jnp.bfloat16),
            pltpu.VMEM(wide_shape, jnp.float32),
            pltpu.VMEM(wide_shape, jnp.float32),
            pltpu.VMEM(wide_shape, jnp.bfloat16),
            pltpu.VMEM(wide_shape, jnp.bfloat16),
            pltpu.SemaphoreType.DMA((4,)),
        ],
        [0], copies, lists, weights, 2 * dense_flops(rows, weights), "prepare"
    )


def grads_call(pieces, prepared, copies, lists, weights, pattern, shares):
    rows, width = pieces[0].shape
    rows = rows * len(pieces) // 2
    total = weights.shape[2]
    share_rows = BS // shares
    wide_shape = (FF_BLOCKS, rows, BS)
    pattern_flat = pattern[0].reshape(-1)

    def kernel(loaded, ins, results, scratch):
        normed, split, slopes, sums, hidden, grad_pre, turned, sems, pattern_sem, cells = scratch
        out = results[0]
        own_lists, moved = loaded[0]
        stored, pattern_ref = ins[-5:-1], ins[-1]
        load_cells = pltpu.make_async_copy(pattern_ref, cells, pattern_sem)
        load_cells.start()
        moves = [
            pltpu.make_async_copy(source, target.at[0], sems.at[i])
            for i, (source, target) in enumerate(zip(stored, [hidden, grad_pre, normed, split]))
        ]
        for move in moves:
            move.start()
        own_layer_rows(
            ins[:-5], own_lists, moved, normed.at[1], split.at[1], slopes, sums,
            hidden.at[1], grad_pre.at[1]
        )
        for move in moves:
            move.wait()
        load_cells.wait()
        for which, source in enumerate((normed, split)):
            for b in range(width // BS):
                for part in range(2):
                    turned[which, b, part] = source[part, b].T

        def one(k):
            row, col = cells[2 * k], cells[2 * k + 1]
            up = dot_plain(turned[0, row, 0], grad_pre[0, col])
            up = (up + dot_plain(turned[0, row, 1], grad_pre[1, col])).astype(jnp.bfloat16)
            row, col = cells[2 * (total + k)], cells[2 * (total + k) + 1]
            down = dot_plain(turned[1, col, 0], hidden[0, row])
            down = down + dot_plain(turned[1, col, 1], hidden[1, row])
            down = down.T.astype(jnp.bfloat16)
            for share in range(shares):
                span = slice(share * share_rows, (share + 1) * share_rows)
                out[share, 0, k] = up[span]
                out[share, 1, k] = down[span]

        each(total, one, 6)

    return stage(
        kernel, pieces, list(prepared) + [pattern_flat],
        [(True, jax.ShapeDtypeStruct((shares, 2, total, share_rows, BS), jnp.bfloat16))],
        [
            pltpu.VMEM((2, width // BS, rows, BS), jnp.bfloat16),
            pltpu.VMEM((2, width // BS, rows, BS), jnp.bfloat16),
            pltpu.VMEM(wide_shape, jnp.float32),
            pltpu.VMEM(wide_shape, jnp.float32),
            pltpu.VMEM((2,) + wide_shape, jnp.bfloat16),
            pltpu.VMEM((2,) + wide_shape, jnp.bfloat16),
            pltpu.VMEM((2, width // BS, 2, BS, rows), jnp.bfloat16),
            pltpu.SemaphoreType.DMA((4,)),
            pltpu.SemaphoreType.DMA,
            pltpu.SMEM((2 * total * 2,), jnp.int32),
        ],
        [0], copies, lists, weights, 4 * dense_flops(rows, weights), "grads"
    )[0]


def adam_update(grad_sum, master, moment, variance, token_total):
    gradient = grad_sum / token_total
    moment_next = beta_first * moment + (1.0 - beta_first) * gradient
    variance_next = beta_second * variance + (1.0 - beta_second) * gradient * gradient
    corrected = moment_next / (1.0 - beta_first**update_count)
    spread = jnp.sqrt(variance_next / (1.0 - beta_second**update_count))
    step_direction = corrected / (spread + adam_eps)
    return (step_direction, master - learn_rate * (step_direction + decay_rate * master))


def shards(tokens, targets, weights, pattern, master, moment, variance):
    section = lax.axis_index("section")
    sections = lax.axis_size("section")
    shares = lax.axis_size("dp")
    groups = sections // 2
    micro, rows_each, width = tokens.shape[1:]
    rows = micro * rows_each
    half = rows // 2
    high = section >= groups
    high_member = high.astype(jnp.int32)
    group = jnp.minimum(section, sections - 1 - section)
    copies = jnp.stack([high_member, 1 - high_member])
    own_copy = jnp.stack([jnp.zeros_like(high_member)] * 2)
    weights, pattern = weights[0], pattern[0]
    lists = block_lists(pattern)
    mirror = lambda i: sections - 1 - i

    def stream_half(array, member, h):
        stream = lax.dynamic_index_in_dim(array, member, 0, keepdims=False)
        return stream.reshape(rows, width)[h * half : (h + 1) * half]

    def lane(i, h):
        other = mirror(i + 1) if h else i + 1
        return [(i, other), (mirror(i), mirror(other))]

    def inward(x, i, h):
        return lax.ppermute(x, "section", lane(i, h))

    def outward(x, i, h):
        return lax.ppermute(x, "section", [(b, a) for a, b in lane(i, h)])

    halves = range(2)
    x_low = [[stream_half(tokens, high_member, h) for h in halves]]
    x_high, cot_low, cot_high = [[None] * groups for _ in range(3)]
    current = x_low[0]
    for i in range(groups - 1):
        current = [inward(forward_call(current[h], [0], copies, lists, weights)[0], i, h) for h in halves]
        x_low.append(current)
    both = [forward_call(current[h], [0, 1], copies, lists, weights) for h in halves]
    x_high[groups - 1] = [b[0] for b in both]
    current = [b[1] for b in both]
    for i in reversed(range(groups - 1)):
        current = [outward(current[h], i, h) for h in halves]
        x_high[i] = current
        if i > 0:
            current = [forward_call(current[h], [1], copies, lists, weights)[0] for h in halves]
    aims = [stream_half(targets, high_member, h) for h in halves]
    turned = [turn_call(current[h], aims[h], copies, lists, weights) for h in halves]
    cot_high[0] = [t[0] for t in turned]
    current = [t[1] for t in turned]
    for i in range(groups - 1):
        current = [inward(current[h], i, h) for h in halves]
        cot_high[i + 1] = current
        if i + 1 < groups - 1:
            current = [
                backward_call([x_high[i + 1][h]], current[h], [1], copies, lists, weights)[0]
                for h in halves
            ]
    last = groups - 1
    both = [
        backward_call([x_high[last][h], x_low[last][h]], current[h], [1, 0], copies, lists, weights)
        for h in halves
    ]
    cot_low[last] = [b[0] for b in both]
    current = [b[1] for b in both]
    for i in reversed(range(1, last)):
        current = [outward(current[h], i, h) for h in halves]
        cot_low[i] = current
        current = [
            backward_call([x_low[i][h]], current[h], [0], copies, lists, weights)[0] for h in halves
        ]
    from_low = [lax.ppermute(current[h], "section", [(1, 0)]) for h in halves]
    from_high = [lax.ppermute(current[h], "section", [(mirror(1), 0)]) for h in halves]

    to_low = [(mirror(i), i) for i in range(1, groups)]
    to_high = [(i, mirror(i)) for i in range(groups)]

    def at_half(records, h, start=0):
        value = records[start][h]
        for i in range(start + 1, groups):
            value = jnp.where(group == i, records[i][h], value)
        return value

    pieces = []
    first_group = (group == 0) & ~high
    for h in halves:
        x_from_high = lax.ppermute(at_half(x_low, h, 1), "section", to_low)
        x_from_low = lax.ppermute(at_half(x_high, h), "section", to_high)
        cot_from_high = lax.ppermute(at_half(cot_low, h, 1), "section", to_low)
        cot_from_low = lax.ppermute(at_half(cot_high, h), "section", to_high)
        straight, crossed = (from_high, from_low) if h else (from_low, from_high)
        x_own = jnp.where(high, at_half(x_high, h), at_half(x_low, h))
        x_other = jnp.where(
            high, x_from_low, jnp.where(group == 0, stream_half(tokens, 1, h), x_from_high)
        )
        cot_own = jnp.where(
            high, at_half(cot_high, h), jnp.where(group == 0, straight[h], at_half(cot_low, h, 1))
        )
        cot_other = jnp.where(high, cot_from_low, jnp.where(group == 0, crossed[h], cot_from_high))
        pieces.append([x_own, x_other, cot_own, cot_other])

    prepared = prepare_call(pieces[0], own_copy, lists, weights)
    grads = grads_call(pieces[1], prepared, own_copy, lists, weights, pattern, shares)
    share = lax.psum_scatter(grads, "dp", scatter_dimension=0, tiled=True)[0].astype(jnp.float32)
    token_total = 2 * rows * shares
    step_direction, master_next = adam_update(share, master[0], moment[0], variance[0], token_total)
    return (step_direction[None], master_next[None])


def solution(mesh):
    rows_split = P(None, None, "dp", None)
    by_section = P("section", None, None, "dp", None)
    return jax.shard_map(
        shards,
        mesh=mesh,
        in_specs=(
            rows_split,
            rows_split,
            P("section", None, None, None, None, None),
            P("section", None, None, None, None),
            by_section,
            by_section,
            by_section,
        ),
        out_specs=(by_section, by_section),
        check_vma=False,
    )
```

```python
import functools

import jax
import jax.numpy as jnp
from jax import lax
from jax.experimental import pallas as pl
from jax.experimental.pallas import tpu as pltpu
from jax.sharding import PartitionSpec as P

BS = 128
FF_BLOCKS = 8192 // BS
norm_eps = 1e-06
gelu_coef = 0.7978845608028654
gelu_cubic = gelu_coef * 0.044715
beta_first = 0.9
beta_second = 0.95
adam_eps = 1e-08
learn_rate = 0.001
decay_rate = 0.1
update_count = 10
ROW_TILE = 16
EXTRA_BATCH = 8
VMEM_LIMIT = 48 * 1024 * 1024
COST = 4_000_000_000
LOW_LAYER, HIGH_LAYER, OWN_LAYER, HIGH, GROUP = range(5)
UP_WIDE, DOWN_WIDE, DOWN_NARROW, UP_NARROW = range(4)
FIELDS = 9
FIRST, FIRST_TAKE, SECOND, SECOND_TAKE, PUT, EXTRA, EXTRA_TAKE, EXTRA_PUT, COUNT = range(FIELDS)


def block_lists(pattern, width):
    total = pattern.shape[2]
    up_row, up_col = pattern[:, 0, :, 0], pattern[:, 0, :, 1]
    down_row, down_col = pattern[:, 1, :, 0], pattern[:, 1, :, 1]
    key = jnp.stack([up_col, down_row, down_col, up_row], 1)
    take = jnp.stack([up_row, down_col, down_row, up_col], 1)
    order = jnp.arange(total, dtype=jnp.int32)
    before = order[None, :] < order[:, None]

    def count(mask):
        return jnp.sum(mask.astype(jnp.int32), axis=-1)

    same = key[..., None, :] == key[..., :, None]
    rank = count(same & before)
    even = rank % 2 == 0
    wide = (jnp.arange(4) < 2)[None, :, None]
    extra = rank >= 2
    extra_place = count(extra[..., None, :] & before)
    pair = count((key[..., None, :] < key[..., :, None]) & even[..., None, :]) + rank // 2
    place_first = jnp.where(wide, jnp.where(rank == 0, key, -1), jnp.where(even, pair, -1))
    place_second = jnp.where(wide, jnp.where(rank == 1, key, -1), jnp.where(even, -1, pair))
    place_extra = jnp.where(wide & extra, extra_place, -1)
    number = jnp.broadcast_to(order, key.shape)
    places = jnp.stack(
        [place_first] * 2 + [place_second] * 2 + [place_first] + [place_extra] * 3, 2
    )
    absent = jnp.where(wide, width // BS, FF_BLOCKS)
    lowered = take - absent
    values = jnp.stack([number, lowered, number, lowered, key, number, lowered, key], 2)
    hit = places[..., None, :] == order[:, None]
    fields = jnp.sum(jnp.where(hit, values[..., None, :], 0), axis=-1)
    slot = jnp.arange(8)
    taken = (slot == FIRST_TAKE) | (slot == SECOND_TAKE) | (slot == EXTRA_TAKE)
    fields = fields + jnp.where(taken[:, None], absent[..., None], 0)
    counts = jnp.where(wide[..., 0], count(extra), count(even))
    counts = jnp.broadcast_to(counts[..., None, None], key.shape[:2] + (1, total))
    lists = jnp.concatenate([fields, counts], axis=2).astype(jnp.int32)
    return jnp.concatenate([lists.reshape(-1), pattern[0].reshape(-1)])


class Lists:
    def __init__(self, ref, copy, total):
        self.ref, self.total = ref, total
        self.base = copy * (4 * FIELDS * total)
        self.cells = 2 * 4 * FIELDS * total

    def __call__(self, kind, field, index):
        return self.ref[self.base + ((kind * FIELDS + field) * self.total) + index]


def hidden_of(preact):
    inner = preact * (gelu_coef + gelu_cubic * (preact * preact))
    half = 0.5 * preact
    return half + half * jnp.tanh(inner)


def slope_of(preact):
    cubic = gelu_cubic * (preact * preact)
    tangent = jnp.tanh(preact * (gelu_coef + cubic))
    bend = preact * (gelu_coef + 3.0 * cubic)
    return (0.5 + 0.5 * tangent) * (1.0 + bend * (1.0 - tangent))


def both_of(preact):
    cubic = gelu_cubic * (preact * preact)
    tangent = jnp.tanh(preact * (gelu_coef + cubic))
    bend = preact * (gelu_coef + 3.0 * cubic)
    half = 0.5 + 0.5 * tangent
    return (preact * half, half * (1.0 + bend * (1.0 - tangent)))


def dot_plain(left, right):
    return jnp.dot(left, right, preferred_element_type=jnp.float32)


def dot_right_t(left, right):
    return lax.dot_general(left, right, (((1,), (1,)), ((), ())), preferred_element_type=jnp.float32)


def each(count, body, unroll=1):
    def one(i, carry):
        body(i)
        return carry

    lax.fori_loop(0, count, one, 0, unroll=unroll)


def fill_normed(x_ref, normed, base):
    rows, width = x_ref.shape

    def tile(i):
        at = pl.multiple_of(i * ROW_TILE, ROW_TILE)
        wide = x_ref[pl.ds(at, ROW_TILE), :].astype(jnp.float32)
        factor = lax.rsqrt(jnp.mean(wide * wide, axis=-1, keepdims=True) + norm_eps)
        value = (wide * factor).astype(jnp.bfloat16)
        for b in range(width // BS):
            normed[b, pl.ds(base + at, ROW_TILE), :] = value[:, b * BS : (b + 1) * BS]

    each(rows // ROW_TILE, tile, 7)


def fill_split(x_ref, split, base):
    rows, width = x_ref.shape
    for b in range(width // BS):
        split[b, pl.ds(base, rows), :] = x_ref[:, b * BS : (b + 1) * BS]


def pair_product(source, blocks, lists, kind, p, transposed):
    left = jnp.concatenate(
        [source[lists(kind, FIRST_TAKE, p)], source[lists(kind, SECOND_TAKE, p)]], axis=1
    )
    one, two = blocks[lists(kind, FIRST, p)], blocks[lists(kind, SECOND, p)]
    if transposed:
        return dot_right_t(left, jnp.concatenate([one, two], axis=1))
    return dot_plain(left, jnp.concatenate([one, two], axis=0))


def wide_pass(source, blocks, lists, kind, sums, finish, transposed, batch=16, ahead=None):
    def main(i):
        if ahead is not None:
            ahead(i)
        for j in range(batch):
            c = i * batch + j
            value = pair_product(source, blocks, lists, kind, c, transposed)
            sums[c] = value
            finish(c, value)

    each(sums.shape[0] // batch, main)
    dot = dot_right_t if transposed else dot_plain

    def more(e):
        c = lists(kind, EXTRA_PUT, e)
        left = source[lists(kind, EXTRA_TAKE, e)]
        value = sums[c] + dot(left, blocks[lists(kind, EXTRA, e)])
        sums[c] = value
        finish(c, value)

    def batch(i):
        for j in range(EXTRA_BATCH):
            more(i * EXTRA_BATCH + j)

    each((lists(kind, COUNT, 0) + EXTRA_BATCH - 1) // EXTRA_BATCH, batch)


def narrow_pass(source, blocks, lists, kind, sums, transposed):
    sums[...] = jnp.zeros(sums.shape, sums.dtype)

    def one(p):
        sums[lists(kind, PUT, p)] += pair_product(source, blocks, lists, kind, p, transposed)

    each((lists.total + sums.shape[0]) // 2, one, 14)


def forward_rows(x_ref, out_ref, layer, scratch, slopes=None):
    normed, sums, hidden, narrow = scratch
    rows, width = x_ref.shape
    fill_normed(x_ref, normed, 0)

    def finish(c, value):
        if slopes is None:
            hidden[c] = hidden_of(value).astype(jnp.bfloat16)
        else:
            value, slope = both_of(value)
            hidden[c] = value.astype(jnp.bfloat16)
            slopes[c] = slope

    wide_pass(normed, layer.up, layer.lists, UP_WIDE, sums, finish, False)
    narrow_pass(hidden, layer.down, layer.lists, DOWN_NARROW, narrow, False)
    for b in range(width // BS):
        cols = slice(b * BS, (b + 1) * BS)
        out_ref[:, cols] = (x_ref[:, cols].astype(jnp.float32) + narrow[b]).astype(jnp.bfloat16)


def slope_rows(x_ref, layer, scratch, slopes):
    normed, sums, hidden, narrow = scratch
    fill_normed(x_ref, normed, 0)

    def finish(c, value):
        slopes[c] = slope_of(value)

    wide_pass(normed, layer.up, layer.lists, UP_WIDE, sums, finish, False)


def backward_rows(x_ref, cot_ref, out_ref, layer, scratch, slopes):
    normed, sums, hidden, narrow = scratch
    rows, width = x_ref.shape
    fill_split(cot_ref, normed, 0)

    def finish(c, value):
        hidden[c] = (value * slopes[c]).astype(jnp.bfloat16)

    wide_pass(normed, layer.down, layer.lists, DOWN_WIDE, sums, finish, True)
    narrow_pass(hidden, layer.up, layer.lists, UP_NARROW, narrow, True)

    def tile(i):
        at = pl.multiple_of(i * ROW_TILE, ROW_TILE)
        wide = x_ref[pl.ds(at, ROW_TILE), :].astype(jnp.float32)
        factor = lax.rsqrt(jnp.mean(wide * wide, axis=-1, keepdims=True) + norm_eps)
        grad = jnp.concatenate(
            [narrow[b, pl.ds(at, ROW_TILE), :] for b in range(width // BS)], axis=-1
        )
        coupling = jnp.mean(wide * grad, axis=-1, keepdims=True)
        upstream = cot_ref[pl.ds(at, ROW_TILE), :].astype(jnp.float32)
        value = upstream + factor * grad - wide * (factor * factor * factor * coupling)
        out_ref[pl.ds(at, ROW_TILE), :] = value.astype(jnp.bfloat16)

    each(rows // ROW_TILE, tile)


def own_cell(layer, part, k):
    lists = layer.lists
    at = lists.cells + 2 * (part * lists.total + k)
    return lists.ref[at], lists.ref[at + 1]


class Layer:
    def __init__(self, info, lists_ref, weights_ref, which):
        copy = info[which]
        self.lists = Lists(lists_ref, copy, weights_ref.shape[2])
        self.up = weights_ref.at[copy, 0]
        self.down = weights_ref.at[copy, 1]


def stage(kernel, local_in, remote_in, outs, scratch, operands, cost, name):
    info, lists, weights = operands
    any_spec = pl.BlockSpec(memory_space=pl.ANY)
    smem_spec = pl.BlockSpec(memory_space=pltpu.SMEM)
    vmem_spec = pl.BlockSpec(memory_space=pltpu.VMEM)
    in_total = len(local_in) + len(remote_in)

    def body(info_ref, lists_ref, weights_ref, *rest):
        ins, results, own = rest[:in_total], rest[in_total : in_total + len(outs)], rest[in_total + len(outs) :]

        def layer(which):
            return Layer(info_ref, lists_ref, weights_ref, which)

        kernel(layer, info_ref, ins, results, own)

    return pl.pallas_call(
        body,
        in_specs=[smem_spec, smem_spec, vmem_spec]
        + [vmem_spec] * len(local_in)
        + [any_spec] * len(remote_in),
        out_specs=[vmem_spec if space else any_spec for space, _ in outs],
        out_shape=[shape for _, shape in outs],
        scratch_shapes=scratch,
        name=name,
        cost_estimate=pl.CostEstimate(flops=cost, transcendentals=0, bytes_accessed=0),
        compiler_params=pltpu.CompilerParams(vmem_limit_bytes=VMEM_LIMIT),
    )(info, lists, weights, *local_in, *remote_in)


def layer_scratch(rows, width):
    return [
        pltpu.VMEM((width // BS + 1, rows, BS), jnp.bfloat16),
        pltpu.VMEM((FF_BLOCKS, rows, BS), jnp.float32),
        pltpu.VMEM((FF_BLOCKS + 1, rows, BS), jnp.bfloat16),
        pltpu.VMEM((width // BS, rows, BS), jnp.float32),
    ]


def slope_scratch(rows):
    return [pltpu.VMEM((FF_BLOCKS, rows, BS), jnp.float32)]


def shape_of(shape, dtype=jnp.bfloat16):
    return jax.ShapeDtypeStruct(shape, dtype)


def clear_spare(*refs):
    for ref in refs:
        ref[ref.shape[0] - 1] = jnp.zeros(ref.shape[1:], ref.dtype)


def forward_call(x, whichs, operands):
    rows, width = x.shape

    def kernel(layer, info, ins, results, scratch):
        clear_spare(scratch[0], scratch[2])
        source = ins[0]
        for which, out in zip(whichs, results):
            forward_rows(source, out, layer(which), scratch)
            source = out

    return stage(
        kernel, [x], [], [(True, shape_of(x.shape))] * len(whichs), layer_scratch(rows, width),
        operands, COST * len(whichs), "forward"
    )


def enter_call(tokens, h, rows, operands):
    width = tokens.shape[-1]

    def kernel(layer, info, ins, results, scratch):
        *scratch, x_ref, sem = scratch
        load = pltpu.make_async_copy(ins[0].at[info[HIGH], pl.ds(h * rows, rows)], x_ref, sem)
        load.start()
        clear_spare(scratch[0], scratch[2])
        load.wait()
        forward_rows(x_ref, results[0], layer(LOW_LAYER), scratch)

    return stage(
        kernel, [], [tokens], [(True, shape_of((rows, width)))],
        layer_scratch(rows, width)
        + [pltpu.VMEM((rows, width), jnp.bfloat16), pltpu.SemaphoreType.DMA],
        operands, COST, "enter"
    )


def turn_call(x, targets, h, operands):
    rows, width = x.shape

    def kernel(layer, info, ins, results, scratch):
        *layer_refs, slopes, aim, sem = scratch
        x_ref, target_ref = ins
        residue, out = results
        load = pltpu.make_async_copy(target_ref.at[info[HIGH], pl.ds(h * rows, rows)], aim, sem)
        load.start()
        clear_spare(layer_refs[0], layer_refs[2])
        own = layer(HIGH_LAYER)
        forward_rows(x_ref, residue, own, layer_refs, slopes)
        load.wait()
        for b in range(width // BS):
            cols = slice(b * BS, (b + 1) * BS)
            difference = residue[:, cols].astype(jnp.float32) - aim[:, cols].astype(jnp.float32)
            residue[:, cols] = difference.astype(jnp.bfloat16)
        backward_rows(x_ref, residue, out, own, layer_refs, slopes)

    return stage(
        kernel, [x], [targets], [(True, shape_of(x.shape))] * 2,
        layer_scratch(rows, width) + slope_scratch(rows)
        + [pltpu.VMEM((rows, width), jnp.bfloat16), pltpu.SemaphoreType.DMA],
        operands, 3 * COST, "turn"
    )


def backward_call(xs, cot, whichs, operands):
    rows, width = cot.shape

    def kernel(layer, info, ins, results, scratch):
        *layer_refs, slopes = scratch
        clear_spare(layer_refs[0], layer_refs[2])
        upstream = ins[-1]
        for which, x_ref, out in zip(whichs, ins, results):
            own = layer(which)
            slope_rows(x_ref, own, layer_refs, slopes)
            backward_rows(x_ref, upstream, out, own, layer_refs, slopes)
            upstream = out

    return stage(
        kernel, list(xs) + [cot], [], [(True, shape_of(cot.shape))] * len(whichs),
        layer_scratch(rows, width) + slope_scratch(rows), operands, 2 * COST * len(whichs),
        "backward"
    )


def fetch_pieces(info, choices, refs, local, sem):
    first = (info[HIGH] == 0) & (info[GROUP] == 0)
    moves = []
    for piece, options in enumerate(choices):
        for kind, wanted, number, index in options:
            source = refs[number] if index is None else refs[number].at[index]
            move = pltpu.make_async_copy(source, local.at[piece], sem.at[piece])
            if kind == "first":
                condition = first
            elif kind == "own":
                condition = (info[HIGH] == wanted[0]) & (info[GROUP] == wanted[1]) & ~first
            else:
                condition = ~first

            @pl.when(condition)
            def go(move=move):
                move.start()

        moves.append(move)
    return moves


def ups_call(refs, choices, after, rows, width, operands):
    pieces = len(choices)
    all_rows = rows * pieces
    part_rows = all_rows // 2

    def kernel(layer, info, ins, results, scratch):
        x_refs, normed, sums, hidden, slopes, sem, out_sem = scratch
        hidden_out, slopes_out, normed_out = results
        moves = fetch_pieces(info, choices, ins, x_refs, sem)
        own = layer(OWN_LAYER)
        outs = []
        for part in range(2):
            here = normed.at[part]
            clear_spare(here)
            for i in range(pieces // 2):
                piece = part * (pieces // 2) + i
                moves[piece].wait()
                fill_normed(x_refs.at[piece], here, i * rows)

            def finish(c, value):
                value, slope = both_of(value)
                hidden[part, c] = value.astype(jnp.bfloat16)
                slopes[part, c] = slope

            wide_pass(here, own.up, own.lists, UP_WIDE, sums, finish, False, 8)
            span = pl.ds(part * part_rows, part_rows)
            blocks = pl.ds(0, width // BS)
            outs += [
                pltpu.make_async_copy(hidden.at[part], hidden_out.at[:, span], out_sem.at[part, 0]),
                pltpu.make_async_copy(slopes.at[part], slopes_out.at[:, span], out_sem.at[part, 1]),
                pltpu.make_async_copy(here.at[blocks], normed_out.at[:, span], out_sem.at[part, 2]),
            ]
            for move in outs[-3:]:
                move.start()
        for move in outs:
            move.wait()

    return stage(
        kernel, [], refs + [after],
        [
            (False, shape_of((FF_BLOCKS, all_rows, BS))),
            (False, shape_of((FF_BLOCKS, all_rows, BS), jnp.float32)),
            (False, shape_of((width // BS, all_rows, BS))),
        ],
        [
            pltpu.VMEM((pieces, rows, width), jnp.bfloat16),
            pltpu.VMEM((2, width // BS + 1, part_rows, BS), jnp.bfloat16),
            pltpu.VMEM((FF_BLOCKS, part_rows, BS), jnp.float32),
            pltpu.VMEM((2, FF_BLOCKS, part_rows, BS), jnp.bfloat16),
            pltpu.VMEM((2, FF_BLOCKS, part_rows, BS), jnp.float32),
            pltpu.SemaphoreType.DMA((pieces,)),
            pltpu.SemaphoreType.DMA((2, 3)),
        ],
        operands, 4 * COST, "ups"
    )


def spread(out, k, value, shares):
    share_rows = BS // shares
    for share in range(shares):
        out[share, k] = value[share * share_rows : (share + 1) * share_rows]


def down_grads_call(refs, choices, hidden, rows, width, shares, operands):
    pieces = len(choices)
    all_rows = rows * pieces
    total = operands[2].shape[2]

    def kernel(layer, info, ins, results, scratch):
        cot_refs, hidden_here, turned, sem, hidden_sem = scratch
        out, split = results
        refs, hidden_ref = ins[:-1], ins[-1]
        own = layer(OWN_LAYER)
        load = pltpu.make_async_copy(hidden_ref, hidden_here, hidden_sem)
        load.start()
        moves = fetch_pieces(info, choices, refs, cot_refs, sem)
        for piece in range(pieces):
            moves[piece].wait()
            fill_split(cot_refs.at[piece], split, piece * rows)
        for b in range(width // BS):
            turned[b] = split[b].T
        load.wait()

        def one(k):
            row, col = own_cell(own, 1, k)
            value = dot_plain(turned[col], hidden_here[row])
            spread(out, k, value.T.astype(jnp.bfloat16), shares)

        each(total, one, 12)

    return stage(
        kernel, [], refs + [hidden],
        [
            (True, shape_of((shares, total, BS // shares, BS))),
            (True, shape_of((width // BS, all_rows, BS))),
        ],
        [
            pltpu.VMEM((pieces, rows, width), jnp.bfloat16),
            pltpu.VMEM((FF_BLOCKS, all_rows, BS), jnp.bfloat16),
            pltpu.VMEM((width // BS, BS, all_rows), jnp.bfloat16),
            pltpu.SemaphoreType.DMA((pieces,)),
            pltpu.SemaphoreType.DMA,
        ],
        operands, 2 * COST, "down_grads"
    )


def up_grads_call(split, normed, slopes, width, shares, operands):
    all_rows = split.shape[1]
    total = operands[2].shape[2]
    batch = 8

    def kernel(layer, info, ins, results, scratch):
        split_here, sums, slopes_here, grad_pre, turned, sem = scratch
        split_ref, normed_ref, slopes_ref = ins
        out = results[0]

        def load(i):
            span = pl.ds(i * batch, batch)
            return pltpu.make_async_copy(slopes_ref.at[span], slopes_here.at[span], sem.at[i])

        for i in range(FF_BLOCKS // batch):
            load(i).start()
        clear_spare(split_here)
        split_here[pl.ds(0, width // BS)] = split_ref[...]
        for b in range(width // BS):
            turned[b] = normed_ref[b].T
        own = layer(OWN_LAYER)

        def finish(c, value):
            grad_pre[c] = (value * slopes_here[c]).astype(jnp.bfloat16)

        wide_pass(
            split_here, own.down, own.lists, DOWN_WIDE, sums, finish, True, batch,
            lambda i: load(i).wait()
        )

        def one(k):
            row, col = own_cell(own, 0, k)
            value = dot_plain(turned[row], grad_pre[col])
            spread(out, k, value.astype(jnp.bfloat16), shares)

        each(total, one, 12)

    return stage(
        kernel, [split, normed], [slopes],
        [(True, shape_of((shares, total, BS // shares, BS)))],
        [
            pltpu.VMEM((width // BS + 1, all_rows, BS), jnp.bfloat16),
            pltpu.VMEM((FF_BLOCKS, all_rows, BS), jnp.float32),
            pltpu.VMEM((FF_BLOCKS, all_rows, BS), jnp.float32),
            pltpu.VMEM((FF_BLOCKS, all_rows, BS), jnp.bfloat16),
            pltpu.VMEM((width // BS, BS, all_rows), jnp.bfloat16),
            pltpu.SemaphoreType.DMA((FF_BLOCKS // batch,)),
        ],
        operands, 4 * COST, "up_grads"
    )[0]


def adam_update(grad_sum, master, moment, variance, token_total):
    gradient = grad_sum / token_total
    moment_next = beta_first * moment + (1.0 - beta_first) * gradient
    variance_next = beta_second * variance + (1.0 - beta_second) * gradient * gradient
    corrected = moment_next / (1.0 - beta_first**update_count)
    spread = jnp.sqrt(variance_next / (1.0 - beta_second**update_count))
    step_direction = corrected / (spread + adam_eps)
    return (step_direction, master - learn_rate * (step_direction + decay_rate * master))


def shards(tokens, targets, weights, pattern, master, moment, variance):
    section = lax.axis_index("section")
    sections = lax.axis_size("section")
    shares = lax.axis_size("dp")
    groups = sections // 2
    micro, rows_each, width = tokens.shape[1:]
    rows = micro * rows_each
    half = rows // 2
    high = section >= groups
    high_member = high.astype(jnp.int32)
    group = jnp.minimum(section, sections - 1 - section)
    info = jnp.stack([high_member, 1 - high_member, jnp.zeros_like(high_member), high_member, group])
    tokens = tokens.reshape(2, rows, width)
    targets = targets.reshape(2, rows, width)
    pattern = pattern[0]
    weights = pltpu.with_memory_space_constraint(weights[0], pltpu.VMEM)
    operands = (info, block_lists(pattern, width), weights)
    mirror = lambda i: sections - 1 - i

    def lane(i, h):
        other = mirror(i + 1) if h else i + 1
        return [(i, other), (mirror(i), mirror(other))]

    def inward(x, i, h):
        return lax.ppermute(x, "section", lane(i, h))

    def outward(x, i, h):
        return lax.ppermute(x, "section", [(b, a) for a, b in lane(i, h)])

    def at_half(records, h, start=0):
        value = records[start][h]
        for i in range(start + 1, groups):
            value = jnp.where(group == i, records[i][h], value)
        return value

    def swap(low_records, high_records, h):
        sent = jnp.where(high, at_half(low_records, h, 1), at_half(high_records, h))
        pairs = [(i, mirror(i)) for i in range(groups)] + [(mirror(i), i) for i in range(1, groups)]
        return lax.ppermute(sent, "section", pairs)

    halves = range(2)
    x_low, x_high, cot_low, cot_high = [[None] * groups for _ in range(4)]
    current = [enter_call(tokens, h, half, operands)[0] for h in halves]
    for i in range(groups - 1):
        current = [inward(current[h], i, h) for h in halves]
        x_low[i + 1] = current
        if i + 1 < groups - 1:
            current = [forward_call(current[h], [LOW_LAYER], operands)[0] for h in halves]
    both = [forward_call(current[h], [LOW_LAYER, HIGH_LAYER], operands) for h in halves]
    x_high[groups - 1] = [b[0] for b in both]
    current = [b[1] for b in both]
    for i in reversed(range(groups - 1)):
        current = [outward(current[h], i, h) for h in halves]
        x_high[i] = current
        if i > 0:
            current = [forward_call(current[h], [HIGH_LAYER], operands)[0] for h in halves]
    turned = [turn_call(current[h], targets, h, operands) for h in halves]
    cot_high[0] = [t[0] for t in turned]
    current = [t[1] for t in turned]
    for i in range(groups - 1):
        current = [inward(current[h], i, h) for h in halves]
        cot_high[i + 1] = current
        if i + 1 < groups - 1:
            current = [
                backward_call([x_high[i + 1][h]], current[h], [HIGH_LAYER], operands)[0]
                for h in halves
            ]
    last = groups - 1
    both = [
        backward_call([x_high[last][h], x_low[last][h]], current[h], [HIGH_LAYER, LOW_LAYER], operands)
        for h in halves
    ]
    cot_low[last] = [b[0] for b in both]
    current = [b[1] for b in both]
    for i in reversed(range(1, last)):
        current = [outward(current[h], i, h) for h in halves]
        cot_low[i] = current
        current = [backward_call([x_low[i][h]], current[h], [LOW_LAYER], operands)[0] for h in halves]
    from_low = [lax.ppermute(current[h], "section", [(1, 0)]) for h in halves]
    from_high = [lax.ppermute(current[h], "section", [(mirror(1), 0)]) for h in halves]
    x_other = [swap(x_low, x_high, h) for h in halves]
    cot_other = [swap(cot_low, cot_high, h) for h in halves]

    def choose(low_records, high_records, others, first_own, first_other):
        refs, choices = [], []

        def add(array):
            refs.append(array)
            return len(refs) - 1

        for h in halves:
            array, index = first_own[h]
            options = [("first", None, add(array), index)]
            for i in range(groups):
                if i > 0:
                    options.append(("own", (0, i), add(low_records[i][h]), None))
                options.append(("own", (1, i), add(high_records[i][h]), None))
            choices.append(options)
        for h in halves:
            array, index = first_other[h]
            choices.append([("first", None, add(array), index), ("rest", None, add(others[h]), None)])
        return refs, choices

    def token_piece(member, h):
        return (tokens, (member, pl.ds(h * half, half)))

    refs, choices = choose(
        x_low, x_high, x_other, [token_piece(0, h) for h in halves], [token_piece(1, h) for h in halves]
    )
    hidden, slopes, normed = ups_call(refs, choices, current[1], half, width, operands)
    refs, choices = choose(
        cot_low, cot_high, cot_other,
        [(from_low[0], None), (from_high[1], None)], [(from_high[0], None), (from_low[1], None)]
    )
    downs, split = down_grads_call(refs, choices, hidden, half, width, shares, operands)
    ups = up_grads_call(split, normed, slopes, width, shares, operands)

    def reduce(grads):
        return lax.psum_scatter(grads, "dp", scatter_dimension=0, tiled=True)[0].astype(jnp.float32)

    down_share, up_share = reduce(downs), reduce(ups)
    token_total = 2 * rows * shares
    step_direction, master_next = adam_update(
        jnp.stack([up_share, down_share]), master[0], moment[0], variance[0], token_total
    )
    return (step_direction[None], master_next[None])


def solution(mesh):
    rows_split = P(None, None, "dp", None)
    by_section = P("section", None, None, "dp", None)
    return jax.shard_map(
        shards,
        mesh=mesh,
        in_specs=(
            rows_split,
            rows_split,
            P("section", None, None, None, None, None),
            P("section", None, None, None, None),
            by_section,
            by_section,
            by_section,
        ),
        out_specs=(by_section, by_section),
        check_vma=False,
    )
```

```python
import functools

import jax
import jax.numpy as jnp
from jax import lax
from jax.experimental import pallas as pl
from jax.experimental.pallas import tpu as pltpu
from jax.sharding import PartitionSpec as P

BS = 128
FF_BLOCKS = 8192 // BS
norm_eps = 1e-06
gelu_coef = 0.7978845608028654
gelu_cubic = gelu_coef * 0.044715
beta_first = 0.9
beta_second = 0.95
adam_eps = 1e-08
learn_rate = 0.001
decay_rate = 0.1
update_count = 10
ROW_TILE = 16
EXTRA_BATCH = 8
CHAIN_VMEM = 24 * 1024 * 1024
ENTER_VMEM = 32 * 1024 * 1024
OWN_VMEM = 40 * 1024 * 1024
COST = 4_000_000_000
LOW_LAYER, HIGH_LAYER, OWN_LAYER, HIGH, GROUP = range(5)
UP_WIDE, DOWN_WIDE, DOWN_NARROW, UP_NARROW = range(4)
FIELDS = 9
FIRST, FIRST_TAKE, SECOND, SECOND_TAKE, PUT, EXTRA, EXTRA_TAKE, EXTRA_PUT, COUNT = range(FIELDS)


def block_lists(pattern, width):
    total = pattern.shape[2]
    up_row, up_col = pattern[:, 0, :, 0], pattern[:, 0, :, 1]
    down_row, down_col = pattern[:, 1, :, 0], pattern[:, 1, :, 1]
    key = jnp.stack([up_col, down_row, down_col, up_row], 1)
    take = jnp.stack([up_row, down_col, down_row, up_col], 1)
    order = jnp.arange(total, dtype=jnp.int32)
    before = order[None, :] < order[:, None]

    def count(mask):
        return jnp.sum(mask.astype(jnp.int32), axis=-1)

    same = key[..., None, :] == key[..., :, None]
    rank = count(same & before)
    even = rank % 2 == 0
    wide = (jnp.arange(4) < 2)[None, :, None]
    extra = rank >= 2
    extra_place = count(extra[..., None, :] & before)
    pair = count((key[..., None, :] < key[..., :, None]) & even[..., None, :]) + rank // 2
    place_first = jnp.where(wide, jnp.where(rank == 0, key, -1), jnp.where(even, pair, -1))
    place_second = jnp.where(wide, jnp.where(rank == 1, key, -1), jnp.where(even, -1, pair))
    place_extra = jnp.where(wide & extra, extra_place, -1)
    number = jnp.broadcast_to(order, key.shape)
    places = jnp.stack(
        [place_first] * 2 + [place_second] * 2 + [place_first] + [place_extra] * 3, 2
    )
    absent = jnp.where(wide, width // BS, FF_BLOCKS)
    lowered = take - absent
    values = jnp.stack([number, lowered, number, lowered, key, number, lowered, key], 2)
    hit = places[..., None, :] == order[:, None]
    fields = jnp.sum(jnp.where(hit, values[..., None, :], 0), axis=-1)
    slot = jnp.arange(8)
    taken = (slot == FIRST_TAKE) | (slot == SECOND_TAKE) | (slot == EXTRA_TAKE)
    fields = fields + jnp.where(taken[:, None], absent[..., None], 0)
    counts = jnp.where(wide[..., 0], count(extra), count(even))
    counts = jnp.broadcast_to(counts[..., None, None], key.shape[:2] + (1, total))
    lists = jnp.concatenate([fields, counts], axis=2).astype(jnp.int32)
    return jnp.concatenate([lists.reshape(-1), pattern[0].reshape(-1)])


class Lists:
    def __init__(self, ref, copy, total):
        self.ref, self.total = ref, total
        self.base = copy * (4 * FIELDS * total)
        self.cells = 2 * 4 * FIELDS * total

    def __call__(self, kind, field, index):
        return self.ref[self.base + ((kind * FIELDS + field) * self.total) + index]


def hidden_of(preact):
    inner = preact * (gelu_coef + gelu_cubic * (preact * preact))
    half = 0.5 * preact
    return half + half * jnp.tanh(inner)


def slope_of(preact):
    cubic = gelu_cubic * (preact * preact)
    tangent = jnp.tanh(preact * (gelu_coef + cubic))
    bend = preact * (gelu_coef + 3.0 * cubic)
    return (0.5 + 0.5 * tangent) * (1.0 + bend * (1.0 - tangent))


def both_of(preact):
    cubic = gelu_cubic * (preact * preact)
    tangent = jnp.tanh(preact * (gelu_coef + cubic))
    bend = preact * (gelu_coef + 3.0 * cubic)
    half = 0.5 + 0.5 * tangent
    return (preact * half, half * (1.0 + bend * (1.0 - tangent)))


def dot_plain(left, right):
    return jnp.dot(left, right, preferred_element_type=jnp.float32)


def dot_right_t(left, right):
    return lax.dot_general(left, right, (((1,), (1,)), ((), ())), preferred_element_type=jnp.float32)


def each(count, body, unroll=1):
    def one(i, carry):
        body(i)
        return carry

    lax.fori_loop(0, count, one, 0, unroll=unroll)


def fill_normed(x_ref, normed, base):
    rows, width = x_ref.shape

    def tile(i):
        at = pl.multiple_of(i * ROW_TILE, ROW_TILE)
        wide = x_ref[pl.ds(at, ROW_TILE), :].astype(jnp.float32)
        factor = lax.rsqrt(jnp.mean(wide * wide, axis=-1, keepdims=True) + norm_eps)
        value = (wide * factor).astype(jnp.bfloat16)
        for b in range(width // BS):
            normed[b, pl.ds(base + at, ROW_TILE), :] = value[:, b * BS : (b + 1) * BS]

    each(rows // ROW_TILE, tile, 7)


def fill_split(x_ref, split, base):
    rows, width = x_ref.shape
    for b in range(width // BS):
        split[b, pl.ds(base, rows), :] = x_ref[:, b * BS : (b + 1) * BS]


def pair_product(source, blocks, lists, kind, p, transposed):
    left = jnp.concatenate(
        [source[lists(kind, FIRST_TAKE, p)], source[lists(kind, SECOND_TAKE, p)]], axis=1
    )
    one, two = blocks[lists(kind, FIRST, p)], blocks[lists(kind, SECOND, p)]
    if transposed:
        return dot_right_t(left, jnp.concatenate([one, two], axis=1))
    return dot_plain(left, jnp.concatenate([one, two], axis=0))


def wide_pass(source, blocks, lists, kind, sums, finish, transposed, batch=16, ahead=None):
    def main(i):
        if ahead is not None:
            ahead(i)
        for j in range(batch):
            c = i * batch + j
            value = pair_product(source, blocks, lists, kind, c, transposed)
            sums[c] = value
            finish(c, value)

    each(sums.shape[0] // batch, main)
    dot = dot_right_t if transposed else dot_plain

    def more(e):
        c = lists(kind, EXTRA_PUT, e)
        left = source[lists(kind, EXTRA_TAKE, e)]
        value = sums[c] + dot(left, blocks[lists(kind, EXTRA, e)])
        sums[c] = value
        finish(c, value)

    def batch(i):
        for j in range(EXTRA_BATCH):
            more(i * EXTRA_BATCH + j)

    each((lists(kind, COUNT, 0) + EXTRA_BATCH - 1) // EXTRA_BATCH, batch)


def narrow_pass(source, blocks, lists, kind, sums, transposed):
    sums[...] = jnp.zeros(sums.shape, sums.dtype)

    def one(p):
        sums[lists(kind, PUT, p)] += pair_product(source, blocks, lists, kind, p, transposed)

    each((lists.total + sums.shape[0]) // 2, one, 14)


def forward_rows(x_ref, out_ref, layer, scratch, slopes=None, before=lambda part: None):
    normed, sums, hidden, narrow = scratch
    rows, width = x_ref.shape
    fill_normed(x_ref, normed, 0)

    def finish(c, value):
        if slopes is None:
            hidden[c] = hidden_of(value).astype(jnp.bfloat16)
        else:
            value, slope = both_of(value)
            hidden[c] = value.astype(jnp.bfloat16)
            slopes[c] = slope

    before(0)
    wide_pass(normed, layer.up, layer.lists, UP_WIDE, sums, finish, False)
    before(1)
    narrow_pass(hidden, layer.down, layer.lists, DOWN_NARROW, narrow, False)
    for b in range(width // BS):
        cols = slice(b * BS, (b + 1) * BS)
        out_ref[:, cols] = (x_ref[:, cols].astype(jnp.float32) + narrow[b]).astype(jnp.bfloat16)


def slope_rows(x_ref, layer, scratch, slopes):
    normed, sums, hidden, narrow = scratch
    fill_normed(x_ref, normed, 0)

    def finish(c, value):
        slopes[c] = slope_of(value)

    wide_pass(normed, layer.up, layer.lists, UP_WIDE, sums, finish, False)


def backward_rows(x_ref, cot_ref, out_ref, layer, scratch, slopes):
    normed, sums, hidden, narrow = scratch
    rows, width = x_ref.shape
    fill_split(cot_ref, normed, 0)

    def finish(c, value):
        hidden[c] = (value * slopes[c]).astype(jnp.bfloat16)

    wide_pass(normed, layer.down, layer.lists, DOWN_WIDE, sums, finish, True)
    narrow_pass(hidden, layer.up, layer.lists, UP_NARROW, narrow, True)

    def tile(i):
        at = pl.multiple_of(i * ROW_TILE, ROW_TILE)
        wide = x_ref[pl.ds(at, ROW_TILE), :].astype(jnp.float32)
        factor = lax.rsqrt(jnp.mean(wide * wide, axis=-1, keepdims=True) + norm_eps)
        grad = jnp.concatenate(
            [narrow[b, pl.ds(at, ROW_TILE), :] for b in range(width // BS)], axis=-1
        )
        coupling = jnp.mean(wide * grad, axis=-1, keepdims=True)
        upstream = cot_ref[pl.ds(at, ROW_TILE), :].astype(jnp.float32)
        value = upstream + factor * grad - wide * (factor * factor * factor * coupling)
        out_ref[pl.ds(at, ROW_TILE), :] = value.astype(jnp.bfloat16)

    each(rows // ROW_TILE, tile)


def own_cell(layer, part, k):
    lists = layer.lists
    at = lists.cells + 2 * (part * lists.total + k)
    return lists.ref[at], lists.ref[at + 1]


class Layer:
    def __init__(self, info, lists_ref, weights_ref, which):
        copy = info[which]
        self.lists = Lists(lists_ref, copy, lists_ref.shape[0] // (2 * 4 * FIELDS + 4))
        if weights_ref is not None:
            self.up = weights_ref.at[copy, 0]
            self.down = weights_ref.at[copy, 1]


def stage(kernel, local_in, remote_in, outs, scratch, operands, cost, name, vmem=CHAIN_VMEM):
    info, lists, weights = operands
    held = [] if weights is None else [pltpu.with_memory_space_constraint(weights, pltpu.VMEM)]
    any_spec = pl.BlockSpec(memory_space=pltpu.HBM)
    smem_spec = pl.BlockSpec(memory_space=pltpu.SMEM)
    vmem_spec = pl.BlockSpec(memory_space=pltpu.VMEM)
    in_total = len(local_in) + len(remote_in)
    local_in = [pltpu.with_memory_space_constraint(array, pltpu.VMEM) for array in local_in]

    def body(info_ref, lists_ref, *rest):
        weights_ref, rest = (None, rest) if weights is None else (rest[0], rest[1:])
        ins, results, own = rest[:in_total], rest[in_total : in_total + len(outs)], rest[in_total + len(outs) :]

        def layer(which, weights_ref=weights_ref):
            return Layer(info_ref, lists_ref, weights_ref, which)

        kernel(layer, info_ref, ins, results, own)

    return pl.pallas_call(
        body,
        in_specs=[smem_spec, smem_spec]
        + [vmem_spec] * (len(held) + len(local_in))
        + [any_spec] * len(remote_in),
        out_specs=[vmem_spec if space else any_spec for space, _ in outs],
        out_shape=[shape if space else pltpu.HBM(shape.shape, shape.dtype) for space, shape in outs],
        scratch_shapes=scratch,
        name=name,
        cost_estimate=pl.CostEstimate(flops=cost, transcendentals=0, bytes_accessed=0),
        compiler_params=pltpu.CompilerParams(vmem_limit_bytes=vmem),
    )(info, lists, *held, *local_in, *remote_in)


def layer_scratch(rows, width):
    return [
        pltpu.VMEM((width // BS + 1, rows, BS), jnp.bfloat16),
        pltpu.VMEM((FF_BLOCKS, rows, BS), jnp.float32),
        pltpu.VMEM((FF_BLOCKS + 1, rows, BS), jnp.bfloat16),
        pltpu.VMEM((width // BS, rows, BS), jnp.float32),
    ]


def slope_scratch(rows):
    return [pltpu.VMEM((FF_BLOCKS, rows, BS), jnp.float32)]


def shape_of(shape, dtype=jnp.bfloat16):
    return jax.ShapeDtypeStruct(shape, dtype)


def clear_spare(*refs):
    for ref in refs:
        ref[ref.shape[0] - 1] = jnp.zeros(ref.shape[1:], ref.dtype)


def forward_call(x, whichs, operands):
    rows, width = x.shape

    def kernel(layer, info, ins, results, scratch):
        clear_spare(scratch[0], scratch[2])
        source = ins[0]
        for which, out in zip(whichs, results):
            forward_rows(source, out, layer(which), scratch)
            source = out

    return stage(
        kernel, [x], [], [(True, shape_of(x.shape))] * len(whichs), layer_scratch(rows, width),
        operands, COST * len(whichs), "forward"
    )


def enter_call(tokens, h, rows, unloaded, operands):
    width = tokens.shape[-1]

    def kernel(layer, info, ins, results, scratch):
        *layer_refs, x_ref, local, sem, weight_sem = scratch
        load = pltpu.make_async_copy(ins[0].at[info[HIGH], pl.ds(h * rows, rows)], x_ref, sem)
        load.start()
        low = info[LOW_LAYER]
        moves = [
            pltpu.make_async_copy(ins[1].at[low, part], local.at[low, part], weight_sem.at[part])
            for part in range(2)
        ]

        def before(part):
            moves[part].wait()
            if part == 0:
                moves[1].start()

        moves[0].start()
        clear_spare(layer_refs[0], layer_refs[2])
        load.wait()
        forward_rows(x_ref, results[0], layer(LOW_LAYER, local), layer_refs, before=before)
    outs = [(True, shape_of((rows, width)))]
    scratch = layer_scratch(rows, width) + [
        pltpu.VMEM((rows, width), jnp.bfloat16),
        pltpu.VMEM(unloaded.shape, unloaded.dtype),
        pltpu.SemaphoreType.DMA,
        pltpu.SemaphoreType.DMA((2,)),
    ]
    return stage(kernel, [], [tokens, unloaded], outs, scratch, operands, COST, "enter", ENTER_VMEM)


def turn_call(x, targets, h, operands):
    rows, width = x.shape

    def kernel(layer, info, ins, results, scratch):
        *layer_refs, slopes, aim, sem = scratch
        x_ref, target_ref = ins
        residue, out = results
        load = pltpu.make_async_copy(target_ref.at[info[HIGH], pl.ds(h * rows, rows)], aim, sem)
        load.start()
        clear_spare(layer_refs[0], layer_refs[2])
        own = layer(HIGH_LAYER)
        forward_rows(x_ref, residue, own, layer_refs, slopes)
        load.wait()
        for b in range(width // BS):
            cols = slice(b * BS, (b + 1) * BS)
            difference = residue[:, cols].astype(jnp.float32) - aim[:, cols].astype(jnp.float32)
            residue[:, cols] = difference.astype(jnp.bfloat16)
        backward_rows(x_ref, residue, out, own, layer_refs, slopes)

    return stage(
        kernel, [x], [targets], [(True, shape_of(x.shape))] * 2,
        layer_scratch(rows, width) + slope_scratch(rows)
        + [pltpu.VMEM((rows, width), jnp.bfloat16), pltpu.SemaphoreType.DMA],
        operands, 3 * COST, "turn"
    )


def backward_call(xs, cot, whichs, operands):
    rows, width = cot.shape

    def kernel(layer, info, ins, results, scratch):
        *layer_refs, slopes = scratch
        clear_spare(layer_refs[0], layer_refs[2])
        upstream = ins[-1]
        for which, x_ref, out in zip(whichs, ins, results):
            own = layer(which)
            slope_rows(x_ref, own, layer_refs, slopes)
            backward_rows(x_ref, upstream, out, own, layer_refs, slopes)
            upstream = out

    return stage(
        kernel, list(xs) + [cot], [], [(True, shape_of(cot.shape))] * len(whichs),
        layer_scratch(rows, width) + slope_scratch(rows), operands, 2 * COST * len(whichs),
        "backward"
    )


def fetch_pieces(info, choices, refs, local, sem):
    first = (info[HIGH] == 0) & (info[GROUP] == 0)
    moves = []
    for piece, options in enumerate(choices):
        for kind, wanted, number, index in options:
            source = refs[number] if index is None else refs[number].at[index]
            move = pltpu.make_async_copy(source, local.at[piece], sem.at[piece])
            if kind == "first":
                condition = first
            elif kind == "own":
                condition = (info[HIGH] == wanted[0]) & (info[GROUP] == wanted[1]) & ~first
            else:
                condition = ~first

            @pl.when(condition)
            def go(move=move):
                move.start()

        moves.append(move)
    return moves


def ups_call(refs, choices, after, rows, width, unloaded, operands):
    pieces = len(choices)
    all_rows = rows * pieces
    part_rows = all_rows // 2

    def kernel(layer, info, ins, results, scratch):
        x_refs, normed, sums, hidden, slopes, blocks_here, sem, out_sem, block_sem = scratch
        hidden_out, slopes_out, normed_out = results
        load = pltpu.make_async_copy(ins[-1].at[0, 0], blocks_here, block_sem)
        load.start()
        moves = fetch_pieces(info, choices, ins, x_refs, sem)
        own = layer(OWN_LAYER)
        outs = []
        for part in range(2):
            here = normed.at[part]
            clear_spare(here)
            for i in range(pieces // 2):
                piece = part * (pieces // 2) + i
                moves[piece].wait()
                fill_normed(x_refs.at[piece], here, i * rows)

            if part == 0:
                load.wait()

            def finish(c, value):
                value, slope = both_of(value)
                hidden[part, c] = value.astype(jnp.bfloat16)
                slopes[part, c] = slope

            wide_pass(here, blocks_here, own.lists, UP_WIDE, sums, finish, False, 8)
            span = pl.ds(part * part_rows, part_rows)
            blocks = pl.ds(0, width // BS)
            outs += [
                pltpu.make_async_copy(hidden.at[part], hidden_out.at[:, span], out_sem.at[part, 0]),
                pltpu.make_async_copy(slopes.at[part], slopes_out.at[:, span], out_sem.at[part, 1]),
                pltpu.make_async_copy(here.at[blocks], normed_out.at[:, span], out_sem.at[part, 2]),
            ]
            for move in outs[-3:]:
                move.start()
        for move in outs:
            move.wait()

    return stage(
        kernel, [], refs + [after, unloaded],
        [
            (False, shape_of((FF_BLOCKS, all_rows, BS))),
            (False, shape_of((FF_BLOCKS, all_rows, BS), jnp.float32)),
            (False, shape_of((width // BS, all_rows, BS))),
        ],
        [
            pltpu.VMEM((pieces, rows, width), jnp.bfloat16),
            pltpu.VMEM((2, width // BS + 1, part_rows, BS), jnp.bfloat16),
            pltpu.VMEM((FF_BLOCKS, part_rows, BS), jnp.float32),
            pltpu.VMEM((2, FF_BLOCKS, part_rows, BS), jnp.bfloat16),
            pltpu.VMEM((2, FF_BLOCKS, part_rows, BS), jnp.float32),
            pltpu.VMEM(unloaded.shape[2:], unloaded.dtype),
            pltpu.SemaphoreType.DMA((pieces,)),
            pltpu.SemaphoreType.DMA((2, 3)),
            pltpu.SemaphoreType.DMA,
        ],
        operands, 4 * COST, "ups", OWN_VMEM
    )


def spread(out, k, value, shares):
    share_rows = BS // shares
    for share in range(shares):
        out[share, k] = value[share * share_rows : (share + 1) * share_rows]


def down_grads_call(refs, choices, hidden, rows, width, shares, total, operands):
    pieces = len(choices)
    all_rows = rows * pieces

    def kernel(layer, info, ins, results, scratch):
        cot_refs, hidden_here, split, turned, sem, hidden_sem, split_sem = scratch
        out, split_out = results
        refs, hidden_ref = ins[:-1], ins[-1]
        own = layer(OWN_LAYER)
        load = pltpu.make_async_copy(hidden_ref, hidden_here, hidden_sem)
        load.start()
        moves = fetch_pieces(info, choices, refs, cot_refs, sem)
        for piece in range(pieces):
            moves[piece].wait()
            fill_split(cot_refs.at[piece], split, piece * rows)
        keep = pltpu.make_async_copy(split, split_out, split_sem)
        keep.start()
        for b in range(width // BS):
            turned[b] = split[b].T
        load.wait()

        def one(k):
            row, col = own_cell(own, 1, k)
            value = dot_plain(turned[col], hidden_here[row])
            spread(out, k, value.T.astype(jnp.bfloat16), shares)

        each(total, one, 12)
        keep.wait()

    return stage(
        kernel, [], refs + [hidden],
        [
            (True, shape_of((shares, total, BS // shares, BS))),
            (False, shape_of((width // BS, all_rows, BS))),
        ],
        [
            pltpu.VMEM((pieces, rows, width), jnp.bfloat16),
            pltpu.VMEM((FF_BLOCKS, all_rows, BS), jnp.bfloat16),
            pltpu.VMEM((width // BS, all_rows, BS), jnp.bfloat16),
            pltpu.VMEM((width // BS, BS, all_rows), jnp.bfloat16),
            pltpu.SemaphoreType.DMA((pieces,)),
            pltpu.SemaphoreType.DMA,
            pltpu.SemaphoreType.DMA,
        ],
        operands, 2 * COST, "down_grads", OWN_VMEM
    )


def up_grads_call(split, normed, slopes, width, shares, unloaded, operands):
    all_rows = split.shape[1]
    part_rows = all_rows // 2
    total = unloaded.shape[2]
    batch = 8
    blocks = width // BS

    def kernel(layer, info, ins, results, scratch):
        split_here, normed_here, sums, slopes_here, grad_pre, turned, blocks_here, sem, slope_sem = scratch
        split_ref, normed_ref, slopes_ref, unloaded_ref = ins
        out = results[0]

        def load(part, i):
            span = pl.ds(i * batch, batch)
            rows = pl.ds(part * part_rows, part_rows)
            return pltpu.make_async_copy(
                slopes_ref.at[span, rows], slopes_here.at[part, span], slope_sem.at[part, i]
            )

        moves = [
            pltpu.make_async_copy(
                split_ref.at[:, pl.ds(part * part_rows, part_rows)],
                split_here.at[part, pl.ds(0, blocks)],
                sem.at[part],
            )
            for part in range(2)
        ]
        moves.append(pltpu.make_async_copy(normed_ref, normed_here, sem.at[2]))
        moves.append(pltpu.make_async_copy(unloaded_ref.at[0, 1], blocks_here, sem.at[3]))
        moves[0].start()
        moves[2].start()
        moves[3].start()
        for part in range(2):
            for i in range(FF_BLOCKS // batch):
                load(part, i).start()
            if part == 0:
                moves[1].start()
        own = layer(OWN_LAYER)
        moves[2].wait()
        for b in range(blocks):
            turned[b] = normed_here[b].T
        for part in range(2):
            clear_spare(split_here.at[part])
            moves[part].wait()
            if part == 0:
                moves[3].wait()
            span = pl.ds(part * part_rows, part_rows)

            def finish(c, value):
                grad_pre[c, span, :] = (value * slopes_here[part, c]).astype(jnp.bfloat16)

            wide_pass(
                split_here.at[part], blocks_here, own.lists, DOWN_WIDE, sums, finish, True, batch,
                lambda i: load(part, i).wait()
            )

        def one(k):
            row, col = own_cell(own, 0, k)
            value = dot_plain(turned[row], grad_pre[col])
            spread(out, k, value.astype(jnp.bfloat16), shares)

        each(total, one, 12)

    return stage(
        kernel, [], [split, normed, slopes, unloaded],
        [(True, shape_of((shares, total, BS // shares, BS)))],
        [
            pltpu.VMEM((2, blocks + 1, part_rows, BS), jnp.bfloat16),
            pltpu.VMEM((blocks, all_rows, BS), jnp.bfloat16),
            pltpu.VMEM((FF_BLOCKS, part_rows, BS), jnp.float32),
            pltpu.VMEM((2, FF_BLOCKS, part_rows, BS), jnp.float32),
            pltpu.VMEM((FF_BLOCKS, all_rows, BS), jnp.bfloat16),
            pltpu.VMEM((blocks, BS, all_rows), jnp.bfloat16),
            pltpu.VMEM(unloaded.shape[2:], unloaded.dtype),
            pltpu.SemaphoreType.DMA((4,)),
            pltpu.SemaphoreType.DMA((2, FF_BLOCKS // batch)),
        ],
        operands, 4 * COST, "up_grads", OWN_VMEM
    )[0]


def adam_update(grad_sum, master, moment, variance, token_total):
    gradient = grad_sum / token_total
    moment_next = beta_first * moment + (1.0 - beta_first) * gradient
    variance_next = beta_second * variance + (1.0 - beta_second) * gradient * gradient
    corrected = moment_next / (1.0 - beta_first**update_count)
    spread = jnp.sqrt(variance_next / (1.0 - beta_second**update_count))
    step_direction = corrected / (spread + adam_eps)
    return (step_direction, master - learn_rate * (step_direction + decay_rate * master))


def shards(tokens, targets, weights, pattern, master, moment, variance):
    section = lax.axis_index("section")
    sections = lax.axis_size("section")
    shares = lax.axis_size("dp")
    groups = sections // 2
    micro, rows_each, width = tokens.shape[1:]
    rows = micro * rows_each
    half = rows // 2
    high = section >= groups
    high_member = high.astype(jnp.int32)
    group = jnp.minimum(section, sections - 1 - section)
    info = jnp.stack([high_member, 1 - high_member, jnp.zeros_like(high_member), high_member, group])
    far = lambda array: pltpu.with_memory_space_constraint(array, pltpu.HBM)
    tokens = far(tokens.reshape(2, rows, width))
    targets = far(targets.reshape(2, rows, width))
    pattern = pattern[0]
    lists = block_lists(pattern, width)
    mirror = lambda i: sections - 1 - i

    def lane(i, h):
        other = mirror(i + 1) if h else i + 1
        return [(i, other), (mirror(i), mirror(other))]

    def inward(x, i, h):
        return lax.ppermute(x, "section", lane(i, h))

    def outward(x, i, h):
        return lax.ppermute(x, "section", [(b, a) for a, b in lane(i, h)])

    def at_half(records, h, start=0):
        value = records[start][h]
        for i in range(start + 1, groups):
            value = jnp.where(group == i, records[i][h], value)
        return value

    def swap(low_records, high_records, h):
        sent = jnp.where(high, at_half(low_records, h, 1), at_half(high_records, h))
        pairs = [(i, mirror(i)) for i in range(groups)] + [(mirror(i), i) for i in range(1, groups)]
        return lax.ppermute(sent, "section", pairs)

    halves = range(2)
    x_low, x_high, cot_low, cot_high = [[None] * groups for _ in range(4)]
    unloaded = far(weights[0])
    current = [enter_call(tokens, h, half, unloaded, (info, lists, None))[0] for h in halves]
    operands = (info, lists, weights[0])
    for i in range(groups - 1):
        current = [inward(current[h], i, h) for h in halves]
        x_low[i + 1] = current
        if i + 1 < groups - 1:
            current = [forward_call(current[h], [LOW_LAYER], operands)[0] for h in halves]
    both = [forward_call(current[h], [LOW_LAYER, HIGH_LAYER], operands) for h in halves]
    x_high[groups - 1] = [b[0] for b in both]
    current = [b[1] for b in both]
    for i in reversed(range(groups - 1)):
        current = [outward(current[h], i, h) for h in halves]
        x_high[i] = current
        if i > 0:
            current = [forward_call(current[h], [HIGH_LAYER], operands)[0] for h in halves]
    turned = [turn_call(current[h], targets, h, operands) for h in halves]
    cot_high[0] = [t[0] for t in turned]
    current = [t[1] for t in turned]
    for i in range(groups - 1):
        current = [inward(current[h], i, h) for h in halves]
        cot_high[i + 1] = current
        if i + 1 < groups - 1:
            current = [
                backward_call([x_high[i + 1][h]], current[h], [HIGH_LAYER], operands)[0]
                for h in halves
            ]
    last = groups - 1
    both = [
        backward_call([x_high[last][h], x_low[last][h]], current[h], [HIGH_LAYER, LOW_LAYER], operands)
        for h in halves
    ]
    cot_low[last] = [b[0] for b in both]
    current = [b[1] for b in both]
    for i in reversed(range(1, last)):
        current = [outward(current[h], i, h) for h in halves]
        cot_low[i] = current
        current = [backward_call([x_low[i][h]], current[h], [LOW_LAYER], operands)[0] for h in halves]
    from_low = [lax.ppermute(current[h], "section", [(1, 0)]) for h in halves]
    from_high = [lax.ppermute(current[h], "section", [(mirror(1), 0)]) for h in halves]
    x_other = [swap(x_low, x_high, h) for h in halves]
    cot_other = [swap(cot_low, cot_high, h) for h in halves]

    def choose(low_records, high_records, others, first_own, first_other):
        refs, choices = [], []

        def add(array):
            refs.append(array)
            return len(refs) - 1

        for h in halves:
            array, index = first_own[h]
            options = [("first", None, add(array), index)]
            for i in range(groups):
                if i > 0:
                    options.append(("own", (0, i), add(low_records[i][h]), None))
                options.append(("own", (1, i), add(high_records[i][h]), None))
            choices.append(options)
        for h in halves:
            array, index = first_other[h]
            choices.append([("first", None, add(array), index), ("rest", None, add(others[h]), None)])
        return refs, choices

    def token_piece(member, h):
        return (tokens, (member, pl.ds(h * half, half)))

    refs, choices = choose(
        x_low, x_high, x_other, [token_piece(0, h) for h in halves], [token_piece(1, h) for h in halves]
    )
    hidden, slopes, normed = ups_call(refs, choices, current[1], half, width, unloaded, (info, lists, None))
    refs, choices = choose(
        cot_low, cot_high, cot_other,
        [(from_low[0], None), (from_high[1], None)], [(from_high[0], None), (from_low[1], None)]
    )
    downs, split = down_grads_call(
        refs, choices, far(hidden), half, width, shares, unloaded.shape[2], (info, lists, None)
    )

    def reduce(grads):
        return lax.psum_scatter(grads, "dp", scatter_dimension=0, tiled=True)[0].astype(jnp.float32)

    down_share = reduce(downs)
    up_share = reduce(up_grads_call(far(split), far(normed), far(slopes), width, shares, unloaded, (info, lists, None)))
    token_total = 2 * rows * shares
    step_direction, master_next = adam_update(
        jnp.stack([down_share, up_share])[::-1], master[0], moment[0], variance[0], token_total
    )
    return (step_direction[None], master_next[None])


def solution(mesh):
    rows_split = P(None, None, "dp", None)
    by_section = P("section", None, None, "dp", None)
    return jax.shard_map(
        shards,
        mesh=mesh,
        in_specs=(
            rows_split,
            rows_split,
            P("section", None, None, None, None, None),
            P("section", None, None, None, None),
            by_section,
            by_section,
            by_section,
        ),
        out_specs=(by_section, by_section),
        check_vma=False,
    )
```

```python
import functools

import jax
import jax.numpy as jnp
from jax import lax
from jax.experimental import pallas as pl
from jax.experimental.pallas import tpu as pltpu
from jax.sharding import PartitionSpec as P

BS = 128
FF_BLOCKS = 8192 // BS
norm_eps = 1e-06
gelu_coef = 0.7978845608028654
gelu_cubic = gelu_coef * 0.044715
beta_first = 0.9
beta_second = 0.95
adam_eps = 1e-08
learn_rate = 0.001
decay_rate = 0.1
update_count = 10
ROW_TILE = 16
EXTRA_BATCH = 4
CHAIN_VMEM = 24 * 1024 * 1024
ENTER_VMEM = 32 * 1024 * 1024
OWN_VMEM = 40 * 1024 * 1024
COST = 4_000_000_000
LOCAL = None
LOW_LAYER, HIGH_LAYER, OWN_LAYER, HIGH, GROUP = range(5)
UP_WIDE, DOWN_WIDE, DOWN_NARROW, UP_NARROW = range(4)
FIELDS = 9
FIRST, FIRST_TAKE, SECOND, SECOND_TAKE, PUT, EXTRA, EXTRA_TAKE, EXTRA_PUT, COUNT = range(FIELDS)


def block_lists(pattern, width):
    total = pattern.shape[2]
    up_row, up_col = pattern[:, 0, :, 0], pattern[:, 0, :, 1]
    down_row, down_col = pattern[:, 1, :, 0], pattern[:, 1, :, 1]
    key = jnp.stack([up_col, down_row, down_col, up_row], 1)
    take = jnp.stack([up_row, down_col, down_row, up_col], 1)
    order = jnp.arange(total, dtype=jnp.int32)
    before = order[None, :] < order[:, None]

    def count(mask):
        return jnp.sum(mask.astype(jnp.int32), axis=-1)

    same = key[..., None, :] == key[..., :, None]
    rank = count(same & before)
    even = rank % 2 == 0
    wide = (jnp.arange(4) < 2)[None, :, None]
    extra = rank >= 2
    extra_place = count(extra[..., None, :] & before)
    pair = count((key[..., None, :] < key[..., :, None]) & even[..., None, :]) + rank // 2
    place_first = jnp.where(wide, jnp.where(rank == 0, key, -1), jnp.where(even, pair, -1))
    place_second = jnp.where(wide, jnp.where(rank == 1, key, -1), jnp.where(even, -1, pair))
    place_extra = jnp.where(wide & extra, extra_place, -1)
    number = jnp.broadcast_to(order, key.shape)
    places = jnp.stack(
        [place_first] * 2 + [place_second] * 2 + [place_first] + [place_extra] * 3, 2
    )
    absent = jnp.where(wide, width // BS, FF_BLOCKS)
    lowered = take - absent
    values = jnp.stack([number, lowered, number, lowered, key, number, lowered, key], 2)
    hit = places[..., None, :] == order[:, None]
    fields = jnp.sum(jnp.where(hit, values[..., None, :], 0), axis=-1)
    slot = jnp.arange(8)
    taken = (slot == FIRST_TAKE) | (slot == SECOND_TAKE) | (slot == EXTRA_TAKE)
    fields = fields + jnp.where(taken[:, None], absent[..., None], 0)
    counts = jnp.where(wide[..., 0], count(extra), count(even))
    counts = jnp.broadcast_to(counts[..., None, None], key.shape[:2] + (1, total))
    lists = jnp.concatenate([fields, counts], axis=2).astype(jnp.int32)
    return jnp.concatenate([lists.reshape(-1), pattern[0].reshape(-1)])


class Lists:
    def __init__(self, ref, copy, total):
        self.ref, self.total = ref, total
        self.base = copy * (4 * FIELDS * total)
        self.cells = 2 * 4 * FIELDS * total

    def __call__(self, kind, field, index):
        return self.ref[self.base + ((kind * FIELDS + field) * self.total) + index]


def hidden_of(preact):
    inner = preact * (gelu_coef + gelu_cubic * (preact * preact))
    half = 0.5 * preact
    return half + half * jnp.tanh(inner)


def slope_of(preact):
    cubic = gelu_cubic * (preact * preact)
    tangent = jnp.tanh(preact * (gelu_coef + cubic))
    bend = preact * (gelu_coef + 3.0 * cubic)
    return (0.5 + 0.5 * tangent) * (1.0 + bend * (1.0 - tangent))


def both_of(preact):
    cubic = gelu_cubic * (preact * preact)
    tangent = jnp.tanh(preact * (gelu_coef + cubic))
    bend = preact * (gelu_coef + 3.0 * cubic)
    half = 0.5 + 0.5 * tangent
    return (preact * half, half * (1.0 + bend * (1.0 - tangent)))


def dot_plain(left, right):
    return jnp.dot(left, right, preferred_element_type=jnp.float32)


def dot_right_t(left, right):
    return lax.dot_general(left, right, (((1,), (1,)), ((), ())), preferred_element_type=jnp.float32)


def each(count, body, unroll=1):
    def one(i, carry):
        body(i)
        return carry

    lax.fori_loop(0, count, one, 0, unroll=unroll)


def fill_normed(x_ref, normed, base):
    rows, width = x_ref.shape

    def tile(i):
        at = pl.multiple_of(i * ROW_TILE, ROW_TILE)
        wide = x_ref[pl.ds(at, ROW_TILE), :].astype(jnp.float32)
        factor = lax.rsqrt(jnp.mean(wide * wide, axis=-1, keepdims=True) + norm_eps)
        value = (wide * factor).astype(jnp.bfloat16)
        for b in range(width // BS):
            normed[b, pl.ds(base + at, ROW_TILE), :] = value[:, b * BS : (b + 1) * BS]

    each(rows // ROW_TILE, tile, 7)


def fill_split(x_ref, split, base):
    rows, width = x_ref.shape
    for b in range(width // BS):
        split[b, pl.ds(base, rows), :] = x_ref[:, b * BS : (b + 1) * BS]


def pair_product(source, blocks, lists, kind, p, transposed):
    left = jnp.concatenate(
        [source[lists(kind, FIRST_TAKE, p)], source[lists(kind, SECOND_TAKE, p)]], axis=1
    )
    one, two = blocks[lists(kind, FIRST, p)], blocks[lists(kind, SECOND, p)]
    if transposed:
        return dot_right_t(left, jnp.concatenate([one, two], axis=1))
    return dot_plain(left, jnp.concatenate([one, two], axis=0))


def wide_pass(source, blocks, lists, kind, sums, finish, transposed, batch=16, ahead=None):
    def main(i):
        if ahead is not None:
            ahead(i)
        for j in range(batch):
            c = i * batch + j
            value = pair_product(source, blocks, lists, kind, c, transposed)
            sums[c] = value
            finish(c, value)

    each(sums.shape[0] // batch, main)
    dot = dot_right_t if transposed else dot_plain

    def more(e):
        c = lists(kind, EXTRA_PUT, e)
        left = source[lists(kind, EXTRA_TAKE, e)]
        value = sums[c] + dot(left, blocks[lists(kind, EXTRA, e)])
        sums[c] = value
        finish(c, value)

    def batch(i):
        for j in range(EXTRA_BATCH):
            more(i * EXTRA_BATCH + j)

    each((lists(kind, COUNT, 0) + EXTRA_BATCH - 1) // EXTRA_BATCH, batch)


def narrow_pass(source, blocks, lists, kind, sums, transposed):
    sums[...] = jnp.zeros(sums.shape, sums.dtype)

    def one(p):
        sums[lists(kind, PUT, p)] += pair_product(source, blocks, lists, kind, p, transposed)

    each((lists.total + sums.shape[0]) // 2, one, 14)


def forward_rows(x_ref, out_ref, layer, scratch, slopes=None, before=lambda part: None, done=lambda: None):
    normed, sums, hidden, narrow = scratch
    rows, width = x_ref.shape
    fill_normed(x_ref, normed, 0)

    def finish(c, value):
        if slopes is None:
            hidden[c] = hidden_of(value).astype(jnp.bfloat16)
        else:
            value, slope = both_of(value)
            hidden[c] = value.astype(jnp.bfloat16)
            slopes[c] = slope.astype(slopes.dtype)

    before(0)
    wide_pass(normed, layer.up, layer.lists, UP_WIDE, sums, finish, False)
    before(1)
    done()
    narrow_pass(hidden, layer.down, layer.lists, DOWN_NARROW, narrow, False)
    for b in range(width // BS):
        cols = slice(b * BS, (b + 1) * BS)
        out_ref[:, cols] = (x_ref[:, cols].astype(jnp.float32) + narrow[b]).astype(jnp.bfloat16)


def backward_rows(x_ref, cot_ref, out_ref, layer, scratch, slopes, ready=lambda: None):
    normed, sums, hidden, narrow = scratch
    rows, width = x_ref.shape
    fill_split(cot_ref, normed, 0)
    ready()

    def finish(c, value):
        hidden[c] = (value * slopes[c].astype(jnp.float32)).astype(jnp.bfloat16)

    wide_pass(normed, layer.down, layer.lists, DOWN_WIDE, sums, finish, True)
    narrow_pass(hidden, layer.up, layer.lists, UP_NARROW, narrow, True)

    def tile(i):
        at = pl.multiple_of(i * ROW_TILE, ROW_TILE)
        wide = x_ref[pl.ds(at, ROW_TILE), :].astype(jnp.float32)
        factor = lax.rsqrt(jnp.mean(wide * wide, axis=-1, keepdims=True) + norm_eps)
        grad = jnp.concatenate(
            [narrow[b, pl.ds(at, ROW_TILE), :] for b in range(width // BS)], axis=-1
        )
        coupling = jnp.mean(wide * grad, axis=-1, keepdims=True)
        upstream = cot_ref[pl.ds(at, ROW_TILE), :].astype(jnp.float32)
        value = upstream + factor * grad - wide * (factor * factor * factor * coupling)
        out_ref[pl.ds(at, ROW_TILE), :] = value.astype(jnp.bfloat16)

    each(rows // ROW_TILE, tile)


def own_cell(layer, part, k):
    lists = layer.lists
    at = lists.cells + 2 * (part * lists.total + k)
    return lists.ref[at], lists.ref[at + 1]


class Layer:
    def __init__(self, info, lists_ref, weights_ref, which):
        copy = info[which]
        self.lists = Lists(lists_ref, copy, lists_ref.shape[0] // (2 * 4 * FIELDS + 4))
        if weights_ref is not None:
            self.up = weights_ref.at[copy, 0]
            self.down = weights_ref.at[copy, 1]


def stage(kernel, local_in, remote_in, outs, scratch, operands, cost, name, vmem=CHAIN_VMEM):
    info, lists, weights = operands
    held = [] if weights is None else [pltpu.with_memory_space_constraint(weights, pltpu.VMEM)]
    any_spec = pl.BlockSpec(memory_space=pltpu.HBM)
    smem_spec = pl.BlockSpec(memory_space=pltpu.SMEM)
    vmem_spec = pl.BlockSpec(memory_space=pltpu.VMEM)
    in_total = len(local_in) + len(remote_in)
    local_in = [pltpu.with_memory_space_constraint(array, pltpu.VMEM) for array in local_in]

    def body(info_ref, lists_ref, *rest):
        weights_ref, rest = (None, rest) if weights is None else (rest[0], rest[1:])
        ins, own = rest[:in_total], rest[in_total + len(outs) :]
        results = rest[in_total : in_total + len(outs)]

        def layer(which, weights_ref=weights_ref):
            return Layer(info_ref, lists_ref, weights_ref, which)

        kernel(layer, info_ref, ins, results, own)

    return pl.pallas_call(
        body,
        in_specs=[smem_spec, smem_spec]
        + [vmem_spec] * (len(held) + len(local_in))
        + [any_spec] * len(remote_in),
        out_specs=[any_spec if space is pltpu.HBM else vmem_spec for space, _ in outs],
        out_shape=[
            shape if space is LOCAL else space(shape.shape, shape.dtype) for space, shape in outs
        ],
        scratch_shapes=scratch,
        name=name,
        cost_estimate=pl.CostEstimate(flops=cost, transcendentals=0, bytes_accessed=0),
        compiler_params=pltpu.CompilerParams(vmem_limit_bytes=vmem),
    )(info, lists, *held, *local_in, *remote_in)

def layer_scratch(rows, width):
    return [
        pltpu.VMEM((width // BS + 1, rows, BS), jnp.bfloat16),
        pltpu.VMEM((FF_BLOCKS, rows, BS), jnp.float32),
        pltpu.VMEM((FF_BLOCKS + 1, rows, BS), jnp.bfloat16),
        pltpu.VMEM((width // BS, rows, BS), jnp.float32),
    ]


def slope_scratch(rows):
    return [pltpu.VMEM((FF_BLOCKS, rows, BS), jnp.float32)]


def shape_of(shape, dtype=jnp.bfloat16):
    return jax.ShapeDtypeStruct(shape, dtype)


def clear_spare(*refs):
    for ref in refs:
        ref[ref.shape[0] - 1] = jnp.zeros(ref.shape[1:], ref.dtype)


def forward_call(x, whichs, operands):
    rows, width = x.shape
    steps = len(whichs)
    slope_shape = (steps, FF_BLOCKS, rows, BS)

    def kernel(layer, info, ins, results, scratch):
        *layer_refs, slopes, sem = scratch
        clear_spare(layer_refs[0], layer_refs[2])
        moves = [
            pltpu.make_async_copy(slopes.at[i], results[-1].at[i], sem.at[i]) for i in range(steps)
        ]
        source = ins[0]
        for i, which in enumerate(whichs):
            forward_rows(
                source, results[i], layer(which), layer_refs, slopes.at[i], done=moves[i].start
            )
            source = results[i]
        for move in moves:
            move.wait()

    outs = [(LOCAL, shape_of(x.shape))] * steps + [(pltpu.HBM, shape_of(slope_shape))]
    scratch = [pltpu.VMEM(slope_shape, jnp.bfloat16), pltpu.SemaphoreType.DMA((steps,))]
    return stage(
        kernel, [x], [], outs, layer_scratch(rows, width) + scratch, operands, COST * steps, "forward"
    )


def enter_call(tokens, h, rows, unloaded, operands):
    width = tokens.shape[-1]

    def kernel(layer, info, ins, results, scratch):
        *layer_refs, x_ref, local, sem, weight_sem = scratch
        load = pltpu.make_async_copy(ins[0].at[info[HIGH], pl.ds(h * rows, rows)], x_ref, sem)
        load.start()
        low = info[LOW_LAYER]
        moves = [
            pltpu.make_async_copy(ins[1].at[low, part], local.at[low, part], weight_sem.at[part])
            for part in range(2)
        ]

        def before(part):
            moves[part].wait()
            if part == 0:
                moves[1].start()

        moves[0].start()
        clear_spare(layer_refs[0], layer_refs[2])
        load.wait()
        forward_rows(x_ref, results[0], layer(LOW_LAYER, local), layer_refs, before=before)
    outs = [(LOCAL, shape_of((rows, width)))]
    scratch = layer_scratch(rows, width) + [
        pltpu.VMEM((rows, width), jnp.bfloat16),
        pltpu.VMEM(unloaded.shape, unloaded.dtype),
        pltpu.SemaphoreType.DMA,
        pltpu.SemaphoreType.DMA((2,)),
    ]
    return stage(kernel, [], [tokens, unloaded], outs, scratch, operands, COST, "enter", ENTER_VMEM)


def turn_call(x, targets, h, operands):
    rows, width = x.shape

    def kernel(layer, info, ins, results, scratch):
        *layer_refs, slopes, aim, sem = scratch
        x_ref, target_ref = ins
        residue, out = results
        load = pltpu.make_async_copy(target_ref.at[info[HIGH], pl.ds(h * rows, rows)], aim, sem)
        load.start()
        clear_spare(layer_refs[0], layer_refs[2])
        own = layer(HIGH_LAYER)
        forward_rows(x_ref, residue, own, layer_refs, slopes)
        load.wait()
        for b in range(width // BS):
            cols = slice(b * BS, (b + 1) * BS)
            difference = residue[:, cols].astype(jnp.float32) - aim[:, cols].astype(jnp.float32)
            residue[:, cols] = difference.astype(jnp.bfloat16)
        backward_rows(x_ref, residue, out, own, layer_refs, slopes)

    return stage(
        kernel, [x], [targets], [(LOCAL, shape_of(x.shape))] * 2,
        layer_scratch(rows, width) + slope_scratch(rows)
        + [pltpu.VMEM((rows, width), jnp.bfloat16), pltpu.SemaphoreType.DMA],
        operands, 3 * COST, "turn"
    )


def backward_call(xs, saved, cot, whichs, operands):
    rows, width = cot.shape
    steps = len(whichs)

    def kernel(layer, info, ins, results, scratch):
        *layer_refs, slopes, sem = scratch
        moves = [
            pltpu.make_async_copy(ins[steps + 1 + i].at[saved[i][1]], slopes.at[i], sem.at[i])
            for i in range(steps)
        ]
        for move in moves:
            move.start()
        clear_spare(layer_refs[0], layer_refs[2])
        upstream = ins[steps]
        for i, which in enumerate(whichs):
            backward_rows(
                ins[i], upstream, results[i], layer(which), layer_refs, slopes.at[i], moves[i].wait
            )
            upstream = results[i]

    scratch = [
        pltpu.VMEM((steps, FF_BLOCKS, rows, BS), jnp.bfloat16),
        pltpu.SemaphoreType.DMA((steps,)),
    ]
    return stage(
        kernel, list(xs) + [cot], [array for array, _ in saved],
        [(LOCAL, shape_of(cot.shape))] * steps, layer_scratch(rows, width) + scratch, operands,
        2 * COST * steps, "backward"
    )


def fetch_pieces(info, choices, refs, local, sem):
    first = (info[HIGH] == 0) & (info[GROUP] == 0)
    moves = []
    for piece, options in enumerate(choices):
        for kind, wanted, number, index in options:
            source = refs[number] if index is None else refs[number].at[index]
            move = pltpu.make_async_copy(source, local.at[piece], sem.at[piece])
            if kind == "first":
                condition = first
            elif kind == "own":
                condition = (info[HIGH] == wanted[0]) & (info[GROUP] == wanted[1]) & ~first
            else:
                condition = ~first

            @pl.when(condition)
            def go(move=move):
                move.start()

        moves.append(move)
    return moves


def ups_call(refs, choices, after, rows, width, unloaded, operands):
    pieces = len(choices)
    all_rows = rows * pieces
    part_rows = all_rows // 2

    def kernel(layer, info, ins, results, scratch):
        x_refs, sums, blocks_here, slopes, normed, sem, block_sem, out_sem = scratch
        hidden, slopes_out, normed_out = results
        load = pltpu.make_async_copy(ins[-1].at[0, 0], blocks_here, block_sem.at[0])
        load.start()
        moves = fetch_pieces(info, choices, ins, x_refs, sem)
        own = layer(OWN_LAYER)
        clear_spare(normed)
        for move in moves:
            move.wait()

        def normalise(piece):
            fill_normed(x_refs.at[piece], normed, piece * rows)

        each(pieces, normalise)
        keep = pltpu.make_async_copy(normed, normed_out, block_sem.at[1])
        keep.start()
        load.wait()

        def put(part):
            span = pl.ds(pl.multiple_of(part * part_rows, part_rows), part_rows)
            return pltpu.make_async_copy(slopes.at[part], slopes_out.at[:, span], out_sem.at[part])

        def one(part):
            span = pl.ds(pl.multiple_of(part * part_rows, part_rows), part_rows)

            def finish(c, value):
                value, slope = both_of(value)
                hidden[c, span, :] = value.astype(jnp.bfloat16)
                slopes[part, c] = slope.astype(jnp.bfloat16)

            wide_pass(
                normed.at[:, span], blocks_here, own.lists, UP_WIDE, sums, finish, False, 8
            )
            put(part).start()

        each(2, one)
        keep.wait()
        for part in range(2):
            put(part).wait()

    return stage(
        kernel, [], refs + [after, unloaded],
        [
            (pltpu.VMEM, shape_of((FF_BLOCKS, all_rows, BS))),
            (pltpu.HBM, shape_of((FF_BLOCKS, all_rows, BS))),
            (pltpu.HBM, shape_of((width // BS + 1, all_rows, BS))),
        ],
        [
            pltpu.VMEM((pieces, rows, width), jnp.bfloat16),
            pltpu.VMEM((FF_BLOCKS, part_rows, BS), jnp.float32),
            pltpu.VMEM(unloaded.shape[2:], unloaded.dtype),
            pltpu.VMEM((2, FF_BLOCKS, part_rows, BS), jnp.bfloat16),
            pltpu.VMEM((width // BS + 1, all_rows, BS), jnp.bfloat16),
            pltpu.SemaphoreType.DMA((pieces,)),
            pltpu.SemaphoreType.DMA((2,)),
            pltpu.SemaphoreType.DMA((2,)),
        ],
        operands, 4 * COST, "ups", ENTER_VMEM
    )


def spread(out, k, value, shares):
    share_rows = BS // shares
    for share in range(shares):
        out[share, k] = value[share * share_rows : (share + 1) * share_rows]


def down_grads_call(refs, choices, hidden, rows, width, shares, total, operands):
    pieces = len(choices)
    all_rows = rows * pieces

    def kernel(layer, info, ins, results, scratch):
        cot_refs, split, turned, sem, out_sem = scratch
        out, split_out = results
        hidden_ref, refs = ins[0], ins[1:]
        own = layer(OWN_LAYER)
        moves = fetch_pieces(info, choices, refs, cot_refs, sem)
        clear_spare(split)
        for piece in range(pieces):
            moves[piece].wait()
            fill_split(cot_refs.at[piece], split, piece * rows)
        keep = pltpu.make_async_copy(split, split_out, out_sem)
        keep.start()
        for b in range(width // BS):
            turned[b] = split[b].T

        def one(k):
            row, col = own_cell(own, 1, k)
            value = dot_plain(turned[col], hidden_ref[row])
            spread(out, k, value.T.astype(jnp.bfloat16), shares)

        each(total, one, 12)
        keep.wait()

    return stage(
        kernel, [hidden], refs,
        [
            (LOCAL, shape_of((shares, total, BS // shares, BS))),
            (pltpu.HBM, shape_of((width // BS + 1, all_rows, BS))),
        ],
        [
            pltpu.VMEM((pieces, rows, width), jnp.bfloat16),
            pltpu.VMEM((width // BS + 1, all_rows, BS), jnp.bfloat16),
            pltpu.VMEM((width // BS, BS, all_rows), jnp.bfloat16),
            pltpu.SemaphoreType.DMA((pieces,)),
            pltpu.SemaphoreType.DMA,
        ],
        operands, 2 * COST, "down_grads"
    )


def up_grads_call(split, normed, slopes, width, shares, unloaded, operands):
    all_rows = split.shape[1]
    part_rows = all_rows // 2
    total = unloaded.shape[2]
    blocks = width // BS

    def kernel(layer, info, ins, results, scratch):
        sums, grad_pre, turned, *local, sem = scratch
        normed_ref, split_ref, blocks_here, slopes_ref = local
        out = results[0]
        sources = [ins[0], ins[1], ins[3].at[0, 1], ins[2]]
        moves = [
            pltpu.make_async_copy(source, target, sem.at[i])
            for i, (source, target) in enumerate(zip(sources, local))
        ]
        for move in moves:
            move.start()
        own = layer(OWN_LAYER)
        moves[0].wait()
        for b in range(blocks):
            turned[b] = normed_ref[b].T
        for move in moves[1:]:
            move.wait()

        def part_of(part):
            span = pl.ds(pl.multiple_of(part * part_rows, part_rows), part_rows)

            def finish(c, value):
                slope = slopes_ref[c, span, :].astype(jnp.float32)
                grad_pre[c, span, :] = (value * slope).astype(jnp.bfloat16)

            wide_pass(
                split_ref.at[:, span], blocks_here, own.lists, DOWN_WIDE, sums, finish, True, 4
            )

        each(2, part_of)

        def one(k):
            row, col = own_cell(own, 0, k)
            value = dot_plain(turned[row], grad_pre[col])
            spread(out, k, value.astype(jnp.bfloat16), shares)

        each(total, one, 4)

    return stage(
        kernel, [], [normed, split, slopes, unloaded],
        [(LOCAL, shape_of((shares, total, BS // shares, BS)))],
        [
            pltpu.VMEM((FF_BLOCKS, part_rows, BS), jnp.float32),
            pltpu.VMEM((FF_BLOCKS, all_rows, BS), jnp.bfloat16),
            pltpu.VMEM((blocks, BS, all_rows), jnp.bfloat16),
            pltpu.VMEM(normed.shape, normed.dtype),
            pltpu.VMEM(split.shape, split.dtype),
            pltpu.VMEM(unloaded.shape[2:], unloaded.dtype),
            pltpu.VMEM(slopes.shape, slopes.dtype),
            pltpu.SemaphoreType.DMA((4,)),
        ],
        operands, 4 * COST, "up_grads", OWN_VMEM
    )[0]


def adam_update(grad_sum, master, moment, variance, token_total):
    gradient = grad_sum / token_total
    moment_next = beta_first * moment + (1.0 - beta_first) * gradient
    variance_next = beta_second * variance + (1.0 - beta_second) * gradient * gradient
    corrected = moment_next / (1.0 - beta_first**update_count)
    spread = jnp.sqrt(variance_next / (1.0 - beta_second**update_count))
    step_direction = corrected / (spread + adam_eps)
    return (step_direction, master - learn_rate * (step_direction + decay_rate * master))


def shards(tokens, targets, weights, pattern, master, moment, variance):
    section = lax.axis_index("section")
    sections = lax.axis_size("section")
    shares = lax.axis_size("dp")
    groups = sections // 2
    micro, rows_each, width = tokens.shape[1:]
    rows = micro * rows_each
    half = rows // 2
    high = section >= groups
    high_member = high.astype(jnp.int32)
    group = jnp.minimum(section, sections - 1 - section)
    info = jnp.stack([high_member, 1 - high_member, jnp.zeros_like(high_member), high_member, group])
    far = lambda array: pltpu.with_memory_space_constraint(array, pltpu.HBM)
    tokens = far(tokens.reshape(2, rows, width))
    targets = far(targets.reshape(2, rows, width))
    pattern = pattern[0]
    lists = block_lists(pattern, width)
    mirror = lambda i: sections - 1 - i

    def lane(i, h):
        other = mirror(i + 1) if h else i + 1
        return [(i, other), (mirror(i), mirror(other))]

    def inward(x, i, h):
        return lax.ppermute(x, "section", lane(i, h))

    def outward(x, i, h):
        return lax.ppermute(x, "section", [(b, a) for a, b in lane(i, h)])

    def at_half(records, h, start=0):
        value = records[start][h]
        for i in range(start + 1, groups):
            value = jnp.where(group == i, records[i][h], value)
        return value

    def swap(low_records, high_records, h):
        sent = jnp.where(high, at_half(low_records, h, 1), at_half(high_records, h))
        pairs = [(i, mirror(i)) for i in range(groups)] + [(mirror(i), i) for i in range(1, groups)]
        return lax.ppermute(sent, "section", pairs)

    halves = range(2)
    x_low, x_high, cot_low, cot_high = [[None] * groups for _ in range(4)]
    unloaded = far(weights[0])
    slope_low, slope_high = [[None] * groups for _ in range(2)]
    current = [enter_call(tokens, h, half, unloaded, (info, lists, None))[0] for h in halves]
    operands = (info, lists, weights[0])
    for i in range(groups - 1):
        current = [inward(current[h], i, h) for h in halves]
        x_low[i + 1] = current
        if i + 1 < groups - 1:
            moved = [forward_call(current[h], [LOW_LAYER], operands) for h in halves]
            current = [m[0] for m in moved]
            slope_low[i + 1] = [(far(m[1]), 0) for m in moved]
    both = [forward_call(current[h], [LOW_LAYER, HIGH_LAYER], operands) for h in halves]
    x_high[groups - 1] = [b[0] for b in both]
    slope_low[groups - 1] = [(far(b[2]), 0) for b in both]
    slope_high[groups - 1] = [(far(b[2]), 1) for b in both]
    current = [b[1] for b in both]
    for i in reversed(range(groups - 1)):
        current = [outward(current[h], i, h) for h in halves]
        x_high[i] = current
        if i > 0:
            moved = [forward_call(current[h], [HIGH_LAYER], operands) for h in halves]
            current = [m[0] for m in moved]
            slope_high[i] = [(far(m[1]), 0) for m in moved]
    turned = [turn_call(current[h], targets, h, operands) for h in halves]
    cot_high[0] = [t[0] for t in turned]
    current = [t[1] for t in turned]
    for i in range(groups - 1):
        current = [inward(current[h], i, h) for h in halves]
        cot_high[i + 1] = current
        if i + 1 < groups - 1:
            current = [
                backward_call(
                    [x_high[i + 1][h]], [slope_high[i + 1][h]], current[h], [HIGH_LAYER], operands
                )[0]
                for h in halves
            ]
    last = groups - 1
    both = [
        backward_call(
            [x_high[last][h], x_low[last][h]], [slope_high[last][h], slope_low[last][h]], current[h],
            [HIGH_LAYER, LOW_LAYER], operands
        )
        for h in halves
    ]
    cot_low[last] = [b[0] for b in both]
    current = [b[1] for b in both]
    for i in reversed(range(1, last)):
        current = [outward(current[h], i, h) for h in halves]
        cot_low[i] = current
        current = [
            backward_call([x_low[i][h]], [slope_low[i][h]], current[h], [LOW_LAYER], operands)[0]
            for h in halves
        ]
    from_low = [lax.ppermute(current[h], "section", [(1, 0)]) for h in halves]
    from_high = [lax.ppermute(current[h], "section", [(mirror(1), 0)]) for h in halves]
    x_other = [swap(x_low, x_high, h) for h in halves]
    cot_other = [swap(cot_low, cot_high, h) for h in halves]

    def choose(low_records, high_records, others, first_own, first_other):
        refs, choices = [], []

        def add(array):
            refs.append(array)
            return len(refs) - 1

        for h in halves:
            array, index = first_own[h]
            options = [("first", None, add(array), index)]
            for i in range(groups):
                if i > 0:
                    options.append(("own", (0, i), add(low_records[i][h]), None))
                options.append(("own", (1, i), add(high_records[i][h]), None))
            choices.append(options)
        for h in halves:
            array, index = first_other[h]
            choices.append([("first", None, add(array), index), ("rest", None, add(others[h]), None)])
        return refs, choices

    def token_piece(member, h):
        return (tokens, (member, pl.ds(h * half, half)))

    refs, choices = choose(
        x_low, x_high, x_other, [token_piece(0, h) for h in halves], [token_piece(1, h) for h in halves]
    )
    hidden, slopes, normed = ups_call(refs, choices, current[1], half, width, unloaded, (info, lists, None))
    refs, choices = choose(
        cot_low, cot_high, cot_other,
        [(from_low[0], None), (from_high[1], None)], [(from_high[0], None), (from_low[1], None)]
    )
    downs, split = down_grads_call(
        refs, choices, hidden, half, width, shares, unloaded.shape[2], (info, lists, None)
    )

    def reduce(grads):
        return lax.psum_scatter(grads, "dp", scatter_dimension=0, tiled=True)[0].astype(jnp.float32)

    down_share = reduce(downs)
    up_share = reduce(up_grads_call(far(split), far(normed), far(slopes), width, shares, unloaded, (info, lists, None)))
    token_total = 2 * rows * shares
    step_direction, master_next = adam_update(
        jnp.stack([down_share, up_share])[::-1], master[0], moment[0], variance[0], token_total
    )
    return (step_direction[None], master_next[None])


def solution(mesh):
    rows_split = P(None, None, "dp", None)
    by_section = P("section", None, None, "dp", None)
    return jax.shard_map(
        shards,
        mesh=mesh,
        in_specs=(
            rows_split,
            rows_split,
            P("section", None, None, None, None, None),
            P("section", None, None, None, None),
            by_section,
            by_section,
            by_section,
        ),
        out_specs=(by_section, by_section),
        check_vma=False,
    )
```

```python
import jax
import jax.numpy as jnp
from jax import lax
from jax.experimental import pallas as pl
from jax.experimental.pallas import tpu as pltpu
from jax.sharding import PartitionSpec as P


BS = 128
FF_BLOCKS = 8192 // BS
norm_eps = 1e-06
gelu_coef = 0.7978845608028654
gelu_cubic = gelu_coef * 0.044715
beta_first = 0.9
beta_second = 0.95
adam_eps = 1e-08
learn_rate = 0.001
decay_rate = 0.1
update_count = 10
ROW_TILE = 16
EXTRA_BATCH = 4
CHAIN_VMEM = 24 * 1024 * 1024
ENTER_VMEM = 32 * 1024 * 1024
OWN_VMEM = 40 * 1024 * 1024
COST = 4_000_000_000
LOCAL = None
ENTER_COST = 1
LOW_LAYER, HIGH_LAYER, OWN_LAYER, HIGH, GROUP = range(5)
UP_WIDE, DOWN_WIDE, DOWN_NARROW, UP_NARROW = range(4)
FIELDS = 9
FIRST, FIRST_TAKE, SECOND, SECOND_TAKE, PUT, EXTRA, EXTRA_TAKE, EXTRA_PUT, COUNT = range(FIELDS)


def block_lists(pattern, width):
    total = pattern.shape[2]
    up_row, up_col = pattern[:, 0, :, 0], pattern[:, 0, :, 1]
    down_row, down_col = pattern[:, 1, :, 0], pattern[:, 1, :, 1]
    key = jnp.stack([up_col, down_row, down_col, up_row], 1)
    take = jnp.stack([up_row, down_col, down_row, up_col], 1)
    order = jnp.arange(total, dtype=jnp.int32)
    before = order[None, :] < order[:, None]

    def count(mask):
        return jnp.sum(mask.astype(jnp.int32), axis=-1)

    same = key[..., None, :] == key[..., :, None]
    rank = count(same & before)
    even = rank % 2 == 0
    wide = (jnp.arange(4) < 2)[None, :, None]
    extra = rank >= 2
    extra_place = count(extra[..., None, :] & before)
    pair = count((key[..., None, :] < key[..., :, None]) & even[..., None, :]) + rank // 2
    place_first = jnp.where(wide, jnp.where(rank == 0, key, -1), jnp.where(even, pair, -1))
    place_second = jnp.where(wide, jnp.where(rank == 1, key, -1), jnp.where(even, -1, pair))
    place_extra = jnp.where(wide & extra, extra_place, -1)
    number = jnp.broadcast_to(order, key.shape)
    places = jnp.stack(
        [place_first] * 2 + [place_second] * 2 + [place_first] + [place_extra] * 3, 2
    )
    absent = jnp.where(wide, width // BS, FF_BLOCKS)
    lowered = take - absent
    values = jnp.stack([number, lowered, number, lowered, key, number, lowered, key], 2)
    hit = places[..., None, :] == order[:, None]
    fields = jnp.sum(jnp.where(hit, values[..., None, :], 0), axis=-1)
    slot = jnp.arange(8)
    taken = (slot == FIRST_TAKE) | (slot == SECOND_TAKE) | (slot == EXTRA_TAKE)
    fields = fields + jnp.where(taken[:, None], absent[..., None], 0)
    counts = jnp.where(wide[..., 0], count(extra), count(even))
    counts = jnp.broadcast_to(counts[..., None, None], key.shape[:2] + (1, total))
    lists = jnp.concatenate([fields, counts], axis=2).astype(jnp.int32)
    return jnp.concatenate([lists.reshape(-1), pattern[0].reshape(-1)])


class Lists:
    def __init__(self, ref, copy, total):
        self.ref, self.total = ref, total
        self.base = copy * (4 * FIELDS * total)
        self.cells = 2 * 4 * FIELDS * total

    def __call__(self, kind, field, index):
        return self.ref[self.base + ((kind * FIELDS + field) * self.total) + index]


def hidden_of(preact):
    inner = preact * (gelu_coef + gelu_cubic * (preact * preact))
    half = 0.5 * preact
    return half + half * jnp.tanh(inner)


def both_of(preact):
    cubic = gelu_cubic * (preact * preact)
    tangent = jnp.tanh(preact * (gelu_coef + cubic))
    bend = preact * (gelu_coef + 3.0 * cubic)
    half = 0.5 + 0.5 * tangent
    return (preact * half, half * (1.0 + bend * (1.0 - tangent)))


def dot_plain(left, right):
    return jnp.dot(left, right, preferred_element_type=jnp.float32)


def dot_right_t(left, right):
    return lax.dot_general(left, right, (((1,), (1,)), ((), ())), preferred_element_type=jnp.float32)


def each(count, body, unroll=1):
    def one(i, carry):
        body(i)
        return carry

    lax.fori_loop(0, count, one, 0, unroll=unroll)


def fill_normed(x_ref, normed, base):
    rows, width = x_ref.shape

    def tile(i):
        at = pl.multiple_of(i * ROW_TILE, ROW_TILE)
        wide = x_ref[pl.ds(at, ROW_TILE), :].astype(jnp.float32)
        factor = lax.rsqrt(jnp.mean(wide * wide, axis=-1, keepdims=True) + norm_eps)
        value = (wide * factor).astype(jnp.bfloat16)
        for b in range(width // BS):
            normed[b, pl.ds(base + at, ROW_TILE), :] = value[:, b * BS : (b + 1) * BS]

    each(rows // ROW_TILE, tile, 7)


def fill_split(x_ref, split, base):
    rows, width = x_ref.shape
    for b in range(width // BS):
        split[b, pl.ds(base, rows), :] = x_ref[:, b * BS : (b + 1) * BS]


def pair_product(source, blocks, lists, kind, p, transposed):
    left = jnp.concatenate(
        [source[lists(kind, FIRST_TAKE, p)], source[lists(kind, SECOND_TAKE, p)]], axis=1
    )
    one, two = blocks[lists(kind, FIRST, p)], blocks[lists(kind, SECOND, p)]
    if transposed:
        return dot_right_t(left, jnp.concatenate([one, two], axis=1))
    return dot_plain(left, jnp.concatenate([one, two], axis=0))


def wide_pass(source, blocks, lists, kind, sums, finish, transposed, batch=16, ahead=None):
    def main(i):
        if ahead is not None:
            ahead(i)
        for j in range(batch):
            c = i * batch + j
            value = pair_product(source, blocks, lists, kind, c, transposed)
            sums[c] = value
            finish(c, value)

    each(sums.shape[0] // batch, main)
    dot = dot_right_t if transposed else dot_plain

    def more(e):
        c = lists(kind, EXTRA_PUT, e)
        left = source[lists(kind, EXTRA_TAKE, e)]
        value = sums[c] + dot(left, blocks[lists(kind, EXTRA, e)])
        sums[c] = value
        finish(c, value)

    def batch(i):
        for j in range(EXTRA_BATCH):
            more(i * EXTRA_BATCH + j)

    each((lists(kind, COUNT, 0) + EXTRA_BATCH - 1) // EXTRA_BATCH, batch)


def narrow_pass(source, blocks, lists, kind, sums, transposed):
    sums[...] = jnp.zeros(sums.shape, sums.dtype)

    def one(p):
        sums[lists(kind, PUT, p)] += pair_product(source, blocks, lists, kind, p, transposed)

    each((lists.total + sums.shape[0]) // 2, one, 14)


def forward_rows(x_ref, out_ref, layer, scratch, slopes=None, before=lambda part: None, done=lambda: None):
    normed, sums, hidden, narrow = scratch
    _, width = x_ref.shape
    fill_normed(x_ref, normed, 0)

    def finish(c, value):
        if slopes is None:
            hidden[c] = hidden_of(value).astype(jnp.bfloat16)
        else:
            value, slope = both_of(value)
            hidden[c] = value.astype(jnp.bfloat16)
            slopes[c] = slope.astype(slopes.dtype)

    before(0)
    wide_pass(normed, layer.up, layer.lists, UP_WIDE, sums, finish, False)
    before(1)
    done()
    narrow_pass(hidden, layer.down, layer.lists, DOWN_NARROW, narrow, False)
    for b in range(width // BS):
        cols = slice(b * BS, (b + 1) * BS)
        out_ref[:, cols] = (x_ref[:, cols].astype(jnp.float32) + narrow[b]).astype(jnp.bfloat16)


def backward_rows(x_ref, cot_ref, out_ref, layer, scratch, slopes, ready=lambda: None):
    normed, sums, hidden, narrow = scratch
    rows, width = x_ref.shape
    fill_split(cot_ref, normed, 0)
    ready()

    def finish(c, value):
        hidden[c] = (value * slopes[c].astype(jnp.float32)).astype(jnp.bfloat16)

    wide_pass(normed, layer.down, layer.lists, DOWN_WIDE, sums, finish, True)
    narrow_pass(hidden, layer.up, layer.lists, UP_NARROW, narrow, True)

    def tile(i):
        at = pl.multiple_of(i * ROW_TILE, ROW_TILE)
        wide = x_ref[pl.ds(at, ROW_TILE), :].astype(jnp.float32)
        factor = lax.rsqrt(jnp.mean(wide * wide, axis=-1, keepdims=True) + norm_eps)
        grad = jnp.concatenate(
            [narrow[b, pl.ds(at, ROW_TILE), :] for b in range(width // BS)], axis=-1
        )
        coupling = jnp.mean(wide * grad, axis=-1, keepdims=True)
        upstream = cot_ref[pl.ds(at, ROW_TILE), :].astype(jnp.float32)
        value = upstream + factor * grad - wide * (factor * factor * factor * coupling)
        out_ref[pl.ds(at, ROW_TILE), :] = value.astype(jnp.bfloat16)

    each(rows // ROW_TILE, tile)


def own_cell(layer, part, k):
    lists = layer.lists
    at = lists.cells + 2 * (part * lists.total + k)
    return lists.ref[at], lists.ref[at + 1]


class Layer:
    def __init__(self, info, lists_ref, weights_ref, which, local=None):
        copy = info[which]
        self.lists = Lists(lists_ref, copy, lists_ref.shape[0] // (2 * 4 * FIELDS + 4))
        if weights_ref is not None:
            local = weights_ref.at[copy]
        if local is not None:
            self.up, self.down = local.at[0], local.at[1]


def stage(kernel, local_in, remote_in, outs, scratch, operands, cost, vmem=CHAIN_VMEM):
    info, lists, weights = operands
    held = [] if weights is None else [pltpu.with_memory_space_constraint(weights, pltpu.VMEM)]
    any_spec = pl.BlockSpec(memory_space=pltpu.HBM)
    smem_spec = pl.BlockSpec(memory_space=pltpu.SMEM)
    vmem_spec = pl.BlockSpec(memory_space=pltpu.VMEM)
    in_total = len(local_in) + len(remote_in)
    local_in = [pltpu.with_memory_space_constraint(array, pltpu.VMEM) for array in local_in]

    def body(info_ref, lists_ref, *rest):
        weights_ref, rest = (None, rest) if weights is None else (rest[0], rest[1:])
        ins, own = rest[:in_total], rest[in_total + len(outs) :]
        results = rest[in_total : in_total + len(outs)]

        def layer(which, weights_ref=weights_ref, local=None):
            return Layer(info_ref, lists_ref, weights_ref, which, local)

        kernel(layer, info_ref, ins, results, own)

    return pl.pallas_call(
        body,
        in_specs=[smem_spec, smem_spec]
        + [vmem_spec] * (len(held) + len(local_in))
        + [any_spec] * len(remote_in),
        out_specs=[any_spec if space is pltpu.HBM else vmem_spec for space, _ in outs],
        out_shape=[
            shape if space is LOCAL else space(shape.shape, shape.dtype) for space, shape in outs
        ],
        scratch_shapes=scratch,
        cost_estimate=pl.CostEstimate(flops=cost, transcendentals=0, bytes_accessed=0),
        compiler_params=pltpu.CompilerParams(vmem_limit_bytes=vmem),
    )(info, lists, *held, *local_in, *remote_in)


def layer_scratch(rows, width):
    return [
        pltpu.VMEM((width // BS + 1, rows, BS), jnp.bfloat16),
        pltpu.VMEM((FF_BLOCKS, rows, BS), jnp.float32),
        pltpu.VMEM((FF_BLOCKS + 1, rows, BS), jnp.bfloat16),
        pltpu.VMEM((width // BS, rows, BS), jnp.float32),
    ]


def slope_scratch(rows):
    return [pltpu.VMEM((FF_BLOCKS, rows, BS), jnp.float32)]


def shape_of(shape, dtype=jnp.bfloat16):
    return jax.ShapeDtypeStruct(shape, dtype)


def clear_spare(*refs):
    for ref in refs:
        ref[ref.shape[0] - 1] = jnp.zeros(ref.shape[1:], ref.dtype)


def forward_call(x, whichs, operands):
    rows, width = x.shape
    steps = len(whichs)
    slope_shape = (steps, FF_BLOCKS, rows, BS)

    def kernel(layer, info, ins, results, scratch):
        *layer_refs, slopes, sem = scratch
        clear_spare(layer_refs[0], layer_refs[2])
        moves = [
            pltpu.make_async_copy(slopes.at[i], results[-1].at[i], sem.at[i]) for i in range(steps)
        ]
        source = ins[0]
        for i, which in enumerate(whichs):
            forward_rows(
                source, results[i], layer(which), layer_refs, slopes.at[i], done=moves[i].start
            )
            source = results[i]
        for move in moves:
            move.wait()

    outs = [(LOCAL, shape_of(x.shape))] * steps + [(pltpu.HBM, shape_of(slope_shape))]
    scratch = [pltpu.VMEM(slope_shape, jnp.bfloat16), pltpu.SemaphoreType.DMA((steps,))]
    return stage(
        kernel, [x], [], outs, layer_scratch(rows, width) + scratch, operands, COST * steps
    )


def enter_call(tokens, h, rows, unloaded, operands):
    width = tokens.shape[-1]

    def kernel(layer, info, ins, results, scratch):
        *layer_refs, x_ref, local, sem, weight_sem = scratch
        load = pltpu.make_async_copy(ins[0].at[info[HIGH], pl.ds(h * rows, rows)], x_ref, sem)
        load.start()
        low = info[LOW_LAYER]
        moves = [
            pltpu.make_async_copy(ins[1].at[low, part], local.at[part], weight_sem.at[part])
            for part in range(2)
        ]

        def before(part):
            moves[part].wait()
            if part == 0:
                moves[1].start()

        moves[0].start()
        clear_spare(layer_refs[0], layer_refs[2])
        load.wait()
        forward_rows(x_ref, results[0], layer(LOW_LAYER, None, local), layer_refs, before=before)

    outs = [(LOCAL, shape_of((rows, width)))]
    scratch = layer_scratch(rows, width) + [
        pltpu.VMEM((rows, width), jnp.bfloat16),
        pltpu.VMEM(unloaded.shape[1:], unloaded.dtype),
        pltpu.SemaphoreType.DMA,
        pltpu.SemaphoreType.DMA((2,)),
    ]
    return stage(kernel, [], [tokens, unloaded], outs, scratch, operands, COST * ENTER_COST, CHAIN_VMEM)


def turn_call(x, targets, h, operands, entries=None):
    rows, width = x.shape
    local = [x] + ([] if entries is None else [e for pair in entries for e in pair])

    def kernel(layer, info, ins, results, scratch):
        *layer_refs, slopes, aim, sem = scratch
        x_ref, target_ref = ins[0], ins[-1]
        residue, out = results[:2]
        load = pltpu.make_async_copy(target_ref.at[info[HIGH], pl.ds(h * rows, rows)], aim, sem)
        load.start()
        clear_spare(layer_refs[0], layer_refs[2])
        own = layer(HIGH_LAYER)
        forward_rows(x_ref, residue, own, layer_refs, slopes)
        load.wait()
        for b in range(width // BS):
            cols = slice(b * BS, (b + 1) * BS)
            difference = residue[:, cols].astype(jnp.float32) - aim[:, cols].astype(jnp.float32)
            residue[:, cols] = difference.astype(jnp.bfloat16)
        backward_rows(x_ref, residue, out, own, layer_refs, slopes)
        if entries is not None:
            high, group = info[HIGH] == 1, info[GROUP]
            conditions = [~high & (group == 0), ~high & (group != 0), high]
            for i in range(2):
                sources = [ins[1 + 2 * j + i] for j in range(3)]
                pick_rows(results[2].at[pl.ds(i * rows, rows)], list(zip(conditions, sources)))

    outs = [(LOCAL, shape_of(x.shape))] * 2
    if entries is not None:
        outs.append((LOCAL, shape_of((2 * rows, width))))
    return stage(
        kernel, local, [targets], outs,
        layer_scratch(rows, width) + slope_scratch(rows)
        + [pltpu.VMEM((rows, width), jnp.bfloat16), pltpu.SemaphoreType.DMA],
        operands, 3 * COST
    )


def pick_rows(target, options):
    for condition, source in options:

        @pl.when(condition)
        def take(source=source):
            target[...] = source[...]


def backward_call(xs, saved, cot, whichs, operands, turned=None, last=None):
    rows, width = cot.shape
    steps = len(whichs)
    local = list(xs) + [cot] + ([] if turned is None else [turned])

    def kernel(layer, info, ins, results, scratch):
        *layer_refs, slopes, sem = scratch
        moves = [
            pltpu.make_async_copy(ins[len(local) + i].at[saved[i][1]], slopes.at[i], sem.at[i])
            for i in range(steps)
        ]
        for move in moves:
            move.start()
        clear_spare(layer_refs[0], layer_refs[2])
        upstream = ins[steps]
        for i, which in enumerate(whichs):
            backward_rows(
                ins[i], upstream, results[i], layer(which), layer_refs, slopes.at[i], moves[i].wait
            )
            upstream = results[i]
        if turned is not None:
            high, group = info[HIGH] == 1, info[GROUP]
            pick_rows(
                results[steps],
                [
                    (high, results[0]),
                    (~high & (group == last), ins[steps]),
                    (~high & (group != last), ins[steps + 1]),
                ],
            )

    scratch = [
        pltpu.VMEM((steps, FF_BLOCKS, rows, BS), jnp.bfloat16),
        pltpu.SemaphoreType.DMA((steps,)),
    ]
    outs = [(LOCAL, shape_of(cot.shape))] * (steps + (turned is not None))
    return stage(
        kernel, local, [array for array, _ in saved], outs, layer_scratch(rows, width) + scratch,
        operands, 2 * COST * steps
    )


def fetch_pieces(info, choices, refs, local, sem):
    first = (info[HIGH] == 0) & (info[GROUP] == 0)
    moves = []
    for piece, options in enumerate(choices):
        for kind, wanted, number, index in options:
            source = refs[number] if index is None else refs[number].at[index]
            move = pltpu.make_async_copy(source, local.at[piece], sem.at[piece])
            if kind == "first":
                condition = first
            elif kind == "own":
                condition = (info[HIGH] == wanted[0]) & (info[GROUP] == wanted[1]) & ~first
            else:
                condition = ~first

            @pl.when(condition)
            def go(move=move):
                move.start()

        moves.append(move)
    return moves


def ups_call(refs, choices, after, rows, width, unloaded, operands):
    pieces = len(choices)
    all_rows = rows * pieces
    part_rows = all_rows // 2

    def kernel(layer, info, ins, results, scratch):
        x_refs, sums, blocks_here, slopes, normed, sem, block_sem, out_sem = scratch
        hidden, slopes_out, normed_out = results
        load = pltpu.make_async_copy(ins[-1].at[0, 0], blocks_here, block_sem.at[0])
        load.start()
        moves = fetch_pieces(info, choices, ins, x_refs, sem)
        own = layer(OWN_LAYER)
        clear_spare(normed)
        for move in moves:
            move.wait()

        def normalise(piece):
            fill_normed(x_refs.at[piece], normed, piece * rows)

        each(pieces, normalise)
        keep = pltpu.make_async_copy(normed, normed_out, block_sem.at[1])
        keep.start()
        load.wait()

        def put(part):
            span = pl.ds(pl.multiple_of(part * part_rows, part_rows), part_rows)
            return pltpu.make_async_copy(slopes.at[part], slopes_out.at[:, span], out_sem.at[part])

        def one(part):
            span = pl.ds(pl.multiple_of(part * part_rows, part_rows), part_rows)

            def finish(c, value):
                value, slope = both_of(value)
                hidden[c, span, :] = value.astype(jnp.bfloat16)
                slopes[part, c] = slope.astype(jnp.bfloat16)

            wide_pass(
                normed.at[:, span], blocks_here, own.lists, UP_WIDE, sums, finish, False, 8
            )
            put(part).start()

        each(2, one)
        keep.wait()
        for part in range(2):
            put(part).wait()

    return stage(
        kernel, [], refs + [after, unloaded],
        [
            (pltpu.VMEM, shape_of((FF_BLOCKS, all_rows, BS))),
            (pltpu.HBM, shape_of((FF_BLOCKS, all_rows, BS))),
            (pltpu.HBM, shape_of((width // BS + 1, all_rows, BS))),
        ],
        [
            pltpu.VMEM((pieces, rows, width), jnp.bfloat16),
            pltpu.VMEM((FF_BLOCKS, part_rows, BS), jnp.float32),
            pltpu.VMEM(unloaded.shape[2:], unloaded.dtype),
            pltpu.VMEM((2, FF_BLOCKS, part_rows, BS), jnp.bfloat16),
            pltpu.VMEM((width // BS + 1, all_rows, BS), jnp.bfloat16),
            pltpu.SemaphoreType.DMA((pieces,)),
            pltpu.SemaphoreType.DMA((2,)),
            pltpu.SemaphoreType.DMA((2,)),
        ],
        operands, 4 * COST, ENTER_VMEM
    )


def spread(out, k, value, shares):
    share_rows = BS // shares
    for share in range(shares):
        out[share, k] = value[share * share_rows : (share + 1) * share_rows]


def down_grads_call(refs, choices, hidden, rows, width, shares, total, operands):
    pieces = len(choices)
    all_rows = rows * pieces

    def kernel(layer, info, ins, results, scratch):
        cot_refs, split, turned, sem, out_sem = scratch
        out, split_out = results
        hidden_ref, refs = ins[0], ins[1:]
        own = layer(OWN_LAYER)
        moves = fetch_pieces(info, choices, refs, cot_refs, sem)
        clear_spare(split)
        for piece in range(pieces):
            moves[piece].wait()
            fill_split(cot_refs.at[piece], split, piece * rows)
        keep = pltpu.make_async_copy(split, split_out, out_sem)
        keep.start()
        for b in range(width // BS):
            turned[b] = split[b].T

        def one(k):
            row, col = own_cell(own, 1, k)
            value = dot_plain(turned[col], hidden_ref[row])
            spread(out, k, value.T.astype(jnp.bfloat16), shares)

        each(total, one, 12)
        keep.wait()

    return stage(
        kernel, [hidden], refs,
        [
            (LOCAL, shape_of((shares, total, BS // shares, BS))),
            (pltpu.HBM, shape_of((width // BS + 1, all_rows, BS))),
        ],
        [
            pltpu.VMEM((pieces, rows, width), jnp.bfloat16),
            pltpu.VMEM((width // BS + 1, all_rows, BS), jnp.bfloat16),
            pltpu.VMEM((width // BS, BS, all_rows), jnp.bfloat16),
            pltpu.SemaphoreType.DMA((pieces,)),
            pltpu.SemaphoreType.DMA,
        ],
        operands, 2 * COST
    )


def up_grads_call(split, normed, slopes, width, shares, unloaded, operands):
    all_rows = split.shape[1]
    part_rows = all_rows // 2
    total = unloaded.shape[2]
    blocks = width // BS

    def kernel(layer, info, ins, results, scratch):
        sums, grad_pre, turned, *local, sem = scratch
        normed_ref, split_ref, blocks_here, slopes_ref = local
        out = results[0]
        sources = [ins[0], ins[1], ins[3].at[0, 1], ins[2]]
        moves = [
            pltpu.make_async_copy(source, target, sem.at[i])
            for i, (source, target) in enumerate(zip(sources, local))
        ]
        for move in moves:
            move.start()
        own = layer(OWN_LAYER)
        moves[0].wait()
        for b in range(blocks):
            turned[b] = normed_ref[b].T
        for move in moves[1:]:
            move.wait()

        def part_of(part):
            span = pl.ds(pl.multiple_of(part * part_rows, part_rows), part_rows)

            def finish(c, value):
                slope = slopes_ref[c, span, :].astype(jnp.float32)
                grad_pre[c, span, :] = (value * slope).astype(jnp.bfloat16)

            wide_pass(
                split_ref.at[:, span], blocks_here, own.lists, DOWN_WIDE, sums, finish, True, 4
            )

        each(2, part_of)

        def one(k):
            row, col = own_cell(own, 0, k)
            value = dot_plain(turned[row], grad_pre[col])
            spread(out, k, value.astype(jnp.bfloat16), shares)

        each(total, one, 4)

    return stage(
        kernel, [], [normed, split, slopes, unloaded],
        [(LOCAL, shape_of((shares, total, BS // shares, BS)))],
        [
            pltpu.VMEM((FF_BLOCKS, part_rows, BS), jnp.float32),
            pltpu.VMEM((FF_BLOCKS, all_rows, BS), jnp.bfloat16),
            pltpu.VMEM((blocks, BS, all_rows), jnp.bfloat16),
            pltpu.VMEM(normed.shape, normed.dtype),
            pltpu.VMEM(split.shape, split.dtype),
            pltpu.VMEM(unloaded.shape[2:], unloaded.dtype),
            pltpu.VMEM(slopes.shape, slopes.dtype),
            pltpu.SemaphoreType.DMA((4,)),
        ],
        operands, 4 * COST, OWN_VMEM
    )[0]


def adam_update(grad_sum, master, moment, variance, token_total):
    gradient = grad_sum / token_total
    moment_next = beta_first * moment + (1.0 - beta_first) * gradient
    variance_next = beta_second * variance + (1.0 - beta_second) * gradient * gradient
    corrected = moment_next / (1.0 - beta_first**update_count)
    spread = jnp.sqrt(variance_next / (1.0 - beta_second**update_count))
    step_direction = corrected / (spread + adam_eps)
    return (step_direction, master - learn_rate * (step_direction + decay_rate * master))


def shards(tokens, targets, weights, pattern, master, moment, variance):
    section = lax.axis_index("section")
    sections = lax.axis_size("section")
    shares = lax.axis_size("dp")
    groups = sections // 2
    micro, rows_each, width = tokens.shape[1:]
    rows = micro * rows_each
    half = rows // 2
    high = section >= groups
    high_member = high.astype(jnp.int32)
    group = jnp.minimum(section, sections - 1 - section)
    info = jnp.stack([high_member, 1 - high_member, jnp.zeros_like(high_member), high_member, group])
    far = lambda array: pltpu.with_memory_space_constraint(array, pltpu.HBM)
    tokens = far(tokens.reshape(2, rows, width))
    targets = far(targets.reshape(2, rows, width))
    pattern = pattern[0]
    lists = block_lists(pattern, width)
    mirror = lambda i: sections - 1 - i

    def lane(i, h):
        other = mirror(i + 1) if h else i + 1
        return [(i, other), (mirror(i), mirror(other))]

    def inward(x, i, h):
        return lax.ppermute(x, "section", lane(i, h))

    def outward(x, i, h):
        return lax.ppermute(x, "section", [(b, a) for a, b in lane(i, h)])

    def at_half(records, h, start=0):
        value = records[start][h]
        for i in range(start + 1, groups):
            value = jnp.where(group == i, records[i][h], value)
        return value

    def swap(low_records, high_records, h, sent):
        if sent is None:
            sent = jnp.where(high, at_half(low_records, h, 1), at_half(high_records, h))
        pairs = [(i, mirror(i)) for i in range(groups)] + [(mirror(i), i) for i in range(1, groups)]
        return lax.ppermute(sent, "section", pairs)

    halves = range(2)
    x_low, x_high, cot_low, cot_high = [[None] * groups for _ in range(4)]
    unloaded = far(weights[0])
    slope_low, slope_high = [[None] * groups for _ in range(2)]
    current = [enter_call(tokens, h, half, unloaded, (info, lists, None))[0] for h in halves]
    operands = (info, lists, weights[0])
    for i in range(groups - 1):
        current = [inward(current[h], i, h) for h in halves]
        x_low[i + 1] = current
        if i + 1 < groups - 1:
            moved = [forward_call(current[h], [LOW_LAYER], operands) for h in halves]
            current = [m[0] for m in moved]
            slope_low[i + 1] = [(far(m[1]), 0) for m in moved]
    both = [forward_call(current[h], [LOW_LAYER, HIGH_LAYER], operands) for h in halves]
    x_high[groups - 1] = [b[0] for b in both]
    slope_low[groups - 1] = [(far(b[2]), 0) for b in both]
    slope_high[groups - 1] = [(far(b[2]), 1) for b in both]
    current = [b[1] for b in both]
    for i in reversed(range(groups - 1)):
        current = [outward(current[h], i, h) for h in halves]
        x_high[i] = current
        if i > 0:
            moved = [forward_call(current[h], [HIGH_LAYER], operands) for h in halves]
            current = [m[0] for m in moved]
            slope_high[i] = [(far(m[1]), 0) for m in moved]
    mirrored = groups == 2
    entries = [x_high[0], x_high[1], x_low[1]] if mirrored else None
    turned = [turn_call(current[h], targets, h, operands, entries if h == 1 else None) for h in halves]
    cot_high[0] = [t[0] for t in turned]
    current = [t[1] for t in turned]
    for i in range(groups - 1):
        current = [inward(current[h], i, h) for h in halves]
        cot_high[i + 1] = current
        if i + 1 < groups - 1:
            current = [
                backward_call(
                    [x_high[i + 1][h]], [slope_high[i + 1][h]], current[h], [HIGH_LAYER], operands
                )[0]
                for h in halves
            ]
    last = groups - 1
    cot_sent = [None, None]
    cot_low[last], current, entering = [None, None], [None, None], current
    for h in halves:
        top, bottom = (x_high[last][h], x_low[last][h])
        tops, bottoms = slope_high[last][h], slope_low[last][h]
        sending = dict(turned=cot_high[0][h], last=last) if mirrored else {}
        if h == 0:
            moved = backward_call(
                [top, bottom], [tops, bottoms], entering[h], [HIGH_LAYER, LOW_LAYER], operands, **sending
            )
            cot_low[last][h], current[h], *sent = moved
        else:
            cot_low[last][h], *sent = backward_call(
                [top], [tops], entering[h], [HIGH_LAYER], operands, **sending
            )
            (current[h],) = backward_call(
                [bottom], [bottoms], cot_low[last][h], [LOW_LAYER], operands
            )
        cot_sent[h] = sent[0] if mirrored else None
    for i in reversed(range(1, last)):
        current = [outward(current[h], i, h) for h in halves]
        cot_low[i] = current
        current = [
            backward_call([x_low[i][h]], [slope_low[i][h]], current[h], [LOW_LAYER], operands)[0]
            for h in halves
        ]
    from_low = [lax.ppermute(current[h], "section", [(1, 0)]) for h in halves]
    from_high = [lax.ppermute(current[h], "section", [(mirror(1), 0)]) for h in halves]
    if mirrored:
        x_swapped = swap(None, None, None, turned[1][2])
        x_other = [(x_swapped, pl.ds(h * half, half)) for h in halves]
    else:
        x_other = [(swap(x_low, x_high, h, None), None) for h in halves]
    cot_other = []
    for h in halves:
        cot_other.append((swap(cot_low, cot_high, h, cot_sent[h]), None))

    def choose(low_records, high_records, others, first_own, first_other):
        refs, choices = [], []

        def add(array):
            refs.append(array)
            return len(refs) - 1

        for h in halves:
            array, index = first_own[h]
            options = [("first", None, add(array), index)]
            for i in range(groups):
                if i > 0:
                    options.append(("own", (0, i), add(low_records[i][h]), None))
                options.append(("own", (1, i), add(high_records[i][h]), None))
            choices.append(options)
        for h in halves:
            array, index = first_other[h]
            choices.append([("first", None, add(array), index), ("rest", None, add(others[h][0]), others[h][1])])
        return refs, choices

    def token_piece(member, h):
        return (tokens, (member, pl.ds(h * half, half)))

    refs, choices = choose(
        x_low, x_high, x_other, [token_piece(0, h) for h in halves], [token_piece(1, h) for h in halves]
    )
    hidden, slopes, normed = ups_call(refs, choices, current[1], half, width, unloaded, (info, lists, None))
    refs, choices = choose(
        cot_low, cot_high, cot_other,
        [(from_low[0], None), (from_high[1], None)], [(from_high[0], None), (from_low[1], None)]
    )
    downs, split = down_grads_call(
        refs, choices, hidden, half, width, shares, unloaded.shape[2], (info, lists, None)
    )

    def reduce(grads):
        return lax.psum_scatter(grads, "dp", scatter_dimension=0, tiled=True)[0].astype(jnp.float32)

    down_share = reduce(downs)
    up_share = reduce(up_grads_call(far(split), far(normed), far(slopes), width, shares, unloaded, (info, lists, None)))
    token_total = 2 * rows * shares
    step_direction, master_next = adam_update(
        jnp.stack([down_share, up_share])[::-1], master[0], moment[0], variance[0], token_total
    )
    return (step_direction[None], master_next[None])


def solution(mesh):
    rows_split = P(None, None, "dp", None)
    by_section = P("section", None, None, "dp", None)
    return jax.shard_map(
        shards,
        mesh=mesh,
        in_specs=(
            rows_split,
            rows_split,
            P("section", None, None, None, None, None),
            P("section", None, None, None, None),
            by_section,
            by_section,
            by_section,
        ),
        out_specs=(by_section, by_section),
        check_vma=False,
    )
```

```python
import jax
import jax.numpy as jnp
from jax import lax
from jax.experimental import pallas as pl
from jax.experimental.pallas import tpu as pltpu
from jax.sharding import PartitionSpec as P


BS = 128
FF_BLOCKS = 8192 // BS
norm_eps = 1e-06
gelu_coef = 0.7978845608028654
gelu_cubic = gelu_coef * 0.044715
beta_first = 0.9
beta_second = 0.95
adam_eps = 1e-08
learn_rate = 0.001
decay_rate = 0.1
update_count = 10
ROW_TILE = 16
EXTRA_BATCH = 4
CHAIN_VMEM = 24 * 1024 * 1024
ENTER_VMEM = 32 * 1024 * 1024
OWN_VMEM = 40 * 1024 * 1024
COST = 4_000_000_000
LOCAL = None
ENTER_COST = 1
LOW_LAYER, HIGH_LAYER, OWN_LAYER, HIGH, GROUP = range(5)
UP_WIDE, DOWN_WIDE, DOWN_NARROW, UP_NARROW = range(4)
FIELDS = 9
FIRST, FIRST_TAKE, SECOND, SECOND_TAKE, PUT, EXTRA, EXTRA_TAKE, EXTRA_PUT, COUNT = range(FIELDS)


def block_lists(pattern, width):
    total = pattern.shape[2]
    up_row, up_col = pattern[:, 0, :, 0], pattern[:, 0, :, 1]
    down_row, down_col = pattern[:, 1, :, 0], pattern[:, 1, :, 1]
    key = jnp.stack([up_col, down_row, down_col, up_row], 1)
    take = jnp.stack([up_row, down_col, down_row, up_col], 1)
    order = jnp.arange(total, dtype=jnp.int32)
    before = order[None, :] < order[:, None]

    def count(mask):
        return jnp.sum(mask.astype(jnp.int32), axis=-1)

    same = key[..., None, :] == key[..., :, None]
    rank = count(same & before)
    even = rank % 2 == 0
    wide = (jnp.arange(4) < 2)[None, :, None]
    extra = rank >= 2
    extra_place = count(extra[..., None, :] & before)
    pair = count((key[..., None, :] < key[..., :, None]) & even[..., None, :]) + rank // 2
    place_first = jnp.where(wide, jnp.where(rank == 0, key, -1), jnp.where(even, pair, -1))
    place_second = jnp.where(wide, jnp.where(rank == 1, key, -1), jnp.where(even, -1, pair))
    place_extra = jnp.where(wide & extra, extra_place, -1)
    number = jnp.broadcast_to(order, key.shape)
    places = jnp.stack(
        [place_first] * 2 + [place_second] * 2 + [place_first] + [place_extra] * 3, 2
    )
    absent = jnp.where(wide, width // BS, FF_BLOCKS)
    lowered = take - absent
    values = jnp.stack([number, lowered, number, lowered, key, number, lowered, key], 2)
    hit = places[..., None, :] == order[:, None]
    fields = jnp.sum(jnp.where(hit, values[..., None, :], 0), axis=-1)
    slot = jnp.arange(8)
    taken = (slot == FIRST_TAKE) | (slot == SECOND_TAKE) | (slot == EXTRA_TAKE)
    fields = fields + jnp.where(taken[:, None], absent[..., None], 0)
    counts = jnp.where(wide[..., 0], count(extra), count(even))
    counts = jnp.broadcast_to(counts[..., None, None], key.shape[:2] + (1, total))
    lists = jnp.concatenate([fields, counts], axis=2).astype(jnp.int32)
    return jnp.concatenate([lists.reshape(-1), pattern[0].reshape(-1)])


class Lists:
    def __init__(self, ref, copy, total):
        self.ref, self.total = ref, total
        self.base = copy * (4 * FIELDS * total)
        self.cells = 2 * 4 * FIELDS * total

    def __call__(self, kind, field, index):
        return self.ref[self.base + ((kind * FIELDS + field) * self.total) + index]


def hidden_of(preact):
    inner = preact * (gelu_coef + gelu_cubic * (preact * preact))
    half = 0.5 * preact
    return half + half * jnp.tanh(inner)


def both_of(preact):
    cubic = gelu_cubic * (preact * preact)
    tangent = jnp.tanh(preact * (gelu_coef + cubic))
    bend = preact * (gelu_coef + 3.0 * cubic)
    half = 0.5 + 0.5 * tangent
    return (preact * half, half * (1.0 + bend * (1.0 - tangent)))


def dot_plain(left, right):
    return jnp.dot(left, right, preferred_element_type=jnp.float32)


def dot_right_t(left, right):
    return lax.dot_general(left, right, (((1,), (1,)), ((), ())), preferred_element_type=jnp.float32)


def each(count, body, unroll=1):
    def one(i, carry):
        body(i)
        return carry

    lax.fori_loop(0, count, one, 0, unroll=unroll)


def fill_normed(x_ref, normed, base):
    rows, width = x_ref.shape

    def tile(i):
        at = pl.multiple_of(i * ROW_TILE, ROW_TILE)
        wide = x_ref[pl.ds(at, ROW_TILE), :].astype(jnp.float32)
        factor = lax.rsqrt(jnp.mean(wide * wide, axis=-1, keepdims=True) + norm_eps)
        value = (wide * factor).astype(jnp.bfloat16)
        for b in range(width // BS):
            normed[b, pl.ds(base + at, ROW_TILE), :] = value[:, b * BS : (b + 1) * BS]

    each(rows // ROW_TILE, tile, 7)


def fill_split(x_ref, split, base):
    rows, width = x_ref.shape
    for b in range(width // BS):
        split[b, pl.ds(base, rows), :] = x_ref[:, b * BS : (b + 1) * BS]


def pair_product(source, blocks, lists, kind, p, transposed):
    left = jnp.concatenate(
        [source[lists(kind, FIRST_TAKE, p)], source[lists(kind, SECOND_TAKE, p)]], axis=1
    )
    one, two = blocks[lists(kind, FIRST, p)], blocks[lists(kind, SECOND, p)]
    if transposed:
        return dot_right_t(left, jnp.concatenate([one, two], axis=1))
    return dot_plain(left, jnp.concatenate([one, two], axis=0))


def wide_pass(source, blocks, lists, kind, sums, finish, transposed, batch=16, ahead=None):
    def main(i):
        if ahead is not None:
            ahead(i)
        for j in range(batch):
            c = i * batch + j
            value = pair_product(source, blocks, lists, kind, c, transposed)
            sums[c] = value
            finish(c, value)

    each(sums.shape[0] // batch, main)
    dot = dot_right_t if transposed else dot_plain

    def more(e):
        c = lists(kind, EXTRA_PUT, e)
        left = source[lists(kind, EXTRA_TAKE, e)]
        value = sums[c] + dot(left, blocks[lists(kind, EXTRA, e)])
        sums[c] = value
        finish(c, value)

    def batch(i):
        for j in range(EXTRA_BATCH):
            more(i * EXTRA_BATCH + j)

    each((lists(kind, COUNT, 0) + EXTRA_BATCH - 1) // EXTRA_BATCH, batch)


def narrow_pass(source, blocks, lists, kind, sums, transposed):
    sums[...] = jnp.zeros(sums.shape, sums.dtype)

    def one(p):
        sums[lists(kind, PUT, p)] += pair_product(source, blocks, lists, kind, p, transposed)

    each((lists.total + sums.shape[0]) // 2, one, 14)


def forward_rows(x_ref, out_ref, layer, scratch, slopes=None, before=lambda part: None, done=lambda: None):
    normed, sums, hidden, narrow = scratch
    _, width = x_ref.shape
    fill_normed(x_ref, normed, 0)

    def finish(c, value):
        if slopes is None:
            hidden[c] = hidden_of(value).astype(jnp.bfloat16)
        else:
            value, slope = both_of(value)
            hidden[c] = value.astype(jnp.bfloat16)
            slopes[c] = slope.astype(slopes.dtype)

    before(0)
    wide_pass(normed, layer.up, layer.lists, UP_WIDE, sums, finish, False)
    before(1)
    done()
    narrow_pass(hidden, layer.down, layer.lists, DOWN_NARROW, narrow, False)
    for b in range(width // BS):
        cols = slice(b * BS, (b + 1) * BS)
        out_ref[:, cols] = (x_ref[:, cols].astype(jnp.float32) + narrow[b]).astype(jnp.bfloat16)


def backward_rows(x_ref, cot_ref, out_ref, layer, scratch, slopes, ready=lambda: None):
    normed, sums, hidden, narrow = scratch
    rows, width = x_ref.shape
    fill_split(cot_ref, normed, 0)
    ready()

    def finish(c, value):
        hidden[c] = (value * slopes[c].astype(jnp.float32)).astype(jnp.bfloat16)

    wide_pass(normed, layer.down, layer.lists, DOWN_WIDE, sums, finish, True)
    narrow_pass(hidden, layer.up, layer.lists, UP_NARROW, narrow, True)

    def tile(i):
        at = pl.multiple_of(i * ROW_TILE, ROW_TILE)
        wide = x_ref[pl.ds(at, ROW_TILE), :].astype(jnp.float32)
        factor = lax.rsqrt(jnp.mean(wide * wide, axis=-1, keepdims=True) + norm_eps)
        grad = jnp.concatenate(
            [narrow[b, pl.ds(at, ROW_TILE), :] for b in range(width // BS)], axis=-1
        )
        coupling = jnp.mean(wide * grad, axis=-1, keepdims=True)
        upstream = cot_ref[pl.ds(at, ROW_TILE), :].astype(jnp.float32)
        value = upstream + factor * grad - wide * (factor * factor * factor * coupling)
        out_ref[pl.ds(at, ROW_TILE), :] = value.astype(jnp.bfloat16)

    each(rows // ROW_TILE, tile)


def own_cell(layer, part, k):
    lists = layer.lists
    at = lists.cells + 2 * (part * lists.total + k)
    return lists.ref[at], lists.ref[at + 1]


class Layer:
    def __init__(self, info, lists_ref, weights_ref, which, local=None):
        copy = info[which]
        self.lists = Lists(lists_ref, copy, lists_ref.shape[0] // (2 * 4 * FIELDS + 4))
        if weights_ref is not None:
            local = weights_ref.at[copy]
        if local is not None:
            self.up, self.down = local.at[0], local.at[1]


def stage(kernel, local_in, remote_in, outs, scratch, operands, cost, vmem=CHAIN_VMEM):
    info, lists, weights = operands
    held = [] if weights is None else [pltpu.with_memory_space_constraint(weights, pltpu.VMEM)]
    any_spec = pl.BlockSpec(memory_space=pltpu.HBM)
    smem_spec = pl.BlockSpec(memory_space=pltpu.SMEM)
    vmem_spec = pl.BlockSpec(memory_space=pltpu.VMEM)
    in_total = len(local_in) + len(remote_in)
    local_in = [pltpu.with_memory_space_constraint(array, pltpu.VMEM) for array in local_in]

    def body(info_ref, lists_ref, *rest):
        weights_ref, rest = (None, rest) if weights is None else (rest[0], rest[1:])
        ins, own = rest[:in_total], rest[in_total + len(outs) :]
        results = rest[in_total : in_total + len(outs)]

        def layer(which, weights_ref=weights_ref, local=None):
            return Layer(info_ref, lists_ref, weights_ref, which, local)

        kernel(layer, info_ref, ins, results, own)

    return pl.pallas_call(
        body,
        in_specs=[smem_spec, smem_spec]
        + [vmem_spec] * (len(held) + len(local_in))
        + [any_spec] * len(remote_in),
        out_specs=[any_spec if space is pltpu.HBM else vmem_spec for space, _ in outs],
        out_shape=[
            shape if space is LOCAL else space(shape.shape, shape.dtype) for space, shape in outs
        ],
        scratch_shapes=scratch,
        cost_estimate=pl.CostEstimate(flops=cost, transcendentals=0, bytes_accessed=0),
        compiler_params=pltpu.CompilerParams(vmem_limit_bytes=vmem),
    )(info, lists, *held, *local_in, *remote_in)


def layer_scratch(rows, width):
    return [
        pltpu.VMEM((width // BS + 1, rows, BS), jnp.bfloat16),
        pltpu.VMEM((FF_BLOCKS, rows, BS), jnp.float32),
        pltpu.VMEM((FF_BLOCKS + 1, rows, BS), jnp.bfloat16),
        pltpu.VMEM((width // BS, rows, BS), jnp.float32),
    ]


def slope_scratch(rows):
    return [pltpu.VMEM((FF_BLOCKS, rows, BS), jnp.float32)]


def shape_of(shape, dtype=jnp.bfloat16):
    return jax.ShapeDtypeStruct(shape, dtype)


def clear_spare(*refs):
    for ref in refs:
        ref[ref.shape[0] - 1] = jnp.zeros(ref.shape[1:], ref.dtype)


def forward_call(x, whichs, operands):
    rows, width = x.shape
    steps = len(whichs)
    slope_shape = (steps, FF_BLOCKS, rows, BS)

    def kernel(layer, info, ins, results, scratch):
        *layer_refs, slopes, sem = scratch
        clear_spare(layer_refs[0], layer_refs[2])
        moves = [
            pltpu.make_async_copy(slopes.at[i], results[-1].at[i], sem.at[i]) for i in range(steps)
        ]
        source = ins[0]
        for i, which in enumerate(whichs):
            forward_rows(
                source, results[i], layer(which), layer_refs, slopes.at[i], done=moves[i].start
            )
            source = results[i]
        for move in moves:
            move.wait()

    outs = [(LOCAL, shape_of(x.shape))] * steps + [(pltpu.HBM, shape_of(slope_shape))]
    scratch = [pltpu.VMEM(slope_shape, jnp.bfloat16), pltpu.SemaphoreType.DMA((steps,))]
    return stage(
        kernel, [x], [], outs, layer_scratch(rows, width) + scratch, operands, COST * steps
    )


def enter_call(tokens, h, rows, unloaded, operands):
    width = tokens.shape[-1]

    def kernel(layer, info, ins, results, scratch):
        *layer_refs, x_ref, local, sem, weight_sem = scratch
        load = pltpu.make_async_copy(ins[0].at[info[HIGH], pl.ds(h * rows, rows)], x_ref, sem)
        load.start()
        low = info[LOW_LAYER]
        moves = [
            pltpu.make_async_copy(ins[1].at[low, part], local.at[part], weight_sem.at[part])
            for part in range(2)
        ]

        def before(part):
            moves[part].wait()
            if part == 0:
                moves[1].start()

        moves[0].start()
        clear_spare(layer_refs[0], layer_refs[2])
        load.wait()
        forward_rows(x_ref, results[0], layer(LOW_LAYER, None, local), layer_refs, before=before)

    outs = [(LOCAL, shape_of((rows, width)))]
    scratch = layer_scratch(rows, width) + [
        pltpu.VMEM((rows, width), jnp.bfloat16),
        pltpu.VMEM(unloaded.shape[1:], unloaded.dtype),
        pltpu.SemaphoreType.DMA,
        pltpu.SemaphoreType.DMA((2,)),
    ]
    return stage(kernel, [], [tokens, unloaded], outs, scratch, operands, COST * ENTER_COST, CHAIN_VMEM)


def turn_call(x, targets, h, operands):
    rows, width = x.shape

    def kernel(layer, info, ins, results, scratch):
        *layer_refs, slopes, aim, sem = scratch
        x_ref, target_ref = ins[0], ins[-1]
        residue, out = results[:2]
        load = pltpu.make_async_copy(target_ref.at[info[HIGH], pl.ds(h * rows, rows)], aim, sem)
        load.start()
        clear_spare(layer_refs[0], layer_refs[2])
        own = layer(HIGH_LAYER)
        forward_rows(x_ref, residue, own, layer_refs, slopes)
        load.wait()
        for b in range(width // BS):
            cols = slice(b * BS, (b + 1) * BS)
            difference = residue[:, cols].astype(jnp.float32) - aim[:, cols].astype(jnp.float32)
            residue[:, cols] = difference.astype(jnp.bfloat16)
        backward_rows(x_ref, residue, out, own, layer_refs, slopes)

    return stage(
        kernel, [x], [targets], [(LOCAL, shape_of(x.shape))] * 2,
        layer_scratch(rows, width) + slope_scratch(rows)
        + [pltpu.VMEM((rows, width), jnp.bfloat16), pltpu.SemaphoreType.DMA],
        operands, 3 * COST
    )


def pick_rows(target, options):
    for condition, source in options:

        @pl.when(condition)
        def take(source=source):
            target[...] = source[...]


def backward_call(xs, saved, cot, whichs, operands, turned=None, last=None, entries=()):
    rows, width = cot.shape
    steps = len(whichs)
    local = list(xs) + [cot] + ([] if turned is None else [turned]) + list(entries)

    def kernel(layer, info, ins, results, scratch):
        *layer_refs, slopes, sem = scratch
        moves = [
            pltpu.make_async_copy(ins[len(local) + i].at[saved[i][1]], slopes.at[i], sem.at[i])
            for i in range(steps)
        ]
        for move in moves:
            move.start()
        clear_spare(layer_refs[0], layer_refs[2])
        upstream = ins[steps]
        for i, which in enumerate(whichs):
            backward_rows(
                ins[i], upstream, results[i], layer(which), layer_refs, slopes.at[i], moves[i].wait
            )
            upstream = results[i]
        if turned is not None:
            high, group = info[HIGH] == 1, info[GROUP]
            pick_rows(
                results[steps],
                [
                    (high, results[0]),
                    (~high & (group == last), ins[steps]),
                    (~high & (group != last), ins[steps + 1]),
                ],
            )
        if entries:
            conditions = [~high & (group != last), ~high & (group == last), high]
            pick_rows(results[steps + 1], list(zip(conditions, ins[steps + 2 :])))

    scratch = [
        pltpu.VMEM((steps, FF_BLOCKS, rows, BS), jnp.bfloat16),
        pltpu.SemaphoreType.DMA((steps,)),
    ]
    outs = [(LOCAL, shape_of(cot.shape))] * (steps + (turned is not None) + bool(entries))
    return stage(
        kernel, local, [array for array, _ in saved], outs, layer_scratch(rows, width) + scratch,
        operands, 2 * COST * steps
    )


def fetch_pieces(info, choices, refs, local, sem):
    first = (info[HIGH] == 0) & (info[GROUP] == 0)
    moves = []
    for piece, options in enumerate(choices):
        for kind, wanted, number, index in options:
            source = refs[number] if index is None else refs[number].at[index]
            move = pltpu.make_async_copy(source, local.at[piece], sem.at[piece])
            if kind == "first":
                condition = first
            elif kind == "own":
                condition = (info[HIGH] == wanted[0]) & (info[GROUP] == wanted[1]) & ~first
            else:
                condition = ~first

            @pl.when(condition)
            def go(move=move):
                move.start()

        moves.append(move)
    return moves


def ups_call(refs, choices, after, rows, width, unloaded, operands):
    pieces = len(choices)
    all_rows = rows * pieces
    part_rows = all_rows // 2

    def kernel(layer, info, ins, results, scratch):
        x_refs, sums, blocks_here, slopes, normed, sem, block_sem, out_sem = scratch
        hidden, slopes_out, normed_out = results
        load = pltpu.make_async_copy(ins[-1].at[0, 0], blocks_here, block_sem.at[0])
        load.start()
        moves = fetch_pieces(info, choices, ins, x_refs, sem)
        own = layer(OWN_LAYER)
        clear_spare(normed)
        for move in moves:
            move.wait()

        def normalise(piece):
            fill_normed(x_refs.at[piece], normed, piece * rows)

        each(pieces, normalise)
        keep = pltpu.make_async_copy(normed, normed_out, block_sem.at[1])
        keep.start()
        load.wait()

        def put(part):
            span = pl.ds(pl.multiple_of(part * part_rows, part_rows), part_rows)
            return pltpu.make_async_copy(slopes.at[part], slopes_out.at[:, span], out_sem.at[part])

        def one(part):
            span = pl.ds(pl.multiple_of(part * part_rows, part_rows), part_rows)

            def finish(c, value):
                value, slope = both_of(value)
                hidden[c, span, :] = value.astype(jnp.bfloat16)
                slopes[part, c] = slope.astype(jnp.bfloat16)

            wide_pass(
                normed.at[:, span], blocks_here, own.lists, UP_WIDE, sums, finish, False, 8
            )
            put(part).start()

        each(2, one)
        keep.wait()
        for part in range(2):
            put(part).wait()

    return stage(
        kernel, [], refs + [after, unloaded],
        [
            (pltpu.VMEM, shape_of((FF_BLOCKS, all_rows, BS))),
            (pltpu.HBM, shape_of((FF_BLOCKS, all_rows, BS))),
            (pltpu.HBM, shape_of((width // BS + 1, all_rows, BS))),
        ],
        [
            pltpu.VMEM((pieces, rows, width), jnp.bfloat16),
            pltpu.VMEM((FF_BLOCKS, part_rows, BS), jnp.float32),
            pltpu.VMEM(unloaded.shape[2:], unloaded.dtype),
            pltpu.VMEM((2, FF_BLOCKS, part_rows, BS), jnp.bfloat16),
            pltpu.VMEM((width // BS + 1, all_rows, BS), jnp.bfloat16),
            pltpu.SemaphoreType.DMA((pieces,)),
            pltpu.SemaphoreType.DMA((2,)),
            pltpu.SemaphoreType.DMA((2,)),
        ],
        operands, 4 * COST, ENTER_VMEM
    )


def spread(out, k, value, shares):
    share_rows = BS // shares
    for share in range(shares):
        out[share, k] = value[share * share_rows : (share + 1) * share_rows]


def down_grads_call(refs, choices, hidden, rows, width, shares, total, operands):
    pieces = len(choices)
    all_rows = rows * pieces

    def kernel(layer, info, ins, results, scratch):
        cot_refs, split, turned, sem, out_sem = scratch
        out, split_out = results
        hidden_ref, refs = ins[0], ins[1:]
        own = layer(OWN_LAYER)
        moves = fetch_pieces(info, choices, refs, cot_refs, sem)
        clear_spare(split)
        for piece in range(pieces):
            moves[piece].wait()
            fill_split(cot_refs.at[piece], split, piece * rows)
        keep = pltpu.make_async_copy(split, split_out, out_sem)
        keep.start()
        for b in range(width // BS):
            turned[b] = split[b].T

        def one(k):
            row, col = own_cell(own, 1, k)
            value = dot_plain(turned[col], hidden_ref[row])
            spread(out, k, value.T.astype(jnp.bfloat16), shares)

        each(total, one, 12)
        keep.wait()

    return stage(
        kernel, [hidden], refs,
        [
            (LOCAL, shape_of((shares, total, BS // shares, BS))),
            (pltpu.HBM, shape_of((width // BS + 1, all_rows, BS))),
        ],
        [
            pltpu.VMEM((pieces, rows, width), jnp.bfloat16),
            pltpu.VMEM((width // BS + 1, all_rows, BS), jnp.bfloat16),
            pltpu.VMEM((width // BS, BS, all_rows), jnp.bfloat16),
            pltpu.SemaphoreType.DMA((pieces,)),
            pltpu.SemaphoreType.DMA,
        ],
        operands, 2 * COST
    )


def up_grads_call(split, normed, slopes, width, shares, unloaded, operands):
    all_rows = split.shape[1]
    part_rows = all_rows // 2
    total = unloaded.shape[2]
    blocks = width // BS

    def kernel(layer, info, ins, results, scratch):
        sums, grad_pre, turned, *local, sem = scratch
        normed_ref, split_ref, blocks_here, slopes_ref = local
        out = results[0]
        sources = [ins[0], ins[1], ins[3].at[0, 1], ins[2]]
        moves = [
            pltpu.make_async_copy(source, target, sem.at[i])
            for i, (source, target) in enumerate(zip(sources, local))
        ]
        for move in moves:
            move.start()
        own = layer(OWN_LAYER)
        moves[0].wait()
        for b in range(blocks):
            turned[b] = normed_ref[b].T
        for move in moves[1:]:
            move.wait()

        def part_of(part):
            span = pl.ds(pl.multiple_of(part * part_rows, part_rows), part_rows)

            def finish(c, value):
                slope = slopes_ref[c, span, :].astype(jnp.float32)
                grad_pre[c, span, :] = (value * slope).astype(jnp.bfloat16)

            wide_pass(
                split_ref.at[:, span], blocks_here, own.lists, DOWN_WIDE, sums, finish, True, 4
            )

        each(2, part_of)

        def one(k):
            row, col = own_cell(own, 0, k)
            value = dot_plain(turned[row], grad_pre[col])
            spread(out, k, value.astype(jnp.bfloat16), shares)

        each(total, one, 4)

    return stage(
        kernel, [], [normed, split, slopes, unloaded],
        [(LOCAL, shape_of((shares, total, BS // shares, BS)))],
        [
            pltpu.VMEM((FF_BLOCKS, part_rows, BS), jnp.float32),
            pltpu.VMEM((FF_BLOCKS, all_rows, BS), jnp.bfloat16),
            pltpu.VMEM((blocks, BS, all_rows), jnp.bfloat16),
            pltpu.VMEM(normed.shape, normed.dtype),
            pltpu.VMEM(split.shape, split.dtype),
            pltpu.VMEM(unloaded.shape[2:], unloaded.dtype),
            pltpu.VMEM(slopes.shape, slopes.dtype),
            pltpu.SemaphoreType.DMA((4,)),
        ],
        operands, 4 * COST, OWN_VMEM
    )[0]


def adam_update(grad_sum, master, moment, variance, token_total):
    gradient = grad_sum / token_total
    moment_next = beta_first * moment + (1.0 - beta_first) * gradient
    variance_next = beta_second * variance + (1.0 - beta_second) * gradient * gradient
    corrected = moment_next / (1.0 - beta_first**update_count)
    spread = jnp.sqrt(variance_next / (1.0 - beta_second**update_count))
    step_direction = corrected / (spread + adam_eps)
    return (step_direction, master - learn_rate * (step_direction + decay_rate * master))


def shards(tokens, targets, weights, pattern, master, moment, variance):
    section = lax.axis_index("section")
    sections = lax.axis_size("section")
    shares = lax.axis_size("dp")
    groups = sections // 2
    micro, rows_each, width = tokens.shape[1:]
    rows = micro * rows_each
    half = rows // 2
    high = section >= groups
    high_member = high.astype(jnp.int32)
    group = jnp.minimum(section, sections - 1 - section)
    info = jnp.stack([high_member, 1 - high_member, jnp.zeros_like(high_member), high_member, group])
    far = lambda array: pltpu.with_memory_space_constraint(array, pltpu.HBM)
    tokens = far(tokens.reshape(2, rows, width))
    targets = far(targets.reshape(2, rows, width))
    pattern = pattern[0]
    lists = block_lists(pattern, width)
    mirror = lambda i: sections - 1 - i

    def lane(i, h):
        other = mirror(i + 1) if h else i + 1
        return [(i, other), (mirror(i), mirror(other))]

    def inward(x, i, h):
        return lax.ppermute(x, "section", lane(i, h))

    def outward(x, i, h):
        return lax.ppermute(x, "section", [(b, a) for a, b in lane(i, h)])

    def at_half(records, h, start=0):
        value = records[start][h]
        for i in range(start + 1, groups):
            value = jnp.where(group == i, records[i][h], value)
        return value

    def swap(low_records, high_records, h, sent):
        if sent is None:
            sent = jnp.where(high, at_half(low_records, h, 1), at_half(high_records, h))
        pairs = [(i, mirror(i)) for i in range(groups)] + [(mirror(i), i) for i in range(1, groups)]
        return lax.ppermute(sent, "section", pairs)

    halves = range(2)
    x_low, x_high, cot_low, cot_high = [[None] * groups for _ in range(4)]
    unloaded = far(weights[0])
    slope_low, slope_high = [[None] * groups for _ in range(2)]
    current = [enter_call(tokens, h, half, unloaded, (info, lists, None))[0] for h in halves]
    operands = (info, lists, weights[0])
    for i in range(groups - 1):
        current = [inward(current[h], i, h) for h in halves]
        x_low[i + 1] = current
        if i + 1 < groups - 1:
            moved = [forward_call(current[h], [LOW_LAYER], operands) for h in halves]
            current = [m[0] for m in moved]
            slope_low[i + 1] = [(far(m[1]), 0) for m in moved]
    both = [forward_call(current[h], [LOW_LAYER, HIGH_LAYER], operands) for h in halves]
    x_high[groups - 1] = [b[0] for b in both]
    slope_low[groups - 1] = [(far(b[2]), 0) for b in both]
    slope_high[groups - 1] = [(far(b[2]), 1) for b in both]
    current = [b[1] for b in both]
    for i in reversed(range(groups - 1)):
        current = [outward(current[h], i, h) for h in halves]
        x_high[i] = current
        if i > 0:
            moved = [forward_call(current[h], [HIGH_LAYER], operands) for h in halves]
            current = [m[0] for m in moved]
            slope_high[i] = [(far(m[1]), 0) for m in moved]
    mirrored = groups == 2
    turned = []
    for h in halves:
        turned.append(turn_call(current[h], targets, h, operands))
    cot_high[0] = [t[0] for t in turned]
    current = [t[1] for t in turned]
    for i in range(groups - 1):
        current = [inward(current[h], i, h) for h in halves]
        cot_high[i + 1] = current
        if i + 1 < groups - 1:
            current = [
                backward_call(
                    [x_high[i + 1][h]], [slope_high[i + 1][h]], current[h], [HIGH_LAYER], operands
                )[0]
                for h in halves
            ]
    last = groups - 1
    cot_sent = [None, None]
    cot_low[last], current, entering = [None, None], [None, None], current
    for h in halves:
        top, bottom = (x_high[last][h], x_low[last][h])
        tops, bottoms = slope_high[last][h], slope_low[last][h]
        sending = dict(turned=cot_high[0][h], last=last) if mirrored else {}
        if h == 0:
            if mirrored:
                sending["entries"] = [x_high[0][1], x_high[1][1], x_low[1][1]]
            moved = backward_call(
                [top, bottom], [tops, bottoms], entering[h], [HIGH_LAYER, LOW_LAYER], operands, **sending
            )
            cot_low[last][h], current[h], *sent = moved
            x_sent = sent[1] if mirrored else None
        else:
            cot_low[last][h], *sent = backward_call(
                [top], [tops], entering[h], [HIGH_LAYER], operands, **sending
            )
            (current[h],) = backward_call(
                [bottom], [bottoms], cot_low[last][h], [LOW_LAYER], operands
            )
        cot_sent[h] = sent[0] if mirrored else None
    for i in reversed(range(1, last)):
        current = [outward(current[h], i, h) for h in halves]
        cot_low[i] = current
        current = [
            backward_call([x_low[i][h]], [slope_low[i][h]], current[h], [LOW_LAYER], operands)[0]
            for h in halves
        ]
    from_low, from_high = [], []
    for h in halves:
        from_low.append(lax.ppermute(current[h], "section", [(1, 0)]))
        from_high.append(lax.ppermute(current[h], "section", [(mirror(1), 0)]))
    x_other = []
    for h in halves:
        x_other.append((swap(x_low, x_high, h, x_sent if h else None), None))
    cot_other = []
    for h in halves:
        cot_other.append((swap(cot_low, cot_high, h, cot_sent[h]), None))

    def choose(low_records, high_records, others, first_own, first_other):
        refs, choices = [], []

        def add(array):
            refs.append(array)
            return len(refs) - 1

        for h in halves:
            array, index = first_own[h]
            options = [("first", None, add(array), index)]
            for i in range(groups):
                if i > 0:
                    options.append(("own", (0, i), add(low_records[i][h]), None))
                options.append(("own", (1, i), add(high_records[i][h]), None))
            choices.append(options)
        for h in halves:
            array, index = first_other[h]
            choices.append([("first", None, add(array), index), ("rest", None, add(others[h][0]), others[h][1])])
        return refs, choices

    def token_piece(member, h):
        return (tokens, (member, pl.ds(h * half, half)))

    refs, choices = choose(
        x_low, x_high, x_other, [token_piece(0, h) for h in halves], [token_piece(1, h) for h in halves]
    )
    hidden, slopes, normed = ups_call(refs, choices, current[1], half, width, unloaded, (info, lists, None))
    refs, choices = choose(
        cot_low, cot_high, cot_other,
        [(from_low[0], None), (from_high[1], None)], [(from_high[0], None), (from_low[1], None)]
    )
    downs, split = down_grads_call(
        refs, choices, hidden, half, width, shares, unloaded.shape[2], (info, lists, None)
    )

    def reduce(grads):
        return lax.psum_scatter(grads, "dp", scatter_dimension=0, tiled=True)[0].astype(jnp.float32)

    down_share = reduce(downs)
    up_share = reduce(up_grads_call(far(split), far(normed), far(slopes), width, shares, unloaded, (info, lists, None)))
    token_total = 2 * rows * shares
    step_direction, master_next = adam_update(
        jnp.stack([down_share, up_share])[::-1], master[0], moment[0], variance[0], token_total
    )
    return (step_direction[None], master_next[None])


def solution(mesh):
    rows_split = P(None, None, "dp", None)
    by_section = P("section", None, None, "dp", None)
    return jax.shard_map(
        shards,
        mesh=mesh,
        in_specs=(
            rows_split,
            rows_split,
            P("section", None, None, None, None, None),
            P("section", None, None, None, None),
            by_section,
            by_section,
            by_section,
        ),
        out_specs=(by_section, by_section),
        check_vma=False,
    )
```

```python
import jax
import jax.numpy as jnp
from jax import lax
from jax.experimental import pallas as pl
from jax.experimental.pallas import tpu as pltpu
from jax.sharding import PartitionSpec as P


BS = 128
FF_BLOCKS = 8192 // BS
norm_eps = 1e-06
gelu_coef = 0.7978845608028654
gelu_cubic = gelu_coef * 0.044715
beta_first = 0.9
beta_second = 0.95
adam_eps = 1e-08
learn_rate = 0.001
decay_rate = 0.1
update_count = 10
ROW_TILE = 16
EXTRA_BATCH = 4
CHAIN_VMEM = 24 * 1024 * 1024
ENTER_VMEM = 32 * 1024 * 1024
OWN_VMEM = 40 * 1024 * 1024
COST = 4_000_000_000
LOCAL = None
WINDOW = "window"
ENTER_COST = 1
LOW_LAYER, HIGH_LAYER, OWN_LAYER, HIGH, GROUP = range(5)
UP_WIDE, DOWN_WIDE, DOWN_NARROW, UP_NARROW = range(4)
FIELDS = 9
FIRST, FIRST_TAKE, SECOND, SECOND_TAKE, PUT, EXTRA, EXTRA_TAKE, EXTRA_PUT, COUNT = range(FIELDS)


def block_lists(pattern, width):
    total = pattern.shape[2]
    up_row, up_col = pattern[:, 0, :, 0], pattern[:, 0, :, 1]
    down_row, down_col = pattern[:, 1, :, 0], pattern[:, 1, :, 1]
    key = jnp.stack([up_col, down_row, down_col, up_row], 1)
    take = jnp.stack([up_row, down_col, down_row, up_col], 1)
    order = jnp.arange(total, dtype=jnp.int32)
    before = order[None, :] < order[:, None]

    def count(mask):
        return jnp.sum(mask.astype(jnp.int32), axis=-1)

    same = key[..., None, :] == key[..., :, None]
    rank = count(same & before)
    even = rank % 2 == 0
    wide = (jnp.arange(4) < 2)[None, :, None]
    extra = rank >= 2
    extra_place = count(extra[..., None, :] & before)
    pair = count((key[..., None, :] < key[..., :, None]) & even[..., None, :]) + rank // 2
    place_first = jnp.where(wide, jnp.where(rank == 0, key, -1), jnp.where(even, pair, -1))
    place_second = jnp.where(wide, jnp.where(rank == 1, key, -1), jnp.where(even, -1, pair))
    place_extra = jnp.where(wide & extra, extra_place, -1)
    number = jnp.broadcast_to(order, key.shape)
    places = jnp.stack(
        [place_first] * 2 + [place_second] * 2 + [place_first] + [place_extra] * 3, 2
    )
    absent = jnp.where(wide, width // BS, FF_BLOCKS)
    lowered = take - absent
    values = jnp.stack([number, lowered, number, lowered, key, number, lowered, key], 2)
    hit = places[..., None, :] == order[:, None]
    fields = jnp.sum(jnp.where(hit, values[..., None, :], 0), axis=-1)
    slot = jnp.arange(8)
    taken = (slot == FIRST_TAKE) | (slot == SECOND_TAKE) | (slot == EXTRA_TAKE)
    fields = fields + jnp.where(taken[:, None], absent[..., None], 0)
    counts = jnp.where(wide[..., 0], count(extra), count(even))
    counts = jnp.broadcast_to(counts[..., None, None], key.shape[:2] + (1, total))
    lists = jnp.concatenate([fields, counts], axis=2).astype(jnp.int32)
    return jnp.concatenate([lists.reshape(-1), pattern[0].reshape(-1)])


class Lists:
    def __init__(self, ref, copy, total):
        self.ref, self.total = ref, total
        self.base = copy * (4 * FIELDS * total)
        self.cells = 2 * 4 * FIELDS * total

    def __call__(self, kind, field, index):
        return self.ref[self.base + ((kind * FIELDS + field) * self.total) + index]


def hidden_of(preact):
    inner = preact * (gelu_coef + gelu_cubic * (preact * preact))
    half = 0.5 * preact
    return half + half * jnp.tanh(inner)


def both_of(preact):
    cubic = gelu_cubic * (preact * preact)
    tangent = jnp.tanh(preact * (gelu_coef + cubic))
    bend = preact * (gelu_coef + 3.0 * cubic)
    half = 0.5 + 0.5 * tangent
    return (preact * half, half * (1.0 + bend * (1.0 - tangent)))


def dot_plain(left, right):
    return jnp.dot(left, right, preferred_element_type=jnp.float32)


def dot_right_t(left, right):
    return lax.dot_general(left, right, (((1,), (1,)), ((), ())), preferred_element_type=jnp.float32)


def each(count, body, unroll=1):
    def one(i, carry):
        body(i)
        return carry

    lax.fori_loop(0, count, one, 0, unroll=unroll)


def fill_normed(x_ref, normed, base):
    rows, width = x_ref.shape

    def tile(i):
        at = pl.multiple_of(i * ROW_TILE, ROW_TILE)
        wide = x_ref[pl.ds(at, ROW_TILE), :].astype(jnp.float32)
        factor = lax.rsqrt(jnp.mean(wide * wide, axis=-1, keepdims=True) + norm_eps)
        value = (wide * factor).astype(jnp.bfloat16)
        for b in range(width // BS):
            normed[b, pl.ds(base + at, ROW_TILE), :] = value[:, b * BS : (b + 1) * BS]

    each(rows // ROW_TILE, tile, 7)


def fill_split(x_ref, split, base):
    rows, width = x_ref.shape
    for b in range(width // BS):
        split[b, pl.ds(base, rows), :] = x_ref[:, b * BS : (b + 1) * BS]


def pair_product(source, blocks, lists, kind, p, transposed):
    left = jnp.concatenate(
        [source[lists(kind, FIRST_TAKE, p)], source[lists(kind, SECOND_TAKE, p)]], axis=1
    )
    one, two = blocks[lists(kind, FIRST, p)], blocks[lists(kind, SECOND, p)]
    if transposed:
        return dot_right_t(left, jnp.concatenate([one, two], axis=1))
    return dot_plain(left, jnp.concatenate([one, two], axis=0))


def wide_pass(source, blocks, lists, kind, sums, finish, transposed, batch=16, ahead=None):
    def main(i):
        if ahead is not None:
            ahead(i)
        for j in range(batch):
            c = i * batch + j
            value = pair_product(source, blocks, lists, kind, c, transposed)
            sums[c] = value
            finish(c, value)

    each(sums.shape[0] // batch, main)
    dot = dot_right_t if transposed else dot_plain

    def more(e):
        c = lists(kind, EXTRA_PUT, e)
        left = source[lists(kind, EXTRA_TAKE, e)]
        value = sums[c] + dot(left, blocks[lists(kind, EXTRA, e)])
        sums[c] = value
        finish(c, value)

    def batch(i):
        for j in range(EXTRA_BATCH):
            more(i * EXTRA_BATCH + j)

    each((lists(kind, COUNT, 0) + EXTRA_BATCH - 1) // EXTRA_BATCH, batch)


def narrow_pass(source, blocks, lists, kind, sums, transposed):
    sums[...] = jnp.zeros(sums.shape, sums.dtype)

    def one(p):
        sums[lists(kind, PUT, p)] += pair_product(source, blocks, lists, kind, p, transposed)

    each((lists.total + sums.shape[0]) // 2, one, 14)


def forward_rows(x_ref, out_ref, layer, scratch, slopes=None, before=lambda part: None, done=lambda: None):
    normed, sums, hidden, narrow = scratch
    _, width = x_ref.shape
    fill_normed(x_ref, normed, 0)

    def finish(c, value):
        if slopes is None:
            hidden[c] = hidden_of(value).astype(jnp.bfloat16)
        else:
            value, slope = both_of(value)
            hidden[c] = value.astype(jnp.bfloat16)
            slopes[c] = slope.astype(slopes.dtype)

    before(0)
    wide_pass(normed, layer.up, layer.lists, UP_WIDE, sums, finish, False)
    before(1)
    done()
    narrow_pass(hidden, layer.down, layer.lists, DOWN_NARROW, narrow, False)
    for b in range(width // BS):
        cols = slice(b * BS, (b + 1) * BS)
        out_ref[:, cols] = (x_ref[:, cols].astype(jnp.float32) + narrow[b]).astype(jnp.bfloat16)


def backward_rows(x_ref, cot_ref, out_ref, layer, scratch, slopes, ready=lambda: None):
    normed, sums, hidden, narrow = scratch
    rows, width = x_ref.shape
    fill_split(cot_ref, normed, 0)
    ready()

    def finish(c, value):
        hidden[c] = (value * slopes[c].astype(jnp.float32)).astype(jnp.bfloat16)

    wide_pass(normed, layer.down, layer.lists, DOWN_WIDE, sums, finish, True)
    narrow_pass(hidden, layer.up, layer.lists, UP_NARROW, narrow, True)

    def tile(i):
        at = pl.multiple_of(i * ROW_TILE, ROW_TILE)
        wide = x_ref[pl.ds(at, ROW_TILE), :].astype(jnp.float32)
        factor = lax.rsqrt(jnp.mean(wide * wide, axis=-1, keepdims=True) + norm_eps)
        grad = jnp.concatenate(
            [narrow[b, pl.ds(at, ROW_TILE), :] for b in range(width // BS)], axis=-1
        )
        coupling = jnp.mean(wide * grad, axis=-1, keepdims=True)
        upstream = cot_ref[pl.ds(at, ROW_TILE), :].astype(jnp.float32)
        value = upstream + factor * grad - wide * (factor * factor * factor * coupling)
        out_ref[pl.ds(at, ROW_TILE), :] = value.astype(jnp.bfloat16)

    each(rows // ROW_TILE, tile)


def own_cell(layer, part, k):
    lists = layer.lists
    at = lists.cells + 2 * (part * lists.total + k)
    return lists.ref[at], lists.ref[at + 1]


class Layer:
    def __init__(self, info, lists_ref, weights_ref, which, local=None):
        copy = info[which]
        self.lists = Lists(lists_ref, copy, lists_ref.shape[0] // (2 * 4 * FIELDS + 4))
        if weights_ref is not None:
            local = weights_ref.at[copy]
        if local is not None:
            self.up, self.down = local.at[0], local.at[1]


def space_of(space):
    return pltpu.HBM if space is WINDOW else space


def stage(kernel, local_in, remote_in, outs, scratch, operands, cost, vmem=CHAIN_VMEM):
    info, lists, weights = operands
    held = [] if weights is None else [pltpu.with_memory_space_constraint(weights, pltpu.VMEM)]
    any_spec = pl.BlockSpec(memory_space=pltpu.HBM)
    smem_spec = pl.BlockSpec(memory_space=pltpu.SMEM)
    vmem_spec = pl.BlockSpec(memory_space=pltpu.VMEM)
    in_total = len(local_in) + len(remote_in)
    local_in = [pltpu.with_memory_space_constraint(array, pltpu.VMEM) for array in local_in]

    def body(info_ref, lists_ref, *rest):
        weights_ref, rest = (None, rest) if weights is None else (rest[0], rest[1:])
        ins, own = rest[:in_total], rest[in_total + len(outs) :]
        results = rest[in_total : in_total + len(outs)]

        def layer(which, weights_ref=weights_ref, local=None):
            return Layer(info_ref, lists_ref, weights_ref, which, local)

        kernel(layer, info_ref, ins, results, own)

    return pl.pallas_call(
        body,
        in_specs=[smem_spec, smem_spec]
        + [vmem_spec] * (len(held) + len(local_in))
        + [any_spec] * len(remote_in),
        out_specs=[any_spec if space is pltpu.HBM else vmem_spec for space, _ in outs],
        out_shape=[
            shape if space is LOCAL else space_of(space)(shape.shape, shape.dtype)
            for space, shape in outs
        ],
        scratch_shapes=scratch,
        cost_estimate=pl.CostEstimate(flops=cost, transcendentals=0, bytes_accessed=0),
        compiler_params=pltpu.CompilerParams(vmem_limit_bytes=vmem),
    )(info, lists, *held, *local_in, *remote_in)


def layer_scratch(rows, width):
    return [
        pltpu.VMEM((width // BS + 1, rows, BS), jnp.bfloat16),
        pltpu.VMEM((FF_BLOCKS, rows, BS), jnp.float32),
        pltpu.VMEM((FF_BLOCKS + 1, rows, BS), jnp.bfloat16),
        pltpu.VMEM((width // BS, rows, BS), jnp.float32),
    ]


def slope_scratch(rows):
    return [pltpu.VMEM((FF_BLOCKS, rows, BS), jnp.float32)]


def shape_of(shape, dtype=jnp.bfloat16):
    return jax.ShapeDtypeStruct(shape, dtype)


def clear_spare(*refs):
    for ref in refs:
        ref[ref.shape[0] - 1] = jnp.zeros(ref.shape[1:], ref.dtype)


def forward_call(x, whichs, operands):
    rows, width = x.shape
    steps = len(whichs)
    slope_shape = (steps, FF_BLOCKS, rows, BS)

    def kernel(layer, info, ins, results, scratch):
        *layer_refs, slopes, sem = scratch
        clear_spare(layer_refs[0], layer_refs[2])
        moves = [
            pltpu.make_async_copy(slopes.at[i], results[-1].at[i], sem.at[i]) for i in range(steps)
        ]
        source = ins[0]
        for i, which in enumerate(whichs):
            forward_rows(
                source, results[i], layer(which), layer_refs, slopes.at[i], done=moves[i].start
            )
            source = results[i]
        for move in moves:
            move.wait()

    outs = [(LOCAL, shape_of(x.shape))] * steps + [(pltpu.HBM, shape_of(slope_shape))]
    scratch = [pltpu.VMEM(slope_shape, jnp.bfloat16), pltpu.SemaphoreType.DMA((steps,))]
    return stage(
        kernel, [x], [], outs, layer_scratch(rows, width) + scratch, operands, COST * steps
    )


def enter_call(tokens, h, rows, unloaded, operands):
    width = tokens.shape[-1]

    def kernel(layer, info, ins, results, scratch):
        *layer_refs, x_ref, local, sem, weight_sem = scratch
        load = pltpu.make_async_copy(ins[0].at[info[HIGH], pl.ds(h * rows, rows)], x_ref, sem)
        load.start()
        low = info[LOW_LAYER]
        moves = [
            pltpu.make_async_copy(ins[1].at[low, part], local.at[part], weight_sem.at[part])
            for part in range(2)
        ]

        def before(part):
            moves[part].wait()
            if part == 0:
                moves[1].start()

        moves[0].start()
        clear_spare(layer_refs[0], layer_refs[2])
        load.wait()
        forward_rows(x_ref, results[0], layer(LOW_LAYER, None, local), layer_refs, before=before)

    outs = [(LOCAL, shape_of((rows, width)))]
    scratch = layer_scratch(rows, width) + [
        pltpu.VMEM((rows, width), jnp.bfloat16),
        pltpu.VMEM(unloaded.shape[1:], unloaded.dtype),
        pltpu.SemaphoreType.DMA,
        pltpu.SemaphoreType.DMA((2,)),
    ]
    return stage(kernel, [], [tokens, unloaded], outs, scratch, operands, COST * ENTER_COST, CHAIN_VMEM)


def turn_call(x, targets, h, operands, entries=()):
    rows, width = x.shape

    def kernel(layer, info, ins, results, scratch):
        *layer_refs, slopes, aim, sem = scratch
        x_ref, target_ref = ins[0], ins[-1]
        residue, out = results[:2]
        load = pltpu.make_async_copy(target_ref.at[info[HIGH], pl.ds(h * rows, rows)], aim, sem)
        load.start()
        clear_spare(layer_refs[0], layer_refs[2])
        own = layer(HIGH_LAYER)
        forward_rows(x_ref, residue, own, layer_refs, slopes)
        load.wait()
        for b in range(width // BS):
            cols = slice(b * BS, (b + 1) * BS)
            difference = residue[:, cols].astype(jnp.float32) - aim[:, cols].astype(jnp.float32)
            residue[:, cols] = difference.astype(jnp.bfloat16)
        backward_rows(x_ref, residue, out, own, layer_refs, slopes)
        if entries:
            high, group = info[HIGH] == 1, info[GROUP]
            conditions = [~high & (group == 0), ~high & (group != 0), high]
            pick_rows(results[2], list(zip(conditions, ins[:3])))

    return stage(
        kernel, [x] + list(entries), [targets], [(LOCAL, shape_of(x.shape))] * (2 + bool(entries)),
        layer_scratch(rows, width) + slope_scratch(rows)
        + [pltpu.VMEM((rows, width), jnp.bfloat16), pltpu.SemaphoreType.DMA],
        operands, 3 * COST
    )


def pick_rows(target, options):
    for condition, source in options:

        @pl.when(condition)
        def take(source=source):
            target[...] = source[...]


def backward_call(xs, saved, cot, whichs, operands, turned=None, last=None):
    rows, width = cot.shape
    steps = len(whichs)
    local = list(xs) + [cot] + ([] if turned is None else [turned])

    def kernel(layer, info, ins, results, scratch):
        *layer_refs, slopes, sem = scratch
        moves = [
            pltpu.make_async_copy(ins[len(local) + i].at[saved[i][1]], slopes.at[i], sem.at[i])
            for i in range(steps)
        ]
        for move in moves:
            move.start()
        clear_spare(layer_refs[0], layer_refs[2])
        upstream = ins[steps]
        for i, which in enumerate(whichs):
            backward_rows(
                ins[i], upstream, results[i], layer(which), layer_refs, slopes.at[i], moves[i].wait
            )
            upstream = results[i]
        if turned is not None:
            high, group = info[HIGH] == 1, info[GROUP]
            pick_rows(
                results[steps],
                [
                    (high, results[0]),
                    (~high & (group == last), ins[steps]),
                    (~high & (group != last), ins[steps + 1]),
                ],
            )

    scratch = [
        pltpu.VMEM((steps, FF_BLOCKS, rows, BS), jnp.bfloat16),
        pltpu.SemaphoreType.DMA((steps,)),
    ]
    outs = [(LOCAL, shape_of(cot.shape))] * (steps + (turned is not None))
    return stage(
        kernel, local, [array for array, _ in saved], outs, layer_scratch(rows, width) + scratch,
        operands, 2 * COST * steps
    )


def fetch_pieces(info, choices, refs, local, sem):
    first = (info[HIGH] == 0) & (info[GROUP] == 0)
    moves = []
    for piece, options in enumerate(choices):
        for kind, wanted, number, index in options:
            source = refs[number] if index is None else refs[number].at[index]
            move = pltpu.make_async_copy(source, local.at[piece], sem.at[piece])
            if kind == "first":
                condition = first
            elif kind == "own":
                condition = (info[HIGH] == wanted[0]) & (info[GROUP] == wanted[1]) & ~first
            else:
                condition = ~first

            @pl.when(condition)
            def go(move=move):
                move.start()

        moves.append(move)
    return moves


def ups_call(refs, choices, after, rows, width, unloaded, operands):
    pieces = len(choices)
    all_rows = rows * pieces
    part_rows = all_rows // 2

    def kernel(layer, info, ins, results, scratch):
        x_refs, sums, blocks_here, slopes, normed, sem, block_sem, out_sem = scratch
        hidden, slopes_out, normed_out = results
        load = pltpu.make_async_copy(ins[-1].at[0, 0], blocks_here, block_sem.at[0])
        load.start()
        moves = fetch_pieces(info, choices, ins, x_refs, sem)
        own = layer(OWN_LAYER)
        clear_spare(normed)
        for move in moves:
            move.wait()

        def normalise(piece):
            fill_normed(x_refs.at[piece], normed, piece * rows)

        each(pieces, normalise)
        keep = pltpu.make_async_copy(normed, normed_out, block_sem.at[1])
        keep.start()
        load.wait()

        def put(part):
            span = pl.ds(pl.multiple_of(part * part_rows, part_rows), part_rows)
            return pltpu.make_async_copy(slopes.at[part], slopes_out.at[:, span], out_sem.at[part])

        def one(part):
            span = pl.ds(pl.multiple_of(part * part_rows, part_rows), part_rows)

            def finish(c, value):
                value, slope = both_of(value)
                hidden[c, span, :] = value.astype(jnp.bfloat16)
                slopes[part, c] = slope.astype(jnp.bfloat16)

            wide_pass(
                normed.at[:, span], blocks_here, own.lists, UP_WIDE, sums, finish, False, 8
            )
            put(part).start()

        each(2, one)
        keep.wait()
        for part in range(2):
            put(part).wait()

    return stage(
        kernel, [], refs + [after, unloaded],
        [
            (pltpu.VMEM, shape_of((FF_BLOCKS, all_rows, BS))),
            (pltpu.HBM, shape_of((FF_BLOCKS, all_rows, BS))),
            (pltpu.HBM, shape_of((width // BS + 1, all_rows, BS))),
        ],
        [
            pltpu.VMEM((pieces, rows, width), jnp.bfloat16),
            pltpu.VMEM((FF_BLOCKS, part_rows, BS), jnp.float32),
            pltpu.VMEM(unloaded.shape[2:], unloaded.dtype),
            pltpu.VMEM((2, FF_BLOCKS, part_rows, BS), jnp.bfloat16),
            pltpu.VMEM((width // BS + 1, all_rows, BS), jnp.bfloat16),
            pltpu.SemaphoreType.DMA((pieces,)),
            pltpu.SemaphoreType.DMA((2,)),
            pltpu.SemaphoreType.DMA((2,)),
        ],
        operands, 4 * COST, ENTER_VMEM
    )


def spread(out, k, value, shares):
    share_rows = BS // shares
    for share in range(shares):
        out[share, k] = value[share * share_rows : (share + 1) * share_rows]


def down_grads_call(refs, choices, hidden, rows, width, shares, total, operands):
    pieces = len(choices)
    all_rows = rows * pieces

    def kernel(layer, info, ins, results, scratch):
        cot_refs, split, turned, sem, out_sem = scratch
        out, split_out = results
        hidden_ref, refs = ins[0], ins[1:]
        own = layer(OWN_LAYER)
        moves = fetch_pieces(info, choices, refs, cot_refs, sem)
        clear_spare(split)
        for piece in range(pieces):
            moves[piece].wait()
            fill_split(cot_refs.at[piece], split, piece * rows)
        keep = pltpu.make_async_copy(split, split_out, out_sem)
        keep.start()
        for b in range(width // BS):
            turned[b] = split[b].T

        def one(k):
            row, col = own_cell(own, 1, k)
            value = dot_plain(turned[col], hidden_ref[row])
            spread(out, k, value.T.astype(jnp.bfloat16), shares)

        each(total, one, 12)
        keep.wait()

    return stage(
        kernel, [hidden], refs,
        [
            (WINDOW, shape_of((shares, total, BS // shares, BS))),
            (pltpu.HBM, shape_of((width // BS + 1, all_rows, BS))),
        ],
        [
            pltpu.VMEM((pieces, rows, width), jnp.bfloat16),
            pltpu.VMEM((width // BS + 1, all_rows, BS), jnp.bfloat16),
            pltpu.VMEM((width // BS, BS, all_rows), jnp.bfloat16),
            pltpu.SemaphoreType.DMA((pieces,)),
            pltpu.SemaphoreType.DMA,
        ],
        operands, 2 * COST
    )


def up_grads_call(split, normed, slopes, width, shares, unloaded, operands):
    all_rows = split.shape[1]
    part_rows = all_rows // 2
    total = unloaded.shape[2]
    blocks = width // BS

    def kernel(layer, info, ins, results, scratch):
        sums, grad_pre, turned, *local, sem = scratch
        normed_ref, split_ref, blocks_here, slopes_ref = local
        out = results[0]
        sources = [ins[0], ins[1], ins[3].at[0, 1], ins[2]]
        moves = [
            pltpu.make_async_copy(source, target, sem.at[i])
            for i, (source, target) in enumerate(zip(sources, local))
        ]
        for move in moves:
            move.start()
        own = layer(OWN_LAYER)
        moves[0].wait()
        for b in range(blocks):
            turned[b] = normed_ref[b].T
        for move in moves[1:]:
            move.wait()

        def part_of(part):
            span = pl.ds(pl.multiple_of(part * part_rows, part_rows), part_rows)

            def finish(c, value):
                slope = slopes_ref[c, span, :].astype(jnp.float32)
                grad_pre[c, span, :] = (value * slope).astype(jnp.bfloat16)

            wide_pass(
                split_ref.at[:, span], blocks_here, own.lists, DOWN_WIDE, sums, finish, True, 4
            )

        each(2, part_of)

        def one(k):
            row, col = own_cell(own, 0, k)
            value = dot_plain(turned[row], grad_pre[col])
            spread(out, k, value.astype(jnp.bfloat16), shares)

        each(total, one, 4)

    return stage(
        kernel, [], [normed, split, slopes, unloaded],
        [(WINDOW, shape_of((shares, total, BS // shares, BS)))],
        [
            pltpu.VMEM((FF_BLOCKS, part_rows, BS), jnp.float32),
            pltpu.VMEM((FF_BLOCKS, all_rows, BS), jnp.bfloat16),
            pltpu.VMEM((blocks, BS, all_rows), jnp.bfloat16),
            pltpu.VMEM(normed.shape, normed.dtype),
            pltpu.VMEM(split.shape, split.dtype),
            pltpu.VMEM(unloaded.shape[2:], unloaded.dtype),
            pltpu.VMEM(slopes.shape, slopes.dtype),
            pltpu.SemaphoreType.DMA((4,)),
        ],
        operands, 4 * COST, OWN_VMEM
    )[0]


def adam_update(grad_sum, master, moment, variance, token_total):
    gradient = grad_sum / token_total
    moment_next = beta_first * moment + (1.0 - beta_first) * gradient
    variance_next = beta_second * variance + (1.0 - beta_second) * gradient * gradient
    corrected = moment_next / (1.0 - beta_first**update_count)
    spread = jnp.sqrt(variance_next / (1.0 - beta_second**update_count))
    step_direction = corrected / (spread + adam_eps)
    return (step_direction, master - learn_rate * (step_direction + decay_rate * master))


def adam_call(share, part, state, token_total, filled=()):
    shape = state[0].shape
    span = pl.BlockSpec((None,) + shape[1:], lambda i: (part, 0, 0, 0))
    whole = pl.BlockSpec(share.shape, lambda i: (0, 0, 0))

    def kernel(share_ref, master_ref, moment_ref, variance_ref, *rest):
        direction, master_next = rest[-2:]
        direction[...], master_next[...] = adam_update(
            share_ref[...].astype(jnp.float32), master_ref[...], moment_ref[...], variance_ref[...],
            token_total
        )

    return pl.pallas_call(
        kernel,
        grid=(1,),
        in_specs=[whole] + [span] * 3 + [pl.BlockSpec(memory_space=pl.ANY)] * len(filled),
        out_specs=[span, span],
        out_shape=[shape_of(shape, jnp.float32)] * 2,
        input_output_aliases={4 + i: i for i in range(len(filled))},
        name="adam",
        compiler_params=pltpu.CompilerParams(vmem_limit_bytes=CHAIN_VMEM),
    )(share, *state, *filled)


def shards(tokens, targets, weights, pattern, master, moment, variance):
    section = lax.axis_index("section")
    sections = lax.axis_size("section")
    shares = lax.axis_size("dp")
    groups = sections // 2
    micro, rows_each, width = tokens.shape[1:]
    rows = micro * rows_each
    half = rows // 2
    high = section >= groups
    high_member = high.astype(jnp.int32)
    group = jnp.minimum(section, sections - 1 - section)
    info = jnp.stack([high_member, 1 - high_member, jnp.zeros_like(high_member), high_member, group])
    far = lambda array: pltpu.with_memory_space_constraint(array, pltpu.HBM)
    tokens = far(tokens.reshape(2, rows, width))
    targets = far(targets.reshape(2, rows, width))
    pattern = pattern[0]
    lists = block_lists(pattern, width)
    mirror = lambda i: sections - 1 - i

    def lane(i, h):
        other = mirror(i + 1) if h else i + 1
        return [(i, other), (mirror(i), mirror(other))]

    def inward(x, i, h):
        return lax.ppermute(x, "section", lane(i, h))

    def outward(x, i, h):
        return lax.ppermute(x, "section", [(b, a) for a, b in lane(i, h)])

    def at_half(records, h, start=0):
        value = records[start][h]
        for i in range(start + 1, groups):
            value = jnp.where(group == i, records[i][h], value)
        return value

    def swap(low_records, high_records, h, sent):
        if sent is None:
            sent = jnp.where(high, at_half(low_records, h, 1), at_half(high_records, h))
        pairs = [(i, mirror(i)) for i in range(groups)] + [(mirror(i), i) for i in range(1, groups)]
        return lax.ppermute(sent, "section", pairs)

    halves = range(2)
    x_low, x_high, cot_low, cot_high = [[None] * groups for _ in range(4)]
    unloaded = far(weights[0])
    slope_low, slope_high = [[None] * groups for _ in range(2)]
    current = [enter_call(tokens, h, half, unloaded, (info, lists, None))[0] for h in halves]
    operands = (info, lists, weights[0])
    for i in range(groups - 1):
        current = [inward(current[h], i, h) for h in halves]
        x_low[i + 1] = current
        if i + 1 < groups - 1:
            moved = [forward_call(current[h], [LOW_LAYER], operands) for h in halves]
            current = [m[0] for m in moved]
            slope_low[i + 1] = [(far(m[1]), 0) for m in moved]
    both = [forward_call(current[h], [LOW_LAYER, HIGH_LAYER], operands) for h in halves]
    x_high[groups - 1] = [b[0] for b in both]
    slope_low[groups - 1] = [(far(b[2]), 0) for b in both]
    slope_high[groups - 1] = [(far(b[2]), 1) for b in both]
    current = [b[1] for b in both]
    for i in reversed(range(groups - 1)):
        current = [outward(current[h], i, h) for h in halves]
        x_high[i] = current
        if i > 0:
            moved = [forward_call(current[h], [HIGH_LAYER], operands) for h in halves]
            current = [m[0] for m in moved]
            slope_high[i] = [(far(m[1]), 0) for m in moved]
    mirrored = groups == 2
    turned = []
    for h in halves:
        entries = [x_high[1][1], x_low[1][1]] if mirrored and h else []
        turned.append(turn_call(current[h], targets, h, operands, entries))
    x_sent = turned[1][2] if mirrored else None
    cot_high[0] = [t[0] for t in turned]
    current = [t[1] for t in turned]
    for i in range(groups - 1):
        current = [inward(current[h], i, h) for h in halves]
        cot_high[i + 1] = current
        if i + 1 < groups - 1:
            current = [
                backward_call(
                    [x_high[i + 1][h]], [slope_high[i + 1][h]], current[h], [HIGH_LAYER], operands
                )[0]
                for h in halves
            ]
    last = groups - 1
    cot_sent = [None, None]
    cot_low[last], current, entering = [None, None], [None, None], current
    for h in halves:
        top, bottom = (x_high[last][h], x_low[last][h])
        tops, bottoms = slope_high[last][h], slope_low[last][h]
        sending = dict(turned=cot_high[0][h], last=last) if mirrored else {}
        if h == 0:
            moved = backward_call(
                [top, bottom], [tops, bottoms], entering[h], [HIGH_LAYER, LOW_LAYER], operands,
                **sending
            )
            cot_low[last][h], current[h], *sent = moved
        else:
            cot_low[last][h], *sent = backward_call(
                [top], [tops], entering[h], [HIGH_LAYER], operands, **sending
            )
            (current[h],) = backward_call(
                [bottom], [bottoms], cot_low[last][h], [LOW_LAYER], operands
            )
        cot_sent[h] = sent[0] if mirrored else None
    for i in reversed(range(1, last)):
        current = [outward(current[h], i, h) for h in halves]
        cot_low[i] = current
        current = [
            backward_call([x_low[i][h]], [slope_low[i][h]], current[h], [LOW_LAYER], operands)[0]
            for h in halves
        ]
    from_low, from_high = [], []
    for h in halves:
        from_low.append(lax.ppermute(current[h], "section", [(1, 0)]))
        from_high.append(lax.ppermute(current[h], "section", [(mirror(1), 0)]))
    x_other = []
    for h in halves:
        x_other.append((swap(x_low, x_high, h, x_sent if h else None), None))
    cot_other = []
    for h in halves:
        cot_other.append((swap(cot_low, cot_high, h, cot_sent[h]), None))

    def choose(low_records, high_records, others, first_own, first_other):
        refs, choices = [], []

        def add(array):
            refs.append(array)
            return len(refs) - 1

        for h in halves:
            array, index = first_own[h]
            options = [("first", None, add(array), index)]
            for i in range(groups):
                if i > 0:
                    options.append(("own", (0, i), add(low_records[i][h]), None))
                options.append(("own", (1, i), add(high_records[i][h]), None))
            choices.append(options)
        for h in halves:
            array, index = first_other[h]
            choices.append([("first", None, add(array), index), ("rest", None, add(others[h][0]), others[h][1])])
        return refs, choices

    def token_piece(member, h):
        return (tokens, (member, pl.ds(h * half, half)))

    refs, choices = choose(
        x_low, x_high, x_other, [token_piece(0, h) for h in halves], [token_piece(1, h) for h in halves]
    )
    hidden, slopes, normed = ups_call(refs, choices, current[1], half, width, unloaded, (info, lists, None))
    refs, choices = choose(
        cot_low, cot_high, cot_other,
        [(from_low[0], None), (from_high[1], None)], [(from_high[0], None), (from_low[1], None)]
    )
    downs, split = down_grads_call(
        refs, choices, hidden, half, width, shares, unloaded.shape[2], (info, lists, None)
    )

    def reduce(grads):
        return lax.psum_scatter(grads, "dp", scatter_dimension=0, tiled=True)[0]

    down_share = reduce(downs)
    up_share = reduce(
        up_grads_call(far(split), far(normed), far(slopes), width, shares, unloaded, (info, lists, None))
    )
    token_total = 2 * rows * shares
    state = (far(master[0]), far(moment[0]), far(variance[0]))
    filled = adam_call(far(down_share), 1, state, token_total)
    step_direction, master_next = adam_call(far(up_share), 0, state, token_total, filled)
    return (step_direction[None], master_next[None])


def solution(mesh):
    rows_split = P(None, None, "dp", None)
    by_section = P("section", None, None, "dp", None)
    return jax.shard_map(
        shards,
        mesh=mesh,
        in_specs=(
            rows_split,
            rows_split,
            P("section", None, None, None, None, None),
            P("section", None, None, None, None),
            by_section,
            by_section,
            by_section,
        ),
        out_specs=(by_section, by_section),
        check_vma=False,
    )
```

```python
import jax
import jax.numpy as jnp
from jax import lax
from jax.experimental import pallas as pl
from jax.experimental.pallas import tpu as pltpu
from jax.sharding import PartitionSpec as P


BS = 128
FF_BLOCKS = 8192 // BS
norm_eps = 1e-06
gelu_coef = 0.7978845608028654
gelu_cubic = gelu_coef * 0.044715
beta_first = 0.9
beta_second = 0.95
adam_eps = 1e-08
learn_rate = 0.001
decay_rate = 0.1
update_count = 10
ROW_TILE = 16
EXTRA_BATCH = 4
CHAIN_VMEM = 24 * 1024 * 1024
ENTER_VMEM = 32 * 1024 * 1024
OWN_VMEM = 40 * 1024 * 1024
COST = 4_000_000_000
LOCAL = None
WINDOW = "window"
ENTER_COST = 1
LOW_LAYER, HIGH_LAYER, OWN_LAYER, HIGH, GROUP = range(5)
UP_WIDE, DOWN_WIDE, DOWN_NARROW, UP_NARROW = range(4)
FIELDS = 9
FIRST, FIRST_TAKE, SECOND, SECOND_TAKE, PUT, EXTRA, EXTRA_TAKE, EXTRA_PUT, COUNT = range(FIELDS)


def block_lists(pattern, width):
    total = pattern.shape[2]
    up_row, up_col = pattern[:, 0, :, 0], pattern[:, 0, :, 1]
    down_row, down_col = pattern[:, 1, :, 0], pattern[:, 1, :, 1]
    key = jnp.stack([up_col, down_row, down_col, up_row], 1)
    take = jnp.stack([up_row, down_col, down_row, up_col], 1)
    order = jnp.arange(total, dtype=jnp.int32)
    before = order[None, :] < order[:, None]

    def count(mask):
        return jnp.sum(mask.astype(jnp.int32), axis=-1)

    same = key[..., None, :] == key[..., :, None]
    rank = count(same & before)
    even = rank % 2 == 0
    wide = (jnp.arange(4) < 2)[None, :, None]
    extra = rank >= 2
    extra_place = count(extra[..., None, :] & before)
    pair = count((key[..., None, :] < key[..., :, None]) & even[..., None, :]) + rank // 2
    place_first = jnp.where(wide, jnp.where(rank == 0, key, -1), jnp.where(even, pair, -1))
    place_second = jnp.where(wide, jnp.where(rank == 1, key, -1), jnp.where(even, -1, pair))
    place_extra = jnp.where(wide & extra, extra_place, -1)
    number = jnp.broadcast_to(order, key.shape)
    places = jnp.stack(
        [place_first] * 2 + [place_second] * 2 + [place_first] + [place_extra] * 3, 2
    )
    absent = jnp.where(wide, width // BS, FF_BLOCKS)
    lowered = take - absent
    values = jnp.stack([number, lowered, number, lowered, key, number, lowered, key], 2)
    hit = places[..., None, :] == order[:, None]
    fields = jnp.sum(jnp.where(hit, values[..., None, :], 0), axis=-1)
    slot = jnp.arange(8)
    taken = (slot == FIRST_TAKE) | (slot == SECOND_TAKE) | (slot == EXTRA_TAKE)
    fields = fields + jnp.where(taken[:, None], absent[..., None], 0)
    counts = jnp.where(wide[..., 0], count(extra), count(even))
    counts = jnp.broadcast_to(counts[..., None, None], key.shape[:2] + (1, total))
    lists = jnp.concatenate([fields, counts], axis=2).astype(jnp.int32)
    return jnp.concatenate([lists.reshape(-1), pattern[0].reshape(-1)])


class Lists:
    def __init__(self, ref, copy, total):
        self.ref, self.total = ref, total
        self.base = copy * (4 * FIELDS * total)
        self.cells = 2 * 4 * FIELDS * total

    def __call__(self, kind, field, index):
        return self.ref[self.base + ((kind * FIELDS + field) * self.total) + index]


def hidden_of(preact):
    inner = preact * (gelu_coef + gelu_cubic * (preact * preact))
    half = 0.5 * preact
    return half + half * jnp.tanh(inner)


def both_of(preact):
    cubic = gelu_cubic * (preact * preact)
    tangent = jnp.tanh(preact * (gelu_coef + cubic))
    bend = preact * (gelu_coef + 3.0 * cubic)
    half = 0.5 + 0.5 * tangent
    return (preact * half, half * (1.0 + bend * (1.0 - tangent)))


def dot_plain(left, right):
    return jnp.dot(left, right, preferred_element_type=jnp.float32)


def dot_right_t(left, right):
    return lax.dot_general(left, right, (((1,), (1,)), ((), ())), preferred_element_type=jnp.float32)


def each(count, body, unroll=1):
    def one(i, carry):
        body(i)
        return carry

    lax.fori_loop(0, count, one, 0, unroll=unroll)


def fill_normed(x_ref, normed, base):
    rows, width = x_ref.shape

    def tile(i):
        at = pl.multiple_of(i * ROW_TILE, ROW_TILE)
        wide = x_ref[pl.ds(at, ROW_TILE), :].astype(jnp.float32)
        factor = lax.rsqrt(jnp.mean(wide * wide, axis=-1, keepdims=True) + norm_eps)
        value = (wide * factor).astype(jnp.bfloat16)
        for b in range(width // BS):
            normed[b, pl.ds(base + at, ROW_TILE), :] = value[:, b * BS : (b + 1) * BS]

    each(rows // ROW_TILE, tile, 7)


def fill_split(x_ref, split, base):
    rows, width = x_ref.shape
    for b in range(width // BS):
        split[b, pl.ds(base, rows), :] = x_ref[:, b * BS : (b + 1) * BS]


def pair_product(source, blocks, lists, kind, p, transposed):
    left = jnp.concatenate(
        [source[lists(kind, FIRST_TAKE, p)], source[lists(kind, SECOND_TAKE, p)]], axis=1
    )
    one, two = blocks[lists(kind, FIRST, p)], blocks[lists(kind, SECOND, p)]
    if transposed:
        return dot_right_t(left, jnp.concatenate([one, two], axis=1))
    return dot_plain(left, jnp.concatenate([one, two], axis=0))


def wide_pass(source, blocks, lists, kind, sums, finish, transposed, batch=16, ahead=None):
    def main(i):
        if ahead is not None:
            ahead(i)
        for j in range(batch):
            c = i * batch + j
            value = pair_product(source, blocks, lists, kind, c, transposed)
            sums[c] = value
            finish(c, value)

    each(sums.shape[0] // batch, main)
    dot = dot_right_t if transposed else dot_plain

    def more(e):
        c = lists(kind, EXTRA_PUT, e)
        left = source[lists(kind, EXTRA_TAKE, e)]
        value = sums[c] + dot(left, blocks[lists(kind, EXTRA, e)])
        sums[c] = value
        finish(c, value)

    def batch(i):
        for j in range(EXTRA_BATCH):
            more(i * EXTRA_BATCH + j)

    each((lists(kind, COUNT, 0) + EXTRA_BATCH - 1) // EXTRA_BATCH, batch)


def narrow_pass(source, blocks, lists, kind, sums, transposed):
    sums[...] = jnp.zeros(sums.shape, sums.dtype)

    def one(p):
        sums[lists(kind, PUT, p)] += pair_product(source, blocks, lists, kind, p, transposed)

    each((lists.total + sums.shape[0]) // 2, one, 14)


def forward_rows(x_ref, out_ref, layer, scratch, slopes=None, before=lambda part: None, done=lambda: None):
    normed, sums, hidden, narrow = scratch
    _, width = x_ref.shape
    fill_normed(x_ref, normed, 0)

    def finish(c, value):
        if slopes is None:
            hidden[c] = hidden_of(value).astype(jnp.bfloat16)
        else:
            value, slope = both_of(value)
            hidden[c] = value.astype(jnp.bfloat16)
            slopes[c] = slope.astype(slopes.dtype)

    before(0)
    wide_pass(normed, layer.up, layer.lists, UP_WIDE, sums, finish, False)
    before(1)
    done()
    narrow_pass(hidden, layer.down, layer.lists, DOWN_NARROW, narrow, False)
    for b in range(width // BS):
        cols = slice(b * BS, (b + 1) * BS)
        out_ref[:, cols] = (x_ref[:, cols].astype(jnp.float32) + narrow[b]).astype(jnp.bfloat16)


def backward_rows(x_ref, cot_ref, out_ref, layer, scratch, slopes, ready=lambda: None):
    normed, sums, hidden, narrow = scratch
    rows, width = x_ref.shape
    fill_split(cot_ref, normed, 0)
    ready()

    def finish(c, value):
        hidden[c] = (value * slopes[c].astype(jnp.float32)).astype(jnp.bfloat16)

    wide_pass(normed, layer.down, layer.lists, DOWN_WIDE, sums, finish, True)
    narrow_pass(hidden, layer.up, layer.lists, UP_NARROW, narrow, True)

    def tile(i):
        at = pl.multiple_of(i * ROW_TILE, ROW_TILE)
        wide = x_ref[pl.ds(at, ROW_TILE), :].astype(jnp.float32)
        factor = lax.rsqrt(jnp.mean(wide * wide, axis=-1, keepdims=True) + norm_eps)
        grad = jnp.concatenate(
            [narrow[b, pl.ds(at, ROW_TILE), :] for b in range(width // BS)], axis=-1
        )
        coupling = jnp.mean(wide * grad, axis=-1, keepdims=True)
        upstream = cot_ref[pl.ds(at, ROW_TILE), :].astype(jnp.float32)
        value = upstream + factor * grad - wide * (factor * factor * factor * coupling)
        out_ref[pl.ds(at, ROW_TILE), :] = value.astype(jnp.bfloat16)

    each(rows // ROW_TILE, tile)


def own_cell(layer, part, k):
    lists = layer.lists
    at = lists.cells + 2 * (part * lists.total + k)
    return lists.ref[at], lists.ref[at + 1]


class Layer:
    def __init__(self, info, lists_ref, weights_ref, which, local=None):
        copy = info[which]
        self.lists = Lists(lists_ref, copy, lists_ref.shape[0] // (2 * 4 * FIELDS + 4))
        if weights_ref is not None:
            local = weights_ref.at[copy]
        if local is not None:
            self.up, self.down = local.at[0], local.at[1]


def space_of(space):
    return pltpu.HBM if space is WINDOW else space


def stage(kernel, local_in, remote_in, outs, scratch, operands, cost, vmem=CHAIN_VMEM):
    info, lists, weights = operands
    held = [] if weights is None else [pltpu.with_memory_space_constraint(weights, pltpu.VMEM)]
    any_spec = pl.BlockSpec(memory_space=pltpu.HBM)
    smem_spec = pl.BlockSpec(memory_space=pltpu.SMEM)
    vmem_spec = pl.BlockSpec(memory_space=pltpu.VMEM)
    in_total = len(local_in) + len(remote_in)
    local_in = [pltpu.with_memory_space_constraint(array, pltpu.VMEM) for array in local_in]

    def body(info_ref, lists_ref, *rest):
        weights_ref, rest = (None, rest) if weights is None else (rest[0], rest[1:])
        ins, own = rest[:in_total], rest[in_total + len(outs) :]
        results = rest[in_total : in_total + len(outs)]

        def layer(which, weights_ref=weights_ref, local=None):
            return Layer(info_ref, lists_ref, weights_ref, which, local)

        kernel(layer, info_ref, ins, results, own)

    return pl.pallas_call(
        body,
        in_specs=[smem_spec, smem_spec]
        + [vmem_spec] * (len(held) + len(local_in))
        + [any_spec] * len(remote_in),
        out_specs=[any_spec if space is pltpu.HBM else vmem_spec for space, _ in outs],
        out_shape=[
            shape if space is LOCAL else space_of(space)(shape.shape, shape.dtype)
            for space, shape in outs
        ],
        scratch_shapes=scratch,
        cost_estimate=pl.CostEstimate(flops=cost, transcendentals=0, bytes_accessed=0),
        compiler_params=pltpu.CompilerParams(vmem_limit_bytes=vmem),
    )(info, lists, *held, *local_in, *remote_in)


def layer_scratch(rows, width):
    return [
        pltpu.VMEM((width // BS + 1, rows, BS), jnp.bfloat16),
        pltpu.VMEM((FF_BLOCKS, rows, BS), jnp.float32),
        pltpu.VMEM((FF_BLOCKS + 1, rows, BS), jnp.bfloat16),
        pltpu.VMEM((width // BS, rows, BS), jnp.float32),
    ]


def slope_scratch(rows):
    return [pltpu.VMEM((FF_BLOCKS, rows, BS), jnp.float32)]


def shape_of(shape, dtype=jnp.bfloat16):
    return jax.ShapeDtypeStruct(shape, dtype)


def clear_spare(*refs):
    for ref in refs:
        ref[ref.shape[0] - 1] = jnp.zeros(ref.shape[1:], ref.dtype)


def forward_call(x, whichs, operands):
    rows, width = x.shape
    steps = len(whichs)
    slope_shape = (steps, FF_BLOCKS, rows, BS)

    def kernel(layer, info, ins, results, scratch):
        *layer_refs, slopes, sem = scratch
        clear_spare(layer_refs[0], layer_refs[2])
        moves = [
            pltpu.make_async_copy(slopes.at[i], results[-1].at[i], sem.at[i]) for i in range(steps)
        ]
        source = ins[0]
        for i, which in enumerate(whichs):
            forward_rows(
                source, results[i], layer(which), layer_refs, slopes.at[i], done=moves[i].start
            )
            source = results[i]
        for move in moves:
            move.wait()

    outs = [(LOCAL, shape_of(x.shape))] * steps + [(pltpu.HBM, shape_of(slope_shape))]
    scratch = [pltpu.VMEM(slope_shape, jnp.bfloat16), pltpu.SemaphoreType.DMA((steps,))]
    return stage(
        kernel, [x], [], outs, layer_scratch(rows, width) + scratch, operands, COST * steps
    )


def enter_call(tokens, h, rows, unloaded, operands):
    width = tokens.shape[-1]

    def kernel(layer, info, ins, results, scratch):
        *layer_refs, x_ref, local, sem, weight_sem = scratch
        load = pltpu.make_async_copy(ins[0].at[info[HIGH], pl.ds(h * rows, rows)], x_ref, sem)
        load.start()
        low = info[LOW_LAYER]
        moves = [
            pltpu.make_async_copy(ins[1].at[low, part], local.at[part], weight_sem.at[part])
            for part in range(2)
        ]

        def before(part):
            moves[part].wait()
            if part == 0:
                moves[1].start()

        moves[0].start()
        clear_spare(layer_refs[0], layer_refs[2])
        load.wait()
        forward_rows(x_ref, results[0], layer(LOW_LAYER, None, local), layer_refs, before=before)

    outs = [(LOCAL, shape_of((rows, width)))]
    scratch = layer_scratch(rows, width) + [
        pltpu.VMEM((rows, width), jnp.bfloat16),
        pltpu.VMEM(unloaded.shape[1:], unloaded.dtype),
        pltpu.SemaphoreType.DMA,
        pltpu.SemaphoreType.DMA((2,)),
    ]
    return stage(kernel, [], [tokens, unloaded], outs, scratch, operands, COST * ENTER_COST, CHAIN_VMEM)


def turn_call(x, targets, h, operands, entries=()):
    rows, width = x.shape

    def kernel(layer, info, ins, results, scratch):
        *layer_refs, slopes, aim, sem = scratch
        x_ref, target_ref = ins[0], ins[-1]
        residue, out = results[:2]
        load = pltpu.make_async_copy(target_ref.at[info[HIGH], pl.ds(h * rows, rows)], aim, sem)
        load.start()
        clear_spare(layer_refs[0], layer_refs[2])
        own = layer(HIGH_LAYER)
        forward_rows(x_ref, residue, own, layer_refs, slopes)
        load.wait()
        for b in range(width // BS):
            cols = slice(b * BS, (b + 1) * BS)
            difference = residue[:, cols].astype(jnp.float32) - aim[:, cols].astype(jnp.float32)
            residue[:, cols] = difference.astype(jnp.bfloat16)
        backward_rows(x_ref, residue, out, own, layer_refs, slopes)
        if entries:
            high, group = info[HIGH] == 1, info[GROUP]
            conditions = [~high & (group == 0), ~high & (group != 0), high]
            pick_rows(results[2], list(zip(conditions, ins[:3])))

    return stage(
        kernel, [x] + list(entries), [targets], [(LOCAL, shape_of(x.shape))] * (2 + bool(entries)),
        layer_scratch(rows, width) + slope_scratch(rows)
        + [pltpu.VMEM((rows, width), jnp.bfloat16), pltpu.SemaphoreType.DMA],
        operands, 3 * COST
    )


def pick_rows(target, options):
    for condition, source in options:

        @pl.when(condition)
        def take(source=source):
            target[...] = source[...]


def backward_call(xs, saved, cot, whichs, operands, turned=None, last=None):
    rows, width = cot.shape
    steps = len(whichs)
    local = list(xs) + [cot] + ([] if turned is None else [turned])

    def kernel(layer, info, ins, results, scratch):
        *layer_refs, slopes, sem = scratch
        moves = [
            pltpu.make_async_copy(ins[len(local) + i].at[saved[i][1]], slopes.at[i], sem.at[i])
            for i in range(steps)
        ]
        for move in moves:
            move.start()
        clear_spare(layer_refs[0], layer_refs[2])
        upstream = ins[steps]
        for i, which in enumerate(whichs):
            backward_rows(
                ins[i], upstream, results[i], layer(which), layer_refs, slopes.at[i], moves[i].wait
            )
            upstream = results[i]
        if turned is not None:
            high, group = info[HIGH] == 1, info[GROUP]
            pick_rows(
                results[steps],
                [
                    (high, results[0]),
                    (~high & (group == last), ins[steps]),
                    (~high & (group != last), ins[steps + 1]),
                ],
            )

    scratch = [
        pltpu.VMEM((steps, FF_BLOCKS, rows, BS), jnp.bfloat16),
        pltpu.SemaphoreType.DMA((steps,)),
    ]
    outs = [(LOCAL, shape_of(cot.shape))] * (steps + (turned is not None))
    return stage(
        kernel, local, [array for array, _ in saved], outs, layer_scratch(rows, width) + scratch,
        operands, 2 * COST * steps
    )


def fetch_pieces(info, choices, refs, local, sem):
    first = (info[HIGH] == 0) & (info[GROUP] == 0)
    moves = []
    for piece, options in enumerate(choices):
        for kind, wanted, number, index in options:
            source = refs[number] if index is None else refs[number].at[index]
            move = pltpu.make_async_copy(source, local.at[piece], sem.at[piece])
            if kind == "first":
                condition = first
            elif kind == "own":
                condition = (info[HIGH] == wanted[0]) & (info[GROUP] == wanted[1]) & ~first
            else:
                condition = ~first

            @pl.when(condition)
            def go(move=move):
                move.start()

        moves.append(move)
    return moves


def ups_call(refs, choices, after, rows, width, unloaded, operands):
    pieces = len(choices)
    all_rows = rows * pieces
    part_rows = all_rows // 2

    def kernel(layer, info, ins, results, scratch):
        x_refs, sums, blocks_here, slopes, normed, sem, block_sem, out_sem = scratch
        hidden, slopes_out, normed_out = results
        load = pltpu.make_async_copy(ins[-1].at[0, 0], blocks_here, block_sem.at[0])
        load.start()
        moves = fetch_pieces(info, choices, ins, x_refs, sem)
        own = layer(OWN_LAYER)
        clear_spare(normed)
        for move in moves:
            move.wait()

        def normalise(piece):
            fill_normed(x_refs.at[piece], normed, piece * rows)

        each(pieces, normalise)
        keep = pltpu.make_async_copy(normed, normed_out, block_sem.at[1])
        keep.start()
        load.wait()

        def put(part):
            span = pl.ds(pl.multiple_of(part * part_rows, part_rows), part_rows)
            return pltpu.make_async_copy(slopes.at[part], slopes_out.at[:, span], out_sem.at[part])

        def one(part):
            span = pl.ds(pl.multiple_of(part * part_rows, part_rows), part_rows)

            def finish(c, value):
                value, slope = both_of(value)
                hidden[c, span, :] = value.astype(jnp.bfloat16)
                slopes[part, c] = slope.astype(jnp.bfloat16)

            wide_pass(
                normed.at[:, span], blocks_here, own.lists, UP_WIDE, sums, finish, False, 16
            )
            put(part).start()

        each(2, one)
        keep.wait()
        for part in range(2):
            put(part).wait()

    return stage(
        kernel, [], refs + [after, unloaded],
        [
            (pltpu.VMEM, shape_of((FF_BLOCKS, all_rows, BS))),
            (pltpu.HBM, shape_of((FF_BLOCKS, all_rows, BS))),
            (pltpu.HBM, shape_of((width // BS + 1, all_rows, BS))),
        ],
        [
            pltpu.VMEM((pieces, rows, width), jnp.bfloat16),
            pltpu.VMEM((FF_BLOCKS, part_rows, BS), jnp.float32),
            pltpu.VMEM(unloaded.shape[2:], unloaded.dtype),
            pltpu.VMEM((2, FF_BLOCKS, part_rows, BS), jnp.bfloat16),
            pltpu.VMEM((width // BS + 1, all_rows, BS), jnp.bfloat16),
            pltpu.SemaphoreType.DMA((pieces,)),
            pltpu.SemaphoreType.DMA((2,)),
            pltpu.SemaphoreType.DMA((2,)),
        ],
        operands, 4 * COST, ENTER_VMEM
    )


def spread(out, k, value, shares):
    share_rows = BS // shares
    for share in range(shares):
        out[share, k] = value[share * share_rows : (share + 1) * share_rows]


def down_grads_call(refs, choices, hidden, rows, width, shares, total, operands):
    pieces = len(choices)
    all_rows = rows * pieces

    def kernel(layer, info, ins, results, scratch):
        cot_refs, split, turned, sem, out_sem = scratch
        out, split_out = results
        hidden_ref, refs = ins[0], ins[1:]
        own = layer(OWN_LAYER)
        moves = fetch_pieces(info, choices, refs, cot_refs, sem)
        clear_spare(split)
        for piece in range(pieces):
            moves[piece].wait()
            fill_split(cot_refs.at[piece], split, piece * rows)
        keep = pltpu.make_async_copy(split, split_out, out_sem)
        keep.start()
        for b in range(width // BS):
            turned[b] = split[b].T

        def one(k):
            row, col = own_cell(own, 1, k)
            value = dot_plain(turned[col], hidden_ref[row])
            spread(out, k, value.T.astype(jnp.bfloat16), shares)

        each(total, one, 12)
        keep.wait()

    return stage(
        kernel, [hidden], refs,
        [
            (WINDOW, shape_of((shares, total, BS // shares, BS))),
            (pltpu.HBM, shape_of((width // BS + 1, all_rows, BS))),
        ],
        [
            pltpu.VMEM((pieces, rows, width), jnp.bfloat16),
            pltpu.VMEM((width // BS + 1, all_rows, BS), jnp.bfloat16),
            pltpu.VMEM((width // BS, BS, all_rows), jnp.bfloat16),
            pltpu.SemaphoreType.DMA((pieces,)),
            pltpu.SemaphoreType.DMA,
        ],
        operands, 2 * COST
    )


def up_grads_call(split, normed, slopes, width, shares, unloaded, operands):
    all_rows = split.shape[1]
    part_rows = all_rows // 2
    total = unloaded.shape[2]
    blocks = width // BS

    def kernel(layer, info, ins, results, scratch):
        sums, grad_pre, turned, *local, sem = scratch
        normed_ref, split_ref, blocks_here, slopes_ref = local
        out = results[0]
        sources = [ins[0], ins[1], ins[3].at[0, 1], ins[2]]
        moves = [
            pltpu.make_async_copy(source, target, sem.at[i])
            for i, (source, target) in enumerate(zip(sources, local))
        ]
        for move in moves:
            move.start()
        own = layer(OWN_LAYER)
        moves[0].wait()
        for b in range(blocks):
            turned[b] = normed_ref[b].T
        for move in moves[1:]:
            move.wait()

        def part_of(part):
            span = pl.ds(pl.multiple_of(part * part_rows, part_rows), part_rows)

            def finish(c, value):
                slope = slopes_ref[c, span, :].astype(jnp.float32)
                grad_pre[c, span, :] = (value * slope).astype(jnp.bfloat16)

            wide_pass(
                split_ref.at[:, span], blocks_here, own.lists, DOWN_WIDE, sums, finish, True, 4
            )

        each(2, part_of)

        def one(k):
            row, col = own_cell(own, 0, k)
            value = dot_plain(turned[row], grad_pre[col])
            spread(out, k, value.astype(jnp.bfloat16), shares)

        each(total, one, 4)

    return stage(
        kernel, [], [normed, split, slopes, unloaded],
        [(WINDOW, shape_of((shares, total, BS // shares, BS)))],
        [
            pltpu.VMEM((FF_BLOCKS, part_rows, BS), jnp.float32),
            pltpu.VMEM((FF_BLOCKS, all_rows, BS), jnp.bfloat16),
            pltpu.VMEM((blocks, BS, all_rows), jnp.bfloat16),
            pltpu.VMEM(normed.shape, normed.dtype),
            pltpu.VMEM(split.shape, split.dtype),
            pltpu.VMEM(unloaded.shape[2:], unloaded.dtype),
            pltpu.VMEM(slopes.shape, slopes.dtype),
            pltpu.SemaphoreType.DMA((4,)),
        ],
        operands, 4 * COST, OWN_VMEM
    )[0]


def adam_update(grad_sum, master, moment, variance, token_total):
    gradient = grad_sum / token_total
    moment_next = beta_first * moment + (1.0 - beta_first) * gradient
    variance_next = beta_second * variance + (1.0 - beta_second) * gradient * gradient
    corrected = moment_next / (1.0 - beta_first**update_count)
    spread = jnp.sqrt(variance_next / (1.0 - beta_second**update_count))
    step_direction = corrected / (spread + adam_eps)
    return (step_direction, master - learn_rate * (step_direction + decay_rate * master))


def adam_call(share, part, state, token_total, filled=()):
    shape = state[0].shape
    pieces = 1
    piece = shape[1] // pieces
    span = pl.BlockSpec((None, piece) + shape[2:], lambda i: (part, i, 0, 0))
    whole = pl.BlockSpec((piece,) + shape[2:], lambda i: (i, 0, 0))

    def kernel(share_ref, master_ref, moment_ref, variance_ref, *rest):
        direction, master_next = rest[-2:]
        direction[...], master_next[...] = adam_update(
            share_ref[...].astype(jnp.float32), master_ref[...], moment_ref[...], variance_ref[...],
            token_total
        )

    return pl.pallas_call(
        kernel,
        grid=(pieces,),
        in_specs=[whole] + [span] * 3 + [pl.BlockSpec(memory_space=pl.ANY)] * len(filled),
        out_specs=[span, span],
        out_shape=[shape_of(shape, jnp.float32)] * 2,
        input_output_aliases={4 + i: i for i in range(len(filled))},
        name="adam",
        compiler_params=pltpu.CompilerParams(vmem_limit_bytes=CHAIN_VMEM),
    )(share, *state, *filled)


def shards(tokens, targets, weights, pattern, master, moment, variance):
    section = lax.axis_index("section")
    sections = lax.axis_size("section")
    shares = lax.axis_size("dp")
    groups = sections // 2
    micro, rows_each, width = tokens.shape[1:]
    rows = micro * rows_each
    half = rows // 2
    high = section >= groups
    high_member = high.astype(jnp.int32)
    group = jnp.minimum(section, sections - 1 - section)
    info = jnp.stack([high_member, 1 - high_member, jnp.zeros_like(high_member), high_member, group])
    far = lambda array: pltpu.with_memory_space_constraint(array, pltpu.HBM)
    tokens = far(tokens.reshape(2, rows, width))
    targets = far(targets.reshape(2, rows, width))
    pattern = pattern[0]
    lists = block_lists(pattern, width)
    mirror = lambda i: sections - 1 - i

    def lane(i, h):
        other = mirror(i + 1) if h else i + 1
        return [(i, other), (mirror(i), mirror(other))]

    def inward(x, i, h):
        return lax.ppermute(x, "section", lane(i, h))

    def outward(x, i, h):
        return lax.ppermute(x, "section", [(b, a) for a, b in lane(i, h)])

    def at_half(records, h, start=0):
        value = records[start][h]
        for i in range(start + 1, groups):
            value = jnp.where(group == i, records[i][h], value)
        return value

    def swap(low_records, high_records, h, sent):
        if sent is None:
            sent = jnp.where(high, at_half(low_records, h, 1), at_half(high_records, h))
        pairs = [(i, mirror(i)) for i in range(groups)] + [(mirror(i), i) for i in range(1, groups)]
        return lax.ppermute(sent, "section", pairs)

    halves = range(2)
    x_low, x_high, cot_low, cot_high = [[None] * groups for _ in range(4)]
    unloaded = far(weights[0])
    slope_low, slope_high = [[None] * groups for _ in range(2)]
    current = [enter_call(tokens, h, half, unloaded, (info, lists, None))[0] for h in halves]
    operands = (info, lists, weights[0])
    for i in range(groups - 1):
        current = [inward(current[h], i, h) for h in halves]
        x_low[i + 1] = current
        if i + 1 < groups - 1:
            moved = [forward_call(current[h], [LOW_LAYER], operands) for h in halves]
            current = [m[0] for m in moved]
            slope_low[i + 1] = [(far(m[1]), 0) for m in moved]
    both = [forward_call(current[h], [LOW_LAYER, HIGH_LAYER], operands) for h in halves]
    x_high[groups - 1] = [b[0] for b in both]
    slope_low[groups - 1] = [(far(b[2]), 0) for b in both]
    slope_high[groups - 1] = [(far(b[2]), 1) for b in both]
    current = [b[1] for b in both]
    for i in reversed(range(groups - 1)):
        current = [outward(current[h], i, h) for h in halves]
        x_high[i] = current
        if i > 0:
            moved = [forward_call(current[h], [HIGH_LAYER], operands) for h in halves]
            current = [m[0] for m in moved]
            slope_high[i] = [(far(m[1]), 0) for m in moved]
    mirrored = groups == 2
    turned = []
    for h in halves:
        entries = [x_high[1][1], x_low[1][1]] if mirrored and h else []
        turned.append(turn_call(current[h], targets, h, operands, entries))
    x_sent = turned[1][2] if mirrored else None
    cot_high[0] = [t[0] for t in turned]
    current = [t[1] for t in turned]
    for i in range(groups - 1):
        current = [inward(current[h], i, h) for h in halves]
        cot_high[i + 1] = current
        if i + 1 < groups - 1:
            current = [
                backward_call(
                    [x_high[i + 1][h]], [slope_high[i + 1][h]], current[h], [HIGH_LAYER], operands
                )[0]
                for h in halves
            ]
    last = groups - 1
    cot_sent = [None, None]
    cot_low[last], current, entering = [None, None], [None, None], current
    for h in halves:
        top, bottom = (x_high[last][h], x_low[last][h])
        tops, bottoms = slope_high[last][h], slope_low[last][h]
        sending = dict(turned=cot_high[0][h], last=last) if mirrored else {}
        if h == 0:
            moved = backward_call(
                [top, bottom], [tops, bottoms], entering[h], [HIGH_LAYER, LOW_LAYER], operands,
                **sending
            )
            cot_low[last][h], current[h], *sent = moved
        else:
            cot_low[last][h], *sent = backward_call(
                [top], [tops], entering[h], [HIGH_LAYER], operands, **sending
            )
            (current[h],) = backward_call(
                [bottom], [bottoms], cot_low[last][h], [LOW_LAYER], operands
            )
        cot_sent[h] = sent[0] if mirrored else None
    for i in reversed(range(1, last)):
        current = [outward(current[h], i, h) for h in halves]
        cot_low[i] = current
        current = [
            backward_call([x_low[i][h]], [slope_low[i][h]], current[h], [LOW_LAYER], operands)[0]
            for h in halves
        ]
    from_low, from_high = [], []
    for h in halves:
        from_low.append(lax.ppermute(current[h], "section", [(1, 0)]))
        from_high.append(lax.ppermute(current[h], "section", [(mirror(1), 0)]))
    x_other = []
    for h in halves:
        x_other.append((swap(x_low, x_high, h, x_sent if h else None), None))
    cot_other = []
    for h in halves:
        cot_other.append((swap(cot_low, cot_high, h, cot_sent[h]), None))

    def choose(low_records, high_records, others, first_own, first_other):
        refs, choices = [], []

        def add(array):
            refs.append(array)
            return len(refs) - 1

        for h in halves:
            array, index = first_own[h]
            options = [("first", None, add(array), index)]
            for i in range(groups):
                if i > 0:
                    options.append(("own", (0, i), add(low_records[i][h]), None))
                options.append(("own", (1, i), add(high_records[i][h]), None))
            choices.append(options)
        for h in halves:
            array, index = first_other[h]
            choices.append([("first", None, add(array), index), ("rest", None, add(others[h][0]), others[h][1])])
        return refs, choices

    def token_piece(member, h):
        return (tokens, (member, pl.ds(h * half, half)))

    refs, choices = choose(
        x_low, x_high, x_other, [token_piece(0, h) for h in halves], [token_piece(1, h) for h in halves]
    )
    hidden, slopes, normed = ups_call(refs, choices, current[1], half, width, unloaded, (info, lists, None))
    refs, choices = choose(
        cot_low, cot_high, cot_other,
        [(from_low[0], None), (from_high[1], None)], [(from_high[0], None), (from_low[1], None)]
    )
    downs, split = down_grads_call(
        refs, choices, hidden, half, width, shares, unloaded.shape[2], (info, lists, None)
    )

    def reduce(grads):
        return lax.psum_scatter(grads, "dp", scatter_dimension=0, tiled=True)[0]

    down_share = reduce(downs)
    up_share = reduce(
        up_grads_call(far(split), far(normed), far(slopes), width, shares, unloaded, (info, lists, None))
    )
    token_total = 2 * rows * shares
    state = (far(master[0]), far(moment[0]), far(variance[0]))
    filled = adam_call(far(down_share), 1, state, token_total)
    step_direction, master_next = adam_call(far(up_share), 0, state, token_total, filled)
    return (step_direction[None], master_next[None])


def solution(mesh):
    rows_split = P(None, None, "dp", None)
    by_section = P("section", None, None, "dp", None)
    return jax.shard_map(
        shards,
        mesh=mesh,
        in_specs=(
            rows_split,
            rows_split,
            P("section", None, None, None, None, None),
            P("section", None, None, None, None),
            by_section,
            by_section,
            by_section,
        ),
        out_specs=(by_section, by_section),
        check_vma=False,
    )
```
